32 devices in a mesh: dp: 8 (over z, y), mp: 4 (over x, core).
Axes of the slice: x: 2, y: 2, z: 4, core: 2. Of those that a mesh axis runs over, the one named last changes fastest.
Arguments:
- patches: bfloat16 [8, 256, 832], P('dp'), may hold values from -6 to 6
- wavelengths: float32 [32], replicated, may hold values from 0.4 to 12
- band_ids: int32 [4, 13], replicated, may hold values from 0 to 31
- band_mask: int32 [4, 13], replicated, may hold values from 0 to 1
- sensor: int32 [8], P('dp'), may hold values from 0 to 3
- lengths: int32 [8], P('dp'), may hold values from 64 to 256, as said below
- visible: int32 [8, 256], P('dp'), may hold values from 0 to 1023, as said below
- meta: float32 [8, 8], P('dp'), may hold values from -5 to 5
- w_hyper: float32 [128, 128], replicated, may hold values from -0.5 to 0.5
- b_hyper: float32 [128], replicated, may hold values from -3 to 3
- w_gen: bfloat16 [768, 64, 128], P('mp'), may hold values from -0.03125 to 0.03125
- cls_token: float32 [768], replicated, may hold values from -5 to 5
- w_meta: float32 [8, 768], replicated, may hold values from -2 to 2
- gain_one: float32 [768], replicated, may hold values from 0.5 to 1.5
- shift_one: float32 [768], replicated, may hold values from -2 to 2
- w_qkv: bfloat16 [3, 768, 768], P(None, 'mp'), may hold values from -0.21875 to 0.21875
- w_out: bfloat16 [768, 768], P('mp'), may hold values from -1.75 to 1.75
- gain_two: float32 [768], replicated, may hold values from 0.5 to 1.5
- shift_two: float32 [768], replicated, may hold values from -2 to 2
- w_up: bfloat16 [768, 3072], P(None, 'mp'), may hold values from -0.21875 to 0.21875
- b_up: float32 [3072], P('mp'), may hold values from -2 to 2
- w_down: bfloat16 [3072, 768], P('mp'), may hold values from -0.21875 to 0.21875
- b_down: float32 [768], replicated, may hold values from -2 to 2
- cotangent: float32 [8, 258, 768], P('dp'), may hold values from -6 to 6
Outputs:
- output: float32 [8, 258, 768], P('dp')
- grad_patches: float32 [8, 256, 832], P('dp')
- grad_w_hyper: float32 [128, 128], replicated
- grad_b_hyper: float32 [128], replicated
- grad_w_gen: float32 [768, 64, 128], P('mp')
- grad_cls: float32 [768], replicated
- grad_w_meta: float32 [8, 768], replicated
- grad_gain_one: float32 [768], replicated
- grad_shift_one: float32 [768], replicated
- grad_w_qkv: float32 [3, 768, 768], P(None, 'mp')
- grad_w_out: float32 [768, 768], P('mp')
- grad_gain_two: float32 [768], replicated
- grad_shift_two: float32 [768], replicated
- grad_w_up: float32 [768, 3072], P(None, 'mp')
- grad_b_up: float32 [3072], P('mp')
- grad_w_down: float32 [3072, 768], P('mp')
- grad_b_down: float32 [768], replicated
The draws below stay inside these ranges and needn't reach their ends.
Inputs may be any that keep to these rules, and one draw needn't show every extreme that they name: `lengths`: each chip has 256 or 64 visible patches, and both occur. For a chip of 256 visible patches the entries are distinct patch numbers of a grid of 1024 patches; for a smaller chip all 256 entries are distinct numbers below 256, of which the first lengths are used.
All inputs are finite; a program needn't handle non-finite values.
Results may differ from the reference program's by a relative error of at most 0.023.
Values may be sent and summed in bfloat16 or wider, within the bound.
A program may use at most 128 MiB of HBM per device.

```python
import math
import jax
import jax.numpy as jnp
from jax import lax

D = 768
HEADS = 12
HEAD_DIM = 64
FF = 3072
PIX = 64
HYP = 128
BANDS = 13
NB = 32
SENSORS = 4
META = 8
VIS_MAX = 256
CHIPS = 8
SEQ = 258


def chip_lengths(key):
    base_key = jax.random.fold_in(key, 11)
    long_flags = jax.random.randint(base_key, (CHIPS,), 0, 2)
    places = jnp.arange(CHIPS)
    long_flags = jnp.where(places == 0, 1, jnp.where(places == 1, 0, long_flags))
    return jnp.where(long_flags == 1, VIS_MAX, VIS_MAX // 4).astype(jnp.int32)


def draw_lengths(key, part):
    return chip_lengths(key)


def draw_visible(key, part):
    chip_sizes = chip_lengths(key)
    chip_keys = jax.random.split(jax.random.fold_in(key, 23), CHIPS)

    def one_chip(chip_key, count):
        picked = jax.random.permutation(chip_key, 4 * VIS_MAX - 1)[:VIS_MAX - 1]
        long_list = jnp.concatenate([picked, jnp.full((1,), 4 * VIS_MAX - 1, jnp.int32)]).astype(jnp.int32)
        long_list = jax.random.permutation(jax.random.fold_in(chip_key, 5), long_list)
        short_list = jax.random.permutation(jax.random.fold_in(chip_key, 7), VIS_MAX).astype(jnp.int32)
        return jnp.where(count == VIS_MAX, long_list, short_list).astype(jnp.int32)
    return jax.vmap(one_chip)(chip_keys, chip_sizes)


def band_layout(key):
    base_key = jax.random.fold_in(key, 31)
    pair_slots = BANDS // 2
    slot_pairs = SENSORS * pair_slots
    band_pairs = NB // 2
    order = jax.random.permutation(jax.random.fold_in(base_key, 1), slot_pairs)
    pair_perm = jax.random.permutation(jax.random.fold_in(base_key, 2), band_pairs)
    spare = jax.random.randint(jax.random.fold_in(base_key, 3), (slot_pairs - band_pairs,), 0, band_pairs)
    values = jnp.concatenate([pair_perm, spare]).astype(jnp.int32)
    covering = (jnp.arange(slot_pairs) < band_pairs).astype(jnp.int32)
    assigned = jnp.zeros((slot_pairs,), jnp.int32).at[order].set(values)
    covered = jnp.zeros((slot_pairs,), jnp.int32).at[order].set(covering)
    flipped = jax.random.randint(jax.random.fold_in(base_key, 4), (slot_pairs,), 0, 2).astype(jnp.int32)
    first_ids = 2 * assigned + flipped
    second_ids = 2 * assigned + 1 - flipped
    pair_ids = jnp.stack([first_ids, second_ids], axis=1).reshape(SENSORS, 2 * pair_slots)
    remaining = BANDS - 2 * pair_slots
    rest_ids = jax.random.randint(jax.random.fold_in(base_key, 5), (SENSORS, remaining), 0, NB).astype(jnp.int32)
    band_ids = jnp.concatenate([pair_ids, rest_ids], axis=1).astype(jnp.int32)
    chance = jax.random.randint(jax.random.fold_in(base_key, 6), (slot_pairs,), 0, 4)
    pair_live = jnp.where(covered == 1, 1, jnp.where(chance > 0, 1, 0)).astype(jnp.int32)
    pair_mask = jnp.stack([pair_live, pair_live], axis=1).reshape(SENSORS, 2 * pair_slots)
    rest_mask = jax.random.randint(jax.random.fold_in(base_key, 7), (SENSORS, remaining), 0, 2).astype(jnp.int32)
    band_mask = jnp.concatenate([pair_mask, rest_mask], axis=1).astype(jnp.int32)
    return (band_ids, band_mask)


def draw_band_ids(key, part):
    return band_layout(key)[0]


def draw_band_mask(key, part):
    return band_layout(key)[1]


def draw_wavelengths(key, part):
    values = jnp.exp(jax.random.uniform(key, (NB,), jnp.float32, math.log(0.4), math.log(12.0)))
    return values.astype(jnp.float32)


def draw_patches(key, part):
    values = jnp.clip(jax.random.normal(key, (CHIPS, VIS_MAX, BANDS, PIX), jnp.float32), -6.0, 6.0)
    return values.reshape(CHIPS, VIS_MAX, BANDS * PIX).astype(jnp.bfloat16)


def with_ends(values, rng, low, top_value):
    place = [jax.random.randint(jax.random.fold_in(rng, axis), (), 0, length) for axis, length in enumerate(values.shape)]
    widest = values.shape.index(max(values.shape))
    next_to = place[:widest] + [(place[widest] + 1) % values.shape[widest]] + place[widest + 1:]
    return values.at[tuple(place)].set(low).at[tuple(next_to)].set(top_value)


def level_of(own_key, extent, cuts, smallest, high):
    factor_of = 1.0
    for position, parts in cuts:
        heights = jax.random.uniform(jax.random.fold_in(jax.random.fold_in(own_key, 6), position), (parts,), jnp.float32, smallest / len(cuts), high / len(cuts))
        factor_of = factor_of * jnp.repeat(jnp.exp(heights), extent[position] // parts).reshape((-1,) + (1,) * (len(extent) - 1 - position))
    return factor_of


def normal_values(own_key, extent, deviation, most, pieces=(), held_as=jnp.bfloat16):
    array = jax.random.normal(own_key, extent, jnp.float32) * deviation
    if len(pieces) > 0:
        array = level_of(own_key, extent, pieces, -0.22, 0.18) * array
    return jnp.clip(array, min=-most, max=most).astype(held_as)


def setup_inputs(seed: int = 0) -> dict:
    splits = jax.random.split(jax.random.key(seed), 25)
    return {
        "patches": draw_patches(jax.random.fold_in(splits[24], 71), 0),
        "wavelengths": draw_wavelengths(jax.random.fold_in(splits[24], 71), 0),
        "band_ids": draw_band_ids(jax.random.fold_in(splits[24], 71), 0),
        "band_mask": draw_band_mask(jax.random.fold_in(splits[24], 71), 0),
        "sensor": with_ends(jax.random.randint(splits[4], (CHIPS,), 0, SENSORS), jax.random.fold_in(splits[4], 1), 0, SENSORS - 1).astype(jnp.int32),
        "lengths": draw_lengths(jax.random.fold_in(splits[24], 71), 0),
        "visible": draw_visible(jax.random.fold_in(splits[24], 71), 0),
        "meta": normal_values(splits[7], (CHIPS, META), 1.0, 5.0, ((0, 8),), jnp.float32),
        "w_hyper": normal_values(splits[8], (HYP, HYP), HYP ** -0.5, 0.5, (), jnp.float32),
        "b_hyper": normal_values(splits[9], (HYP,), 0.5, 3.0, (), jnp.float32),
        "w_gen": normal_values(splits[10], (D, PIX, HYP), (4 * HYP * PIX) ** -0.5, 0.03125, ((0, 4),)),
        "cls_token": normal_values(splits[11], (D,), 1.0, 5.0, (), jnp.float32),
        "w_meta": normal_values(splits[12], (META, D), META ** -0.5, 2.0, (), jnp.float32),
        "gain_one": jnp.clip(1.0 + 0.1 * jax.random.normal(splits[13], (D,), jnp.float32), 0.5, 1.5),
        "shift_one": normal_values(splits[14], (D,), 0.3, 2.0, (), jnp.float32),
        "w_qkv": normal_values(splits[15], (3, D, D), D ** -0.5, 0.21875, ((1, 4),)),
        "w_out": normal_values(splits[16], (D, D), (D // 64) ** -0.5, 1.75, ((0, 4),)),
        "gain_two": jnp.clip(1.0 + 0.1 * jax.random.normal(splits[17], (D,), jnp.float32), 0.5, 1.5),
        "shift_two": normal_values(splits[18], (D,), 0.3, 2.0, (), jnp.float32),
        "w_up": normal_values(splits[19], (D, FF), D ** -0.5, 0.21875, ((1, 4),)),
        "b_up": normal_values(splits[20], (FF,), 0.3, 2.0, ((0, 4),), jnp.float32),
        "w_down": normal_values(splits[21], (FF, D), (FF // 4) ** -0.5, 0.21875, ((0, 4),)),
        "b_down": normal_values(splits[22], (D,), 0.3, 2.0, (), jnp.float32),
        "cotangent": normal_values(splits[23], (CHIPS, SEQ, D), 1.0, 6.0, ((0, 8),), jnp.float32),
    }


@jax.custom_vjp
def low(v):
    return lax.optimization_barrier(v.astype(jnp.bfloat16)).astype(jnp.float32)

@jax.custom_vjp
def low_back(v):
    return v

def low_keep(v):
    return (low(v), None)

def low_pass(kept, grad):
    return (grad,)

def back_keep(v):
    return (v, None)

def back_low(kept, grad):
    return (low(grad),)
low.defvjp(low_keep, low_pass)
low_back.defvjp(back_keep, back_low)

def sinus_waves(wavelengths, width):
    half_width = width // 2
    steps = jnp.arange(half_width, dtype=jnp.float32)
    freqs = jnp.exp(steps * (6.0 * math.log(2.0) / half_width))
    angles = wavelengths[:, None] * freqs[None, :]
    return jnp.concatenate([jnp.sin(angles), jnp.cos(angles)], axis=1)

def grid_codes(visible, lengths, width, most):
    short_side = math.isqrt(most)
    long_side = 2 * short_side
    sides = jnp.where(lengths == most, long_side, short_side).astype(jnp.int32)[:, None]
    grid_rows = (visible // sides).astype(jnp.float32)
    grid_cols = (visible % sides).astype(jnp.float32)
    quarter = width // 4
    omegas = jnp.exp(jnp.arange(quarter, dtype=jnp.float32) * (-math.log(10000.0) / quarter))
    row_angle = grid_rows[..., None] * omegas
    col_angle = grid_cols[..., None] * omegas
    return jnp.concatenate([jnp.sin(row_angle), jnp.cos(row_angle), jnp.sin(col_angle), jnp.cos(col_angle)], axis=-1)

def layer_norm(values, gain_row, shift_row):
    row_mean = lax.optimization_barrier(jnp.mean(values, axis=-1, keepdims=True))
    centred = values - row_mean
    variance = lax.optimization_barrier(jnp.mean(centred * centred, axis=-1, keepdims=True))
    return centred * lax.rsqrt(variance + 1e-05) * gain_row + shift_row

def reference(patches, wavelengths, band_ids, band_mask, sensor, lengths, visible, meta, w_hyper, b_hyper, w_gen, cls_token, w_meta, gain_one, shift_one, w_qkv, w_out, gain_two, shift_two, w_up, b_up, w_down, b_down, cotangent):
    highest = lax.Precision.HIGHEST
    features = sinus_waves(wavelengths, HYP)
    positions = grid_codes(visible, lengths, D, VIS_MAX)
    live_rows = (jnp.arange(SEQ)[None, :] < lengths[:, None] + 2).astype(jnp.float32)
    selector = (band_ids[:, :, None] == jnp.arange(NB)[None, None, :]).astype(jnp.float32) * band_mask[:, :, None].astype(jnp.float32)
    scale_factor = 1.0 / math.sqrt(HEAD_DIM)

    def forward(w_hyper, b_hyper, w_gen, cls_token, w_meta, gain_one, shift_one, w_qkv, w_out, gain_two, shift_two, w_up, b_up, w_down, b_down, pixels):
        hidden = low(jax.nn.gelu(jnp.dot(features, w_hyper, precision=highest) + b_hyper, approximate=False))
        kernel_table = low(jnp.einsum('nh,dph->npd', hidden, w_gen, precision=highest))
        per_sensor = jnp.einsum('sbn,npd->sbpd', selector, kernel_table, precision=highest)
        kernels = per_sensor[sensor].reshape(CHIPS, BANDS * PIX, D)
        embedded = low_back(low(jnp.einsum('cvk,ckd->cvd', pixels, kernels, precision=highest)))
        cls_rows = jnp.broadcast_to(cls_token, (CHIPS, 1, D))
        meta_rows = jnp.dot(meta, w_meta, precision=highest)[:, None, :]
        tokens_in = jnp.concatenate([cls_rows, meta_rows, embedded + positions], axis=1)
        normed = low(layer_norm(tokens_in, gain_one, shift_one))
        qkv = low_back(low(jnp.einsum('csd,ted->tcse', normed, w_qkv, precision=highest)))
        head_shape = (CHIPS, SEQ, HEADS, HEAD_DIM)
        queries = qkv[0].reshape(head_shape)
        key_rows = qkv[1].reshape(head_shape)
        value_rows = qkv[2].reshape(head_shape)
        scores = low_back(jnp.einsum('cqhe,ckhe->chqk', queries, key_rows, precision=highest) * scale_factor)
        scores = jnp.where(live_rows[:, None, None, :] > 0, scores, -1000000000.0)
        probs_low = low(jax.nn.softmax(scores, axis=-1))
        mixed_heads = jnp.einsum('chqk,ckhe->cqhe', probs_low, value_rows, precision=highest).reshape(CHIPS, SEQ, D)
        mixed_heads = low_back(low(mixed_heads))
        attended = low_back(jnp.einsum('csd,de->cse', mixed_heads, w_out, precision=highest))
        after_attn = tokens_in + attended
        normed_two = low(layer_norm(after_attn, gain_two, shift_two))
        gate_pre = low_back(jnp.einsum('csd,df->csf', normed_two, w_up, precision=highest) + b_up)
        activation = low(jax.nn.gelu(gate_pre, approximate=False))
        branch = low_back(jnp.einsum('csf,fd->csd', activation, w_down, precision=highest) + b_down)
        return live_rows[:, :, None] * (after_attn + branch)
    params = (w_hyper, b_hyper, w_gen.astype(jnp.float32), cls_token, w_meta, gain_one, shift_one, w_qkv.astype(jnp.float32), w_out.astype(jnp.float32), gain_two, shift_two, w_up.astype(jnp.float32), b_up, w_down.astype(jnp.float32), b_down, patches.astype(jnp.float32))
    result, pullback = jax.vjp(forward, *params)
    gradients = pullback(cotangent)
    return (result, gradients[15], gradients[0], gradients[1], gradients[2], gradients[3], gradients[4], gradients[5], gradients[6], gradients[7], gradients[8], gradients[9], gradients[10], gradients[11], gradients[12], gradients[13], gradients[14])
```

```python
import functools
import math

import jax
import jax.numpy as jnp
from jax import lax
from jax.experimental import pallas as pl
from jax.experimental.pallas import tpu as pltpu
from jax.sharding import PartitionSpec as P

F32 = jnp.float32
BF16 = jnp.bfloat16
MESH = pl.DeviceIdType.MESH

D = 768
HEAD_DIM = 64
PIX = 64
HYP = 128
BANDS = 13
NB = 32
SENSORS = 4
VIS_MAX = 256
SEQ = 258


def sinus_waves(wavelengths, width):
    half_width = width // 2
    steps = jnp.arange(half_width, dtype=jnp.float32)
    freqs = jnp.exp(steps * (6.0 * math.log(2.0) / half_width))
    angles = wavelengths[:, None] * freqs[None, :]
    return jnp.concatenate([jnp.sin(angles), jnp.cos(angles)], axis=1)


def grid_codes(visible, lengths, width, most):
    short_side = math.isqrt(most)
    long_side = 2 * short_side
    sides = jnp.where(lengths == most, long_side, short_side).astype(jnp.int32)[:, None]
    grid_rows = (visible // sides).astype(jnp.float32)
    grid_cols = (visible % sides).astype(jnp.float32)
    quarter = width // 4
    omegas = jnp.exp(jnp.arange(quarter, dtype=jnp.float32) * (-math.log(10000.0) / quarter))
    row_angle = grid_rows[..., None] * omegas
    col_angle = grid_cols[..., None] * omegas
    return jnp.concatenate(
        [jnp.sin(row_angle), jnp.cos(row_angle), jnp.sin(col_angle), jnp.cos(col_angle)], axis=-1
    )


def gelu_exact(values):
    return jax.nn.gelu(values, approximate=False)


def remote(src, dst, send_sem, recv_sem, device):
    return pltpu.make_async_remote_copy(
        src_ref=src,
        dst_ref=dst,
        send_sem=send_sem,
        recv_sem=recv_sem,
        device_id=device,
        device_id_type=MESH,
    )


def greet(devices):
    barrier = pltpu.get_barrier_semaphore()
    for device in devices:
        pl.semaphore_signal(barrier, inc=1, device_id=device, device_id_type=MESH)
    pl.semaphore_wait(barrier, len(devices))


def mp_peers():
    place = lax.axis_index("mp")
    core = lax.rem(place, 2)
    return core, {"mp": place + 1 - 2 * core}, {"mp": lax.rem(place + 2, 4)}


class Sender:
    def __init__(self, sends, recvs):
        self.sends, self.recvs, self.copies = sends, recvs, []

    def go(self, number, src, dst, device):
        copy = remote(src, dst, self.sends.at[number], self.recvs.at[number], device)
        copy.start()
        self.copies.append(copy)
        return copy

    def finish(self):
        for copy in self.copies:
            copy.wait_send()


class MpSum(Sender):
    def __init__(self, part, slots, out, cuts, sends, recvs):
        super().__init__(sends, recvs)
        self.part, self.out, self.cuts = part, out, cuts
        self.pair_in, self.chip_sum, self.far_in, self.other_near, self.other_far = slots
        self.core, self.pair, self.far = mp_peers()
        self.first, self.second, self.third = {}, {}, {}

    def number(self, step, i):
        return step * len(self.cuts) + i

    def start(self, i):
        rows = pl.ds(*self.cuts[i])
        self.first[i] = self.go(
            self.number(0, i), self.part.at[1 - self.core, rows], self.pair_in.at[rows], self.pair
        )

    def relay(self, i):
        rows = pl.ds(*self.cuts[i])
        self.first[i].wait_recv()
        self.chip_sum[rows] = (
            self.part[self.core, rows].astype(F32) + self.pair_in[rows].astype(F32)
        ).astype(BF16)
        mine = self.chip_sum.at[rows]
        self.second[i] = (
            self.go(self.number(1, i), mine, self.far_in.at[rows], self.far),
            self.go(self.number(2, i), mine, self.other_near.at[rows], self.pair),
        )

    def forward(self, i):
        rows = pl.ds(*self.cuts[i])
        self.second[i][0].wait_recv()
        self.third[i] = self.go(
            self.number(3, i), self.far_in.at[rows], self.other_far.at[rows], self.pair
        )
        self.out[self.core, rows] = self.chip_sum[rows].astype(F32) + self.far_in[rows].astype(F32)

    def total(self, i):
        rows = pl.ds(*self.cuts[i])
        self.second[i][1].wait_recv()
        self.third[i].wait_recv()
        self.out[1 - self.core, rows] = self.other_near[rows].astype(F32) + self.other_far[
            rows
        ].astype(F32)


class DpPlace:
    def __init__(self, lines):
        place = lax.axis_index("dp")
        self.lines = lines
        self.inner = lax.rem(place, 2)
        self.outer = place // 2
        self.pair = {"dp": self.outer * 2 + 1 - self.inner}

    def peer(self, k):
        return {"dp": lax.rem(self.outer + k, self.lines) * 2 + self.inner}


class DpSum(Sender):
    def __init__(self, place, grad, slots, whole, sends, recvs):
        super().__init__(sends, recvs)
        self.place, self.grad, self.whole = place, grad, whole
        self.pair_in, self.half, self.line_in = slots

    def stage_pair(self):
        self.first = self.go(0, self.grad.at[1 - self.place.inner], self.pair_in, self.place.pair)

    def stage_line(self):
        place, lines = self.place, self.place.lines
        self.first.wait_recv()
        for z in range(lines):
            self.half[z] = (
                self.grad[place.inner, z].astype(F32) + self.pair_in[z].astype(F32)
            ).astype(BF16)
        self.second = []
        for k in range(1, lines):
            target = lax.rem(place.outer + k, lines)
            self.second.append(
                self.go(k, self.half.at[target], self.line_in.at[k - 1], place.peer(k))
            )

    def stage_total(self):
        place, lines = self.place, self.place.lines
        total = self.half[place.outer].astype(F32)
        for k in range(1, lines):
            self.second[k - 1].wait_recv()
            total = total + self.line_in[k - 1].astype(F32)
        self.whole[place.inner, place.outer] = total.astype(BF16)
        mine = self.whole.at[place.inner, place.outer]
        self.third = [self.go(lines + k - 1, mine, mine, place.peer(k)) for k in range(1, lines)]
        self.fourth = [self.go(2 * lines - 1, mine, mine, place.pair)]

    def stage_forward(self):
        place, lines = self.place, self.place.lines
        for k in range(1, lines):
            self.third[k - 1].wait_recv()
            got = self.whole.at[place.inner, lax.rem(place.outer - k + lines, lines)]
            self.fourth.append(self.go(2 * lines + k - 1, got, got, place.pair))

    def stage_end(self):
        for copy in self.fourth:
            copy.wait_recv()
        self.finish()


class SmallSum(Sender):
    def __init__(self, place, part, pair_in, line_in, out, sends, recvs):
        super().__init__(sends, recvs)
        self.place, self.part, self.pair_in, self.line_in, self.out = place, part, pair_in, line_in, out

    def start(self):
        self.first = self.go(0, self.part, self.pair_in, self.place.pair)

    def relay(self):
        place, lines = self.place, self.place.lines
        self.first.wait_recv()
        self.line_in[place.outer] = self.part[...] + self.pair_in[...]
        mine = self.line_in.at[place.outer]
        self.second = [self.go(k, mine, mine, place.peer(k)) for k in range(1, lines)]

    def total(self):
        for copy in self.second:
            copy.wait_recv()
        total = self.line_in[0]
        for z in range(1, self.place.lines):
            total = total + self.line_in[z]
        self.out[...] = total
        self.finish()


def dot(left, right):
    return jnp.dot(left, right, preferred_element_type=F32)


def dot_nt(left, right):
    return lax.dot_general(left, right, (((1,), (1,)), ((), ())), preferred_element_type=F32)


def dot_tn(left, right):
    return lax.dot_general(left, right, (((0,), (0,)), ((), ())), preferred_element_type=F32)


def row_mean(values):
    return jnp.mean(values, axis=-1, keepdims=True)


def col_sum(values):
    return jnp.sum(values, axis=0, keepdims=True)


ROWS = 272
CUTS = [(0, 64), (64, 64), (128, 64), (192, 80)]
PIXEL_CUTS = [(0, 64), (64, 64)]


def layer_kernel(
    lines,
    patches,
    kern,
    positions,
    rows_in,
    meta_col,
    live_row,
    live_col,
    select,
    w_qkv,
    w_out,
    w_up,
    b_up,
    w_down,
    cotangent,
    output,
    grad_patches,
    smalls,
    whole_down,
    whole_up,
    whole_attn,
    whole_table,
    embeds,
    tokens,
    xhat_one,
    rstd_one,
    xhat_two,
    rstd_two,
    after,
    normed,
    normed_two,
    queries,
    keys,
    values,
    probs,
    mixed,
    branch_grad,
    gate_grad,
    activation,
    grad_pre,
    grad_after,
    after_low,
    grad_tokens,
    embed_grad,
    spread,
    part_a,
    part_b,
    part_c,
    part_d,
    part_e,
    slots_a,
    slots_b,
    slots_c,
    slots_d,
    slots_e,
    out_a,
    out_b,
    out_c,
    out_d,
    out_e,
    grad_down,
    grad_up,
    grad_attn,
    grad_table,
    slots_down,
    slots_up,
    slots_attn,
    slots_table,
    small_part,
    small_pair,
    small_line,
    mp_sends,
    mp_recvs,
    dp_sends,
    dp_recvs,
    etc_sends,
    etc_recvs,
):
    core, pair, far = mp_peers()
    place = DpPlace(lines)
    greet([pair, far, place.pair] + [place.peer(k) for k in range(1, lines)])
    me = lax.axis_index("mp")
    width = w_out.shape[0]
    heads = width // HEAD_DIM
    full = D

    def mp_sum(part, slots, out, cuts, number):
        return MpSum(
            part,
            [slots.at[k] for k in range(5)],
            out,
            cuts,
            mp_sends.at[number],
            mp_recvs.at[number],
        )

    sum_a = mp_sum(part_a, slots_a, out_a, CUTS, 0)
    sum_b = mp_sum(part_b, slots_b, out_b, CUTS, 1)
    sum_c = mp_sum(part_c, slots_c, out_c, CUTS, 2)
    sum_d = mp_sum(part_d, slots_d, out_d, CUTS, 3)
    sum_e = mp_sum(part_e, slots_e, out_e, PIXEL_CUTS, 4)

    def dp_sum(grad, slots, whole, number):
        return DpSum(place, grad, slots, whole, dp_sends.at[number], dp_recvs.at[number])

    dp_down = dp_sum(grad_down, slots_down, whole_down, 0)
    dp_up = dp_sum(grad_up, slots_up, whole_up, 1)
    dp_attn = dp_sum(grad_attn, slots_attn, whole_attn, 2)
    dp_table = dp_sum(grad_table, slots_table, whole_table, 3)
    small = SmallSum(place, small_part, small_pair, small_line, smalls, dp_sends.at[4], dp_recvs.at[4])

    def put_piece(grad, first_row, block):
        rows = grad.shape[2]
        for k in range(0, block.shape[0], rows):
            chunk = (first_row + k) // rows
            grad[chunk // lines, chunk % lines] = block[k : k + rows].astype(BF16)

    gain_one, shift_one = rows_in[0:1], rows_in[1:2]
    gain_two, shift_two = rows_in[2:3], rows_in[3:4]
    b_down = rows_in[4:5]
    lane_head = lax.broadcasted_iota(jnp.int32, (1, width), 1) // HEAD_DIM
    head_masks = [(lane_head == h).astype(F32).astype(BF16) for h in range(heads)]

    etc = Sender(etc_sends, etc_recvs)
    embeds[me] = dot(patches[...], kern[...]).astype(BF16)
    mine = embeds.at[me]
    to_pair = etc.go(0, mine, mine, pair)
    to_far = etc.go(1, mine, mine, far)
    branch_grad[0:256] = (live_col[0:256] * cotangent[2:258]).astype(BF16)
    branch_grad[256:272] = jnp.concatenate(
        [cotangent[0:2], jnp.zeros((14, full), F32)], axis=0
    ).astype(BF16)
    small_part[...] = jnp.zeros_like(small_part)
    small_part[5:6] = col_sum(branch_grad[...].astype(F32))
    gate_grad[...] = dot_nt(branch_grad[...], w_down[...])
    far_place = lax.rem(me + 2, 4)
    to_far.wait_recv()
    got = embeds.at[far_place]
    passed = etc.go(2, got, got, pair)
    to_pair.wait_recv()
    passed.wait_recv()

    for lo, n in CUTS:
        hi = min(lo + n, 256)
        for i in range(4):
            cols = slice(i * width, (i + 1) * width)
            tokens[lo:hi, cols] = embeds[i, lo:hi].astype(F32)
        tokens[lo:hi] += positions[lo:hi]
        if lo + n > 256:
            tokens[256:272] = jnp.concatenate([rows_in[5:7], jnp.zeros((14, full), F32)], axis=0)
        rows = slice(lo, lo + n)
        x = tokens[rows]
        centred = x - row_mean(x)
        rstd = lax.rsqrt(row_mean(centred * centred) + 1e-05)
        rstd_one[rows] = rstd
        xhat = centred * rstd
        xhat_one[rows] = xhat
        normed[rows] = (xhat * gain_one + shift_one).astype(BF16)
    queries[...] = dot_nt(normed[...], w_qkv[0]).astype(BF16)
    keys[...] = dot_nt(normed[...], w_qkv[1]).astype(BF16)
    values[...] = dot_nt(normed[...], w_qkv[2]).astype(BF16)

    live_keys = live_row[...] > 0
    total = None
    for h in range(heads):
        raw = dot_nt(queries[...] * head_masks[h], keys[...]) * 0.125
        raw = jnp.where(live_keys, raw, -1000000000.0)
        expo = jnp.exp(raw - jnp.max(raw, axis=-1, keepdims=True))
        prob = expo / jnp.sum(expo, axis=-1, keepdims=True)
        probs[h] = prob
        term = dot(prob.astype(BF16), values[...] * head_masks[h])
        total = term if total is None else total + term
    mixed[...] = total.astype(BF16)

    def put_part(part, rows, block):
        half = block.shape[1] // 2
        part[0, rows] = block[:, :half].astype(BF16)
        part[1, rows] = block[:, half:].astype(BF16)

    def get_out(out, rows):
        return jnp.concatenate([out[0, rows], out[1, rows]], axis=1)

    count = len(CUTS)
    for i, (lo, n) in enumerate(CUTS):
        rows = slice(lo, lo + n)
        put_part(part_a, rows, dot(mixed[rows], w_out[...]))
        sum_a.start(i)
        if i >= 1:
            sum_a.relay(i - 1)
    sum_a.relay(count - 1)
    for i in range(count):
        sum_a.forward(i)

    for i, (lo, n) in enumerate(CUTS):
        rows = slice(lo, lo + n)
        sum_a.total(i)
        x = tokens[rows] + get_out(out_a, rows)
        after[rows] = x
        centred = x - row_mean(x)
        rstd = lax.rsqrt(row_mean(centred * centred) + 1e-05)
        rstd_two[rows] = rstd
        xhat = centred * rstd
        xhat_two[rows] = xhat
        normed_two[rows] = (xhat * gain_two + shift_two).astype(BF16)
        gate = dot(normed_two[rows], w_up[...]) + b_up[...]
        cdf = 0.5 + 0.5 * lax.erf(gate * (2.0**-0.5))
        activation[rows] = (gate * cdf).astype(BF16)
        pdf = jnp.exp(-0.5 * gate * gate) * ((2.0 * math.pi) ** -0.5)
        grad_pre[rows] = (gate_grad[rows] * (cdf + gate * pdf)).astype(BF16)
        put_part(part_c, rows, dot_nt(grad_pre[rows], w_up[...]))
        sum_c.start(i)
        if i >= 1:
            sum_c.relay(i - 1)
    sum_c.relay(count - 1)
    put_piece(grad_down, 0, dot_tn(activation[...], branch_grad[...]))
    dp_down.stage_pair()
    for i in range(count):
        sum_c.forward(i)
    put_piece(grad_up, 0, dot_tn(normed_two[...], grad_pre[...]))
    dp_up.stage_pair()
    small_part[6:7] = col_sum(grad_pre[...].astype(F32))

    for i, (lo, n) in enumerate(CUTS):
        rows = slice(lo, lo + n)
        sum_c.total(i)
        dy = get_out(out_c, rows)
        xhat = xhat_two[rows]
        small_part[2:3] += col_sum(dy * xhat)
        small_part[3:4] += col_sum(dy)
        e = dy * gain_two
        dx = rstd_two[rows] * (e - row_mean(e) - xhat * row_mean(e * xhat))
        if lo + n <= 256:
            grad_out = live_col[rows] * cotangent[lo + 2 : lo + n + 2]
        else:
            grad_out = jnp.concatenate(
                [live_col[lo:256] * cotangent[lo + 2 : 258], cotangent[0:2], jnp.zeros((14, full), F32)],
                axis=0,
            )
        grad_x = dx + grad_out
        grad_after[rows] = grad_x
        after_low[rows] = grad_x.astype(BF16)
    grad_mixed = dot_nt(after_low[...], w_out[...]).astype(BF16)
    put_piece(grad_attn, 0, dot_tn(mixed[...], after_low[...]))
    parts = [None, None, None]
    for h in range(heads):
        mixed_h = grad_mixed * head_masks[h]
        grad_probs = dot_nt(mixed_h, values[...])
        prob = probs[h]
        scores = prob * (grad_probs - jnp.sum(grad_probs * prob, axis=-1, keepdims=True))
        scores = scores.astype(BF16)
        terms = [
            dot(scores, keys[...] * head_masks[h]),
            dot_tn(scores, queries[...] * head_masks[h]),
            dot_tn(prob.astype(BF16), mixed_h),
        ]
        parts = [t if p is None else p + t for p, t in zip(parts, terms)]
    grad_q = (parts[0] * 0.125).astype(BF16)
    grad_k = (parts[1] * 0.125).astype(BF16)
    grad_v = parts[2].astype(BF16)
    for i, (lo, n) in enumerate(CUTS):
        rows = slice(lo, lo + n)
        block = (
            dot(grad_q[rows], w_qkv[0]) + dot(grad_k[rows], w_qkv[1]) + dot(grad_v[rows], w_qkv[2])
        )
        put_part(part_d, rows, block)
        sum_d.start(i)
        if i >= 1:
            sum_d.relay(i - 1)
    sum_d.relay(count - 1)
    for t, grad in enumerate((grad_q, grad_k, grad_v)):
        put_piece(grad_attn, (t + 1) * width, dot_tn(grad, normed[...]))
    for i in range(count):
        sum_d.forward(i)
    dp_attn.stage_pair()

    for i, (lo, n) in enumerate(CUTS):
        rows = slice(lo, lo + n)
        put_part(part_b, rows, dot(activation[rows], w_down[...]))
        sum_b.start(i)
    band = lax.broadcasted_iota(jnp.int32, (BANDS * PIX, 16), 0) // PIX
    slot = lax.broadcasted_iota(jnp.int32, (BANDS * PIX, 16), 1)
    row_select = dot((band == slot).astype(F32).astype(BF16), select[...]).astype(BF16)
    wide = NB * PIX
    table_band = lax.broadcasted_iota(jnp.int32, (NB, wide), 0)
    table_lane = lax.broadcasted_iota(jnp.int32, (NB, wide), 1) // PIX
    widen = (table_band == table_lane).astype(F32).astype(BF16)
    for b in range(BANDS):
        rows = slice(b * PIX, (b + 1) * PIX)
        spot = lax.broadcasted_iota(jnp.int32, (PIX, wide), 0)
        lane = lax.rem(lax.broadcasted_iota(jnp.int32, (PIX, wide), 1), PIX)
        block = dot(row_select[rows], widen)
        spread[rows] = jnp.where(spot == lane, block, 0.0).astype(BF16)

    for i, (lo, n) in enumerate(CUTS):
        rows = slice(lo, lo + n)
        sum_d.total(i)
        dy = get_out(out_d, rows)
        xhat = xhat_one[rows]
        small_part[0:1] += col_sum(dy * xhat)
        small_part[1:2] += col_sum(dy)
        e = dy * gain_one
        dx = rstd_one[rows] * (e - row_mean(e) - xhat * row_mean(e * xhat))
        grad_tokens[rows] = grad_after[rows] + dx
    small_part[4:5] = grad_tokens[256:257]
    small_part[8:16] = meta_col[...] * grad_tokens[257:258]
    small.start()
    for i in range(4):

        @pl.when(me == i)
        def _():
            embed_grad[...] = grad_tokens[0:256, i * width : (i + 1) * width].astype(BF16)

    grad_kern = dot_tn(embed_grad[...], patches[...]).astype(BF16)
    table = dot(grad_kern, spread[...])
    put_piece(grad_table, 0, table[:, : wide // 2])
    put_piece(grad_table, width, table[:, wide // 2 :])
    dp_table.stage_pair()
    pixels = dot_nt(embed_grad[...], kern[...]).astype(BF16)
    part_e[0] = pixels[:128]
    part_e[1] = pixels[128:]
    for i in range(len(PIXEL_CUTS)):
        sum_e.start(i)
    dp_down.stage_line()
    small.relay()
    for i in range(len(PIXEL_CUTS)):
        sum_e.relay(i)
    for i in range(count):
        sum_b.relay(i)
    dp_up.stage_line()
    small.total()
    for i in range(count):
        sum_b.forward(i)
    for i in range(len(PIXEL_CUTS)):
        sum_e.forward(i)
    dp_down.stage_total()
    dp_attn.stage_line()
    for i, (lo, n) in enumerate(CUTS):
        rows = slice(lo, lo + n)
        sum_b.total(i)
        x = after[rows] + get_out(out_b, rows) + b_down
        if lo + n <= 256:
            output[lo + 2 : lo + n + 2] = live_col[rows] * x
        else:
            output[lo + 2 : 258] = live_col[lo:256] * x[: 256 - lo]
            output[0:2] = x[256 - lo : 258 - lo]
    for i in range(len(PIXEL_CUTS)):
        sum_e.total(i)
    grad_patches[0:128] = out_e[0]
    grad_patches[128:256] = out_e[1]
    dp_up.stage_total()
    dp_table.stage_line()
    dp_down.stage_forward()
    dp_attn.stage_total()
    dp_up.stage_forward()
    dp_table.stage_total()
    dp_down.stage_end()
    dp_attn.stage_forward()
    dp_up.stage_end()
    dp_table.stage_forward()
    dp_attn.stage_end()
    dp_table.stage_end()
    for one in (sum_a, sum_b, sum_c, sum_d, sum_e, etc):
        one.finish()


def layer(dp_count, width, operands):
    lines = dp_count // 2

    def piece(rows, lanes):
        chunk = -(-rows // dp_count)
        chunk = -(-chunk // 16) * 16
        return (2, lines, chunk, lanes)

    pieces = [piece(768, D), piece(768, D), piece(4 * width, D), piece(2 * width, NB * PIX // 2)]
    half = D // 2
    pixel_lanes = BANDS * PIX

    def vmem(*shape, dtype=F32):
        return pltpu.VMEM(shape, dtype)

    def low(*shape):
        return pltpu.VMEM(shape, BF16)

    scratch = [
        low(4, 256, width),
        vmem(ROWS, D),
        vmem(ROWS, D),
        vmem(ROWS, 1),
        vmem(ROWS, D),
        vmem(ROWS, 1),
        vmem(ROWS, D),
        low(ROWS, D),
        low(ROWS, D),
        low(ROWS, width),
        low(ROWS, width),
        low(ROWS, width),
        vmem(width // HEAD_DIM, ROWS, ROWS),
        low(ROWS, width),
        low(ROWS, D),
        vmem(ROWS, D),
        low(ROWS, D),
        low(ROWS, D),
        vmem(ROWS, D),
        low(ROWS, D),
        vmem(ROWS, D),
        low(256, width),
        low(pixel_lanes, NB * PIX),
    ]
    scratch += [low(2, ROWS, half)] * 4 + [low(2, 128, pixel_lanes)]
    scratch += [low(5, ROWS, half)] * 4 + [low(5, 128, pixel_lanes)]
    scratch += [vmem(2, ROWS, half)] * 4 + [vmem(2, 128, pixel_lanes)]
    scratch += [low(*shape) for shape in pieces]
    scratch += [[low(*shape[1:])] * 3 for shape in pieces]
    scratch += [vmem(16, D), vmem(16, D), vmem(lines, 16, D)]
    dma = pltpu.SemaphoreType.DMA
    scratch += [dma((5, 16)), dma((5, 16)), dma((5, 3 * lines)), dma((5, 3 * lines)), dma((3,)), dma((3,))]
    ref = pl.BlockSpec(memory_space=pltpu.VMEM)
    shapes = [
        jax.ShapeDtypeStruct((SEQ, D), F32),
        jax.ShapeDtypeStruct((256, pixel_lanes), F32),
        jax.ShapeDtypeStruct((16, D), F32),
    ] + [jax.ShapeDtypeStruct(shape, BF16) for shape in pieces]
    outs = pl.pallas_call(
        functools.partial(layer_kernel, lines),
        out_shape=shapes,
        in_specs=[ref] * len(operands),
        out_specs=[ref] * len(shapes),
        scratch_shapes=scratch,
        compiler_params=pltpu.CompilerParams(
            collective_id=0, has_side_effects=True, vmem_limit_bytes=60 * 1024 * 1024
        ),
        name="layer",
    )(*operands)
    return list(outs[:3]) + [out.reshape(-1, out.shape[-1]) for out in outs[3:]]


def small_sum_kernel(axis, count, part, out, slots, sends, recvs):
    me = lax.axis_index(axis)
    peers = [{axis: lax.rem(me + k, count)} for k in range(1, count)]
    greet(peers)
    copies = []
    for k, peer in enumerate(peers):
        copy = remote(part, slots.at[me], sends.at[k], recvs.at[k], peer)
        copy.start()
        copies.append(copy)
    slots[me] = part[...]
    for copy in copies:
        copy.wait()
    total = slots[0]
    for k in range(1, count):
        total = total + slots[k]
    out[...] = total


def small_sum(part, axis, count, number):
    vmem = pl.BlockSpec(memory_space=pltpu.VMEM)
    return pl.pallas_call(
        functools.partial(small_sum_kernel, axis, count),
        out_shape=jax.ShapeDtypeStruct(part.shape, F32),
        in_specs=[vmem],
        out_specs=vmem,
        scratch_shapes=[
            pltpu.VMEM((count,) + part.shape, F32),
            pltpu.SemaphoreType.DMA((count - 1,)),
            pltpu.SemaphoreType.DMA((count - 1,)),
        ],
        compiler_params=pltpu.CompilerParams(collective_id=number, has_side_effects=True),
        name="small_sum_" + axis,
    )(part)


def local(
    dp_count,
    patches,
    wavelengths,
    band_ids,
    band_mask,
    sensor,
    lengths,
    visible,
    meta,
    w_hyper,
    b_hyper,
    w_gen,
    cls_token,
    w_meta,
    gain_one,
    shift_one,
    w_qkv,
    w_out,
    gain_two,
    shift_two,
    w_up,
    b_up,
    w_down,
    b_down,
    cotangent,
):
    highest = lax.Precision.HIGHEST
    width = w_gen.shape[0]
    features = sinus_waves(wavelengths, HYP)
    positions = grid_codes(visible, lengths, D, VIS_MAX)[0]
    hyper_pre = jnp.dot(features, w_hyper, precision=highest) + b_hyper
    hidden, hyper_pull = jax.vjp(gelu_exact, hyper_pre)
    hidden_low = hidden.astype(BF16)
    ids, mask = band_ids[sensor[0]], band_mask[sensor[0]]
    select = (ids[:, None] == jnp.arange(NB)[None, :]).astype(F32) * mask[:, None].astype(F32)
    chosen = jnp.dot(select.astype(BF16), hidden_low, preferred_element_type=F32).astype(BF16)
    kern = jnp.einsum("bh,dph->bpd", chosen, w_gen, preferred_element_type=F32).astype(BF16)
    kern = kern.reshape(BANDS * PIX, width)
    place = jnp.arange(ROWS)
    live = ((place < lengths[0]) | ((place >= 256) & (place < SEQ))).astype(F32)
    meta_row = jnp.dot(meta, w_meta, precision=highest)[0]
    rows_in = jnp.stack([gain_one, shift_one, gain_two, shift_two, b_down, cls_token, meta_row, meta_row])
    operands = (
        patches[0],
        kern,
        positions,
        rows_in,
        meta.reshape(-1, 1),
        live[None, :],
        live[:, None],
        jnp.pad(select.astype(BF16), ((0, 16 - BANDS), (0, 0))),
        w_qkv,
        w_out,
        w_up,
        b_up[None, :],
        w_down,
        cotangent[0],
    )
    output, grad_patches, smalls, down, up, attn, table = layer(dp_count, width, operands)
    grad_w_down, grad_w_up, attn = (x[:768].astype(F32) for x in (down, up, attn))
    table = table[: 2 * width].reshape(2, width, NB // 2, PIX)
    low_halves = hidden_low.reshape(2, NB // 2, HYP)
    grad_w_gen = jnp.einsum("anh,adnp->dph", low_halves, table, preferred_element_type=F32)
    hidden_part = jnp.einsum("adnp,dph->anh", table, w_gen, preferred_element_type=F32)
    grad_hidden = small_sum(hidden_part.reshape(NB, HYP), "mp", 4, 1)
    grad_inner = hyper_pull(grad_hidden)[0]
    grad_w_hyper = jnp.dot(features.T, grad_inner, precision=highest)
    grad_b_hyper = jnp.sum(grad_inner, axis=0)
    return (
        output[None],
        grad_patches[None],
        grad_w_hyper,
        grad_b_hyper,
        grad_w_gen,
        smalls[4],
        smalls[8:16],
        smalls[0],
        smalls[1],
        attn[width : 4 * width].reshape(3, width, D),
        attn[:width],
        smalls[2],
        smalls[3],
        grad_w_up,
        smalls[6],
        grad_w_down,
        smalls[5],
    )


def solution(mesh):
    return jax.shard_map(
        functools.partial(local, mesh.shape["dp"]),
        mesh=mesh,
        in_specs=(
            P("dp", None, None),
            P(),
            P(),
            P(),
            P("dp"),
            P("dp"),
            P("dp", None),
            P("dp", None),
            P(),
            P(),
            P("mp", None, None),
            P(),
            P(),
            P(),
            P(),
            P(None, "mp", None),
            P("mp", None),
            P(),
            P(),
            P(None, "mp"),
            P("mp"),
            P("mp", None),
            P(),
            P("dp", None, None),
        ),
        out_specs=(
            P("dp", None, None),
            P("dp", None, None),
            P(),
            P(),
            P("mp", None, None),
            P(),
            P(),
            P(),
            P(),
            P(None, "mp", None),
            P("mp", None),
            P(),
            P(),
            P(None, "mp"),
            P("mp"),
            P("mp", None),
            P(),
        ),
        check_vma=False,
    )
```

```python
import functools
import math

import jax
import jax.numpy as jnp
from jax import lax
from jax.experimental import pallas as pl
from jax.experimental.pallas import tpu as pltpu
from jax.sharding import PartitionSpec as P

F32 = jnp.float32
BF16 = jnp.bfloat16
MESH = pl.DeviceIdType.MESH

D = 768
HEAD_DIM = 64
PIX = 64
HYP = 128
BANDS = 13
NB = 32
SENSORS = 4
VIS_MAX = 256
SEQ = 258


def sinus_waves(wavelengths, width):
    half_width = width // 2
    steps = jnp.arange(half_width, dtype=jnp.float32)
    freqs = jnp.exp(steps * (6.0 * math.log(2.0) / half_width))
    angles = wavelengths[:, None] * freqs[None, :]
    return jnp.concatenate([jnp.sin(angles), jnp.cos(angles)], axis=1)


def grid_codes(visible, lengths, width, most):
    short_side = math.isqrt(most)
    long_side = 2 * short_side
    sides = jnp.where(lengths == most, long_side, short_side).astype(jnp.int32)[:, None]
    grid_rows = (visible // sides).astype(jnp.float32)
    grid_cols = (visible % sides).astype(jnp.float32)
    quarter = width // 4
    omegas = jnp.exp(jnp.arange(quarter, dtype=jnp.float32) * (-math.log(10000.0) / quarter))
    row_angle = grid_rows[..., None] * omegas
    col_angle = grid_cols[..., None] * omegas
    return jnp.concatenate(
        [jnp.sin(row_angle), jnp.cos(row_angle), jnp.sin(col_angle), jnp.cos(col_angle)], axis=-1
    )


def gelu_exact(values):
    return jax.nn.gelu(values, approximate=False)


def remote(src, dst, send_sem, recv_sem, device):
    return pltpu.make_async_remote_copy(
        src_ref=src,
        dst_ref=dst,
        send_sem=send_sem,
        recv_sem=recv_sem,
        device_id=device,
        device_id_type=MESH,
    )


def greet(devices):
    barrier = pltpu.get_barrier_semaphore()
    for device in devices:
        pl.semaphore_signal(barrier, inc=1, device_id=device, device_id_type=MESH)
    pl.semaphore_wait(barrier, len(devices))


def mp_peers():
    place = lax.axis_index("mp")
    core = lax.rem(place, 2)
    return core, {"mp": place + 1 - 2 * core}, {"mp": lax.rem(place + 2, 4)}


class Sender:
    def __init__(self, sends, recvs):
        self.sends, self.recvs, self.copies = sends, recvs, []

    def go(self, number, src, dst, device):
        copy = remote(src, dst, self.sends.at[number], self.recvs.at[number], device)
        copy.start()
        self.copies.append(copy)
        return copy

    def finish(self):
        for copy in self.copies:
            copy.wait_send()


class MpSum(Sender):
    def __init__(self, part, slots, out, cuts, sends, recvs):
        super().__init__(sends, recvs)
        self.part, self.out, self.cuts = part, out, cuts
        self.pair_in, self.chip_sum, self.far_in, self.other_near, self.other_far = slots
        self.core, self.pair, self.far = mp_peers()
        self.first, self.second, self.third = {}, {}, {}

    def number(self, step, i):
        return step * len(self.cuts) + i

    def start(self, i):
        rows = pl.ds(*self.cuts[i])
        self.first[i] = self.go(
            self.number(0, i), self.part.at[1 - self.core, rows], self.pair_in.at[rows], self.pair
        )

    def relay(self, i):
        rows = pl.ds(*self.cuts[i])
        self.first[i].wait_recv()
        self.chip_sum[rows] = (
            self.part[self.core, rows].astype(F32) + self.pair_in[rows].astype(F32)
        ).astype(BF16)
        mine = self.chip_sum.at[rows]
        self.second[i] = (
            self.go(self.number(1, i), mine, self.far_in.at[rows], self.far),
            self.go(self.number(2, i), mine, self.other_near.at[rows], self.pair),
        )

    def forward(self, i):
        rows = pl.ds(*self.cuts[i])
        self.second[i][0].wait_recv()
        self.third[i] = self.go(
            self.number(3, i), self.far_in.at[rows], self.other_far.at[rows], self.pair
        )
        self.out[self.core, rows] = self.chip_sum[rows].astype(F32) + self.far_in[rows].astype(F32)

    def total(self, i):
        rows = pl.ds(*self.cuts[i])
        self.second[i][1].wait_recv()
        self.third[i].wait_recv()
        self.out[1 - self.core, rows] = self.other_near[rows].astype(F32) + self.other_far[
            rows
        ].astype(F32)


class DpPlace:
    def __init__(self, lines):
        place = lax.axis_index("dp")
        self.lines = lines
        self.inner = lax.rem(place, 2)
        self.outer = place // 2
        self.pair = {"dp": self.outer * 2 + 1 - self.inner}

    def peer(self, k):
        return {"dp": lax.rem(self.outer + k, self.lines) * 2 + self.inner}


class Chain:
    def __init__(self, place, sends, recvs):
        self.place, self.sends, self.recvs = place, sends, recvs
        self.ends = []
        self.low = place.outer < (place.lines + 1) // 2
        self.depth = jnp.where(self.low, place.outer, place.lines - 1 - place.outer)

    def copy(self, number, src, dst, device):
        return remote(src, dst, self.sends.at[number], self.recvs.at[number], device)

    def start(self, copy, cond=None):
        if cond is None:
            copy.start()
        else:
            pl.when(cond)(copy.start)
        self.ends.append((copy, cond))

    def next_to(self, up):
        place = self.place
        outer = jnp.where(up, place.outer + 1, place.outer - 1)
        outer = jnp.clip(outer, 0, place.lines - 1)
        return {"dp": outer * 2 + place.inner}

    def finish(self):
        for copy, cond in self.ends:
            if cond is None:
                copy.wait_send()
            else:
                pl.when(cond)(copy.wait_send)

    def hop(self, flow, i, outward):
        lines = self.place.lines
        up = self.low if outward else jnp.logical_not(self.low)
        way = jnp.where(up, 0, 1)
        chunk = jnp.where(up, lines - 1 - i, i)
        slot = flow.at[way, chunk]
        return slot, chunk, self.copy(way * lines + chunk, slot, slot, self.next_to(up))

    def out(self, own, flow):
        for i in range(self.place.lines - 1):
            slot, chunk, copy = self.hop(flow, i, True)

            @pl.when(self.depth == 0)
            def _(slot=slot, chunk=chunk):
                slot[...] = own[chunk]

            self.start(copy, self.depth == 0)

    def on(self, own, flow, i, outward):
        slot, chunk, copy = self.hop(flow, i, outward)
        inner = i < self.place.lines - 1 - self.depth if outward else i < self.depth
        active = jnp.logical_and(self.depth > 0, inner)

        @pl.when(active)
        def _():
            copy.wait_recv()
            slot[...] = (slot[...].astype(F32) + own[chunk].astype(F32)).astype(BF16)

        self.start(copy, active)

    def sum_steps(self, own, flow):
        lines = self.place.lines
        steps = [functools.partial(self.out, own, flow)]
        for i in range(lines - 2):
            steps.append(functools.partial(self.on, own, flow, i, True))
            if i < (lines + 1) // 2 - 1:
                steps.append(functools.partial(self.on, own, flow, i, False))
        return steps

    def sum_end(self, own, flow, total):
        lines, z = self.place.lines, self.place.outer
        total[...] = own[z].astype(F32)
        for way, cond in ((0, z > 0), (1, z < lines - 1)):
            slot = flow.at[way, z]
            copy = self.copy(way * lines + z, slot, slot, self.next_to(z > 0))

            @pl.when(cond)
            def _(slot=slot, copy=copy):
                copy.wait_recv()
                total[...] += slot[...].astype(F32)

    def spread_start(self, whole, base):
        lines, z = self.place.lines, self.place.outer
        mine = whole.at[z]
        self.start(self.copy(base + z, mine, mine, self.next_to(True)), z < lines - 1)
        self.start(self.copy(base + z, mine, mine, self.next_to(False)), z > 0)

    def spread_step(self, whole, base, r, then=None):
        lines, z = self.place.lines, self.place.outer
        for up, chunk, cond, more in (
            (True, z - r, z - r >= 0, z < lines - 1),
            (False, z + r, z + r < lines, z > 0),
        ):
            chunk = jnp.clip(chunk, 0, lines - 1)
            slot = whole.at[chunk]
            copy = self.copy(base + chunk, slot, slot, self.next_to(up))
            pl.when(cond)(copy.wait_recv)
            self.start(copy, jnp.logical_and(cond, more))
            if then is not None:
                then(chunk, slot, cond)


class PairFirst(Chain):
    def __init__(self, place, grad, scratch, whole, sends, recvs):
        super().__init__(place, sends, recvs)
        self.grad, self.whole = grad, whole.at[place.inner]
        self.pair_in, self.half, self.flow, self.total = scratch
        lines = place.lines
        steps = [self.pair_start, self.pair_end] + self.sum_steps(self.half, self.flow)
        steps.append(self.line_end)
        for r in range(1, lines):
            steps.append(functools.partial(self.spread_step, self.whole, 2 * lines, r, self.to_pair))
        steps.append(self.end)
        self.steps = steps

    def pair_start(self):
        place = self.place
        copy = self.copy(4 * place.lines, self.grad.at[1 - place.inner], self.pair_in, place.pair)
        self.first = copy
        self.start(copy)

    def pair_end(self):
        self.first.wait_recv()
        for z in range(self.place.lines):
            self.half[z] = (
                self.grad[self.place.inner, z].astype(F32) + self.pair_in[z].astype(F32)
            ).astype(BF16)

    def to_pair(self, chunk, slot, cond=None):
        self.start(self.copy(3 * self.place.lines + chunk, slot, slot, self.place.pair), cond)

    def line_end(self):
        z = self.place.outer
        self.sum_end(self.half, self.flow, self.total)
        self.whole[z] = self.total[...].astype(BF16)
        self.spread_start(self.whole, 2 * self.place.lines)
        self.to_pair(z, self.whole.at[z])

    def end(self):
        for z in range(self.place.lines):
            slot = self.whole.at[z]
            self.copy(3 * self.place.lines + z, slot, slot, self.place.pair).wait_recv()
        self.finish()


class LineFirst(Chain):
    def __init__(self, place, grad, scratch, whole, sends, recvs):
        super().__init__(place, sends, recvs)
        self.grad, self.whole = grad, whole
        self.flow, self.total, self.mine, self.pair_in = scratch
        lines = place.lines
        steps = self.sum_steps(self.grad, self.flow)
        steps += [self.pair_start, self.pair_end]
        for r in range(1, lines):
            steps.append(functools.partial(self.spread_step, self.whole, 2 * lines, r))
        steps.append(self.finish)
        self.steps = steps

    def pair_start(self):
        self.sum_end(self.grad, self.flow, self.total)
        self.mine[...] = self.total[...].astype(BF16)
        copy = self.copy(4 * self.place.lines, self.mine, self.pair_in, self.place.pair)
        self.first = copy
        self.start(copy)

    def pair_end(self):
        self.first.wait_recv()
        self.whole[self.place.outer] = (
            self.mine[...].astype(F32) + self.pair_in[...].astype(F32)
        ).astype(BF16)
        self.spread_start(self.whole, 2 * self.place.lines)


class SmallSum(Sender):
    def __init__(self, place, part, pair_in, line_in, out, sends, recvs):
        super().__init__(sends, recvs)
        self.place, self.part, self.pair_in, self.line_in, self.out = place, part, pair_in, line_in, out

    def start(self):
        self.first = self.go(0, self.part, self.pair_in, self.place.pair)

    def relay(self):
        place, lines = self.place, self.place.lines
        self.first.wait_recv()
        self.line_in[place.outer] = self.part[...] + self.pair_in[...]
        mine = self.line_in.at[place.outer]
        self.second = [self.go(k, mine, mine, place.peer(k)) for k in range(1, lines)]

    def total(self):
        for copy in self.second:
            copy.wait_recv()
        total = self.line_in[0]
        for z in range(1, self.place.lines):
            total = total + self.line_in[z]
        self.out[...] = total
        self.finish()


def dot(left, right):
    return jnp.dot(left, right, preferred_element_type=F32)


def dot_nt(left, right):
    return lax.dot_general(left, right, (((1,), (1,)), ((), ())), preferred_element_type=F32)


def dot_tn(left, right):
    return lax.dot_general(left, right, (((0,), (0,)), ((), ())), preferred_element_type=F32)


def row_mean(values):
    return jnp.mean(values, axis=-1, keepdims=True)


def col_sum(values):
    return jnp.sum(values, axis=0, keepdims=True)


ROWS = 272
CUTS = [(0, 64), (64, 64), (128, 64), (192, 80)]
PIXEL_CUTS = [(0, 64), (64, 64)]


ORDER = (
    ("embed",),
    ("fillgate",),
    ("sel",),
    ("epass",),
    ("tokens",),
    ("attn",),
    ("apart", 0),
    ("a", "start", 0),
    ("apart", 1),
    ("a", "start", 1),
    ("apart", 2),
    ("a", "start", 2),
    ("apart", 3),
    ("a", "start", 3),
    ("a", "relay", 0),
    ("a", "relay", 1),
    ("a", "relay", 2),
    ("a", "relay", 3),
    ("a", "forward", 0),
    ("a", "forward", 1),
    ("a", "total", 0),
    ("ffn", 0),
    ("a", "total", 1),
    ("a", "forward", 2),
    ("c", "start", 0),
    ("ffn", 1),
    ("a", "forward", 3),
    ("a", "total", 2),
    ("c", "relay", 0),
    ("c", "start", 1),
    ("ffn", 2),
    ("a", "total", 3),
    ("c", "start", 2),
    ("ffn", 3),
    ("c", "relay", 1),
    ("c", "relay", 2),
    ("c", "forward", 0),
    ("c", "start", 3),
    ("gdown", 0),
    ("gdown", 1),
    ("down0",),
    ("c", "total", 0),
    ("down1",),
    ("c", "relay", 3),
    ("gup", 0),
    ("up0",),
    ("c", "forward", 1),
    ("gup", 1),
    ("up1",),
    ("c", "forward", 2),
    ("ln2b", 0),
    ("c", "total", 1),
    ("ln2b", 1),
    ("c", "total", 2),
    ("c", "forward", 3),
    ("ln2b", 2),
    ("branch",),
    ("c", "total", 3),
    ("ln2b", 3),
    ("gmix",),
    ("head", 0),
    ("down0",),
    ("down0",),
    ("up1",),
    ("head", 1),
    ("head", 2),
    ("npart", 0),
    ("d", "start", 0),
    ("npart", 1),
    ("d", "start", 1),
    ("npart", 2),
    ("d", "start", 2),
    ("npart", 3),
    ("d", "start", 3),
    ("gattn", 0),
    ("d", "relay", 0),
    ("d", "relay", 1),
    ("d", "relay", 2),
    ("down1",),
    ("d", "relay", 3),
    ("down0",),
    ("down1",),
    ("up1",),
    ("up1",),
    ("attn0",),
    ("gattn", 1),
    ("attn1",),
    ("b", "start", 0),
    ("b", "start", 1),
    ("b", "start", 2),
    ("b", "start", 3),
    ("d", "forward", 0),
    ("b", "relay", 0),
    ("b", "relay", 1),
    ("b", "relay", 2),
    ("d", "forward", 1),
    ("down0",),
    ("down0",),
    ("b", "relay", 3),
    ("d", "total", 0),
    ("ln1b", 0),
    ("d", "forward", 2),
    ("down1",),
    ("d", "total", 1),
    ("ln1b", 1),
    ("d", "forward", 3),
    ("up0",),
    ("d", "total", 2),
    ("up0",),
    ("ln1b", 2),
    ("up1",),
    ("d", "total", 3),
    ("ln1b", 3),
    ("table",),
    ("down0",),
    ("table0",),
    ("down1",),
    ("down1",),
    ("up0",),
    ("sready",),
    ("small", "start"),
    ("pix",),
    ("e", "start", 0),
    ("e", "start", 1),
    ("b", "forward", 0),
    ("b", "forward", 1),
    ("b", "forward", 2),
    ("b", "forward", 3),
    ("attn0",),
    ("attn0",),
    ("e", "relay", 0),
    ("e", "relay", 1),
    ("b", "total", 0),
    ("b", "total", 1),
    ("b", "total", 2),
    ("b", "total", 3),
    ("outp",),
    ("down0",),
    ("down1",),
    ("attn0",),
    ("up0",),
    ("up0",),
    ("e", "forward", 0),
    ("attn1",),
    ("down0",),
    ("attn1",),
    ("e", "total", 0),
    ("e", "forward", 1),
    ("e", "total", 1),
    ("down1",),
    ("pixout",),
    ("up1",),
    ("attn0",),
    ("attn0",),
    ("attn1",),
    ("down0",),
    ("up0",),
    ("down1",),
    ("up1",),
    ("attn0",),
    ("attn1",),
    ("attn1",),
    ("table0",),
    ("table0",),
    ("small", "relay"),
    ("down1",),
    ("up0",),
    ("up1",),
    ("table0",),
    ("attn0",),
    ("attn1",),
    ("down0",),
    ("small", "total"),
    ("up0",),
    ("table0",),
    ("table0",),
    ("down1",),
    ("up1",),
    ("up1",),
    ("attn0",),
    ("attn1",),
    ("up0",),
    ("table0",),
    ("attn0",),
    ("attn1",),
    ("up0",),
    ("table0",),
    ("attn1",),
    ("attn0",),
    ("table0",),
    ("attn1",),
    ("table0",),
    ("table0",),
)
KINDS = (
    ("down0", PairFirst),
    ("down1", PairFirst),
    ("up0", PairFirst),
    ("up1", LineFirst),
    ("attn0", PairFirst),
    ("attn1", PairFirst),
    ("table0", PairFirst),
)


def layer_kernel(
    lines,
    kinds,
    patches,
    kern,
    positions,
    rows_in,
    meta_col,
    live_row,
    live_col,
    select,
    w_qkv,
    w_out,
    w_up,
    b_up,
    w_down,
    cotangent,
    output,
    grad_patches,
    smalls,
    wholes,
    embeds,
    tokens,
    xhat_one,
    rstd_one,
    xhat_two,
    rstd_two,
    after,
    normed,
    normed_two,
    queries,
    keys,
    values,
    probs,
    mixed,
    grad_mixed,
    grad_qkv,
    branch_grad,
    gate_grad,
    activation,
    grad_pre,
    grad_after,
    after_low,
    grad_tokens,
    embed_grad,
    spread,
    part_a,
    part_b,
    part_c,
    part_d,
    part_e,
    slots_a,
    slots_b,
    slots_c,
    slots_d,
    slots_e,
    out_a,
    out_b,
    out_c,
    out_d,
    out_e,
    grads,
    slots,
    small_part,
    small_pair,
    small_line,
    mp_sends,
    mp_recvs,
    dp_sends,
    dp_recvs,
    etc_sends,
    etc_recvs,
):
    core, pair, far = mp_peers()
    place = DpPlace(lines)
    greet([pair, far, place.pair] + [place.peer(k) for k in range(1, lines)])
    me = lax.axis_index("mp")
    width = w_out.shape[0]
    heads = width // HEAD_DIM
    full = D

    def mp_sum(part, slots, out, cuts, number):
        return MpSum(
            part,
            [slots.at[k] for k in range(5)],
            out,
            cuts,
            mp_sends.at[number],
            mp_recvs.at[number],
        )

    sum_a = mp_sum(part_a, slots_a, out_a, CUTS, 0)
    sum_b = mp_sum(part_b, slots_b, out_b, CUTS, 1)
    sum_c = mp_sum(part_c, slots_c, out_c, CUTS, 2)
    sum_d = mp_sum(part_d, slots_d, out_d, CUTS, 3)
    sum_e = mp_sum(part_e, slots_e, out_e, PIXEL_CUTS, 4)

    pieces = {}
    for number, (name, kind) in enumerate(kinds):
        pieces[name] = kind(
            place,
            grads[number],
            slots[number],
            wholes[number],
            dp_sends.at[number],
            dp_recvs.at[number],
        )
    small = SmallSum(place, small_part, small_pair, small_line, smalls, dp_sends.at[len(kinds)], dp_recvs.at[len(kinds)])

    def put_piece(grad, first_row, block):
        rows = grad.shape[-2]
        for k in range(0, block.shape[0], rows):
            chunk = (first_row + k) // rows
            spot = (chunk,) if len(grad.shape) == 3 else (chunk // lines, chunk % lines)
            grad[spot] = block[k : k + rows].astype(BF16)

    gain_one, shift_one = rows_in[0:1], rows_in[1:2]
    gain_two, shift_two = rows_in[2:3], rows_in[3:4]
    b_down = rows_in[4:5]
    lane_head = lax.broadcasted_iota(jnp.int32, (1, width), 1) // HEAD_DIM
    head_masks = [(lane_head == h).astype(F32).astype(BF16) for h in range(heads)]

    etc = Sender(etc_sends, etc_recvs)
    kept = {}

    def embed():
        embeds[me] = dot(patches[...], kern[...]).astype(BF16)
        mine = embeds.at[me]
        kept["pair"] = etc.go(0, mine, mine, pair)
        kept["far"] = etc.go(1, mine, mine, far)

    def epass():
        kept["far"].wait_recv()
        got = embeds.at[lax.rem(me + 2, 4)]
        kept["passed"] = etc.go(2, got, got, pair)

    def fillgate():
        branch_grad[0:256] = (live_col[0:256] * cotangent[2:258]).astype(BF16)
        branch_grad[256:272] = jnp.concatenate(
            [cotangent[0:2], jnp.zeros((14, full), F32)], axis=0
        ).astype(BF16)
        small_part[...] = jnp.zeros_like(small_part)
        small_part[5:6] = col_sum(branch_grad[...].astype(F32))
        gate_grad[...] = dot_nt(branch_grad[...], w_down[...])

    def tokens_norm():
        kept["pair"].wait_recv()
        kept["passed"].wait_recv()
        for lo, n in CUTS:
            hi = min(lo + n, 256)
            for i in range(4):
                cols = slice(i * width, (i + 1) * width)
                tokens[lo:hi, cols] = embeds[i, lo:hi].astype(F32)
            tokens[lo:hi] += positions[lo:hi]
            if lo + n > 256:
                tokens[256:272] = jnp.concatenate([rows_in[5:7], jnp.zeros((14, full), F32)], axis=0)
            rows = slice(lo, lo + n)
            x = tokens[rows]
            centred = x - row_mean(x)
            rstd = lax.rsqrt(row_mean(centred * centred) + 1e-05)
            rstd_one[rows] = rstd
            xhat = centred * rstd
            xhat_one[rows] = xhat
            normed[rows] = (xhat * gain_one + shift_one).astype(BF16)

    def attention():
        queries[...] = dot_nt(normed[...], w_qkv[0]).astype(BF16)
        keys[...] = dot_nt(normed[...], w_qkv[1]).astype(BF16)
        values[...] = dot_nt(normed[...], w_qkv[2]).astype(BF16)
        live_keys = live_row[...] > 0
        total = None
        for h in range(heads):
            raw = dot_nt(queries[...] * head_masks[h], keys[...]) * 0.125
            raw = jnp.where(live_keys, raw, -1000000000.0)
            expo = jnp.exp(raw - jnp.max(raw, axis=-1, keepdims=True))
            prob = expo / jnp.sum(expo, axis=-1, keepdims=True)
            probs[h] = prob
            term = dot(prob.astype(BF16), values[...] * head_masks[h])
            total = term if total is None else total + term
        mixed[...] = total.astype(BF16)

    def put_part(part, rows, block):
        half = block.shape[1] // 2
        part[0, rows] = block[:, :half].astype(BF16)
        part[1, rows] = block[:, half:].astype(BF16)

    def get_out(out, rows):
        return jnp.concatenate([out[0, rows], out[1, rows]], axis=1)

    def span(i):
        lo, n = CUTS[i]
        return slice(lo, lo + n)

    def attn_part(i):
        put_part(part_a, span(i), dot(mixed[span(i)], w_out[...]))

    def feedforward(i):
        rows = span(i)
        x = tokens[rows] + get_out(out_a, rows)
        after[rows] = x
        centred = x - row_mean(x)
        rstd = lax.rsqrt(row_mean(centred * centred) + 1e-05)
        rstd_two[rows] = rstd
        xhat = centred * rstd
        xhat_two[rows] = xhat
        normed_two[rows] = (xhat * gain_two + shift_two).astype(BF16)
        gate = dot(normed_two[rows], w_up[...]) + b_up[...]
        cdf = 0.5 + 0.5 * lax.erf(gate * (2.0**-0.5))
        activation[rows] = (gate * cdf).astype(BF16)
        pdf = jnp.exp(-0.5 * gate * gate) * ((2.0 * math.pi) ** -0.5)
        grad_pre[rows] = (gate_grad[rows] * (cdf + gate * pdf)).astype(BF16)
        put_part(part_c, rows, dot_nt(grad_pre[rows], w_up[...]))

    half = full // 2

    def grad_of_down(j):
        cols = slice(j * half, (j + 1) * half)
        put_piece(pieces[f"down{j}"].grad, 0, dot_tn(activation[...], branch_grad[:, cols]))

    def grad_of_up(j):
        cols = slice(j * half, (j + 1) * half)
        put_piece(pieces[f"up{j}"].grad, 0, dot_tn(normed_two[...], grad_pre[:, cols]))
        if j == 1:
            small_part[6:7] = col_sum(grad_pre[...].astype(F32))

    def norm_two_back(i):
        rows = span(i)
        lo, n = CUTS[i]
        dy = get_out(out_c, rows)
        xhat = xhat_two[rows]
        small_part[2:3] += col_sum(dy * xhat)
        small_part[3:4] += col_sum(dy)
        e = dy * gain_two
        dx = rstd_two[rows] * (e - row_mean(e) - xhat * row_mean(e * xhat))
        if lo + n <= 256:
            grad_out = live_col[rows] * cotangent[lo + 2 : lo + n + 2]
        else:
            grad_out = jnp.concatenate(
                [live_col[lo:256] * cotangent[lo + 2 : 258], cotangent[0:2], jnp.zeros((14, full), F32)],
                axis=0,
            )
        grad_x = dx + grad_out
        grad_after[rows] = grad_x
        after_low[rows] = grad_x.astype(BF16)

    def mixed_back():
        grad_mixed[...] = dot_nt(after_low[...], w_out[...]).astype(BF16)
        kept["parts"] = [None, None, None]

    def head_back(h):
        mixed_h = grad_mixed[...] * head_masks[h]
        grad_probs = dot_nt(mixed_h, values[...])
        prob = probs[h]
        scores = prob * (grad_probs - jnp.sum(grad_probs * prob, axis=-1, keepdims=True))
        scores = scores.astype(BF16)
        terms = [
            dot(scores, keys[...] * head_masks[h]),
            dot_tn(scores, queries[...] * head_masks[h]),
            dot_tn(prob.astype(BF16), mixed_h),
        ]
        kept["parts"] = [t if p is None else p + t for p, t in zip(kept["parts"], terms)]
        if h == heads - 1:
            for t, scale in enumerate((0.125, 0.125, 1.0)):
                grad_qkv[t] = (kept["parts"][t] * scale).astype(BF16)

    def norm_part(i):
        rows = span(i)
        block = dot(grad_qkv[0, rows], w_qkv[0])
        block = block + dot(grad_qkv[1, rows], w_qkv[1])
        put_part(part_d, rows, block + dot(grad_qkv[2, rows], w_qkv[2]))

    def grad_of_attn(j):
        cols = slice(j * half, (j + 1) * half)
        grad = pieces[f"attn{j}"].grad
        put_piece(grad, 0, dot_tn(mixed[...], after_low[:, cols]))
        for t in range(3):
            put_piece(grad, (t + 1) * width, dot_tn(grad_qkv[t], normed[:, cols]))

    wide = NB * PIX

    def selection():
        band = lax.broadcasted_iota(jnp.int32, (BANDS * PIX, 16), 0) // PIX
        slot = lax.broadcasted_iota(jnp.int32, (BANDS * PIX, 16), 1)
        row_select = dot((band == slot).astype(F32).astype(BF16), select[...]).astype(BF16)
        table_band = lax.broadcasted_iota(jnp.int32, (NB, wide), 0)
        table_lane = lax.broadcasted_iota(jnp.int32, (NB, wide), 1) // PIX
        widen = (table_band == table_lane).astype(F32).astype(BF16)
        for b in range(BANDS):
            rows = slice(b * PIX, (b + 1) * PIX)
            spot = lax.broadcasted_iota(jnp.int32, (PIX, wide), 0)
            lane = lax.rem(lax.broadcasted_iota(jnp.int32, (PIX, wide), 1), PIX)
            block = dot(row_select[rows], widen)
            spread[rows] = jnp.where(spot == lane, block, 0.0).astype(BF16)

    def norm_one_back(i):
        rows = span(i)
        dy = get_out(out_d, rows)
        xhat = xhat_one[rows]
        small_part[0:1] += col_sum(dy * xhat)
        small_part[1:2] += col_sum(dy)
        e = dy * gain_one
        dx = rstd_one[rows] * (e - row_mean(e) - xhat * row_mean(e * xhat))
        grad_tokens[rows] = grad_after[rows] + dx

    def table_grad():
        for i in range(4):

            @pl.when(me == i)
            def _():
                embed_grad[...] = grad_tokens[0:256, i * width : (i + 1) * width].astype(BF16)

        grad_kern = dot_tn(embed_grad[...], patches[...]).astype(BF16)
        table = dot(grad_kern, spread[...])
        put_piece(pieces["table0"].grad, 0, table[:, : wide // 2])
        put_piece(pieces["table0"].grad, width, table[:, wide // 2 :])

    def small_ready():
        small_part[4:5] = grad_tokens[256:257]
        small_part[8:16] = meta_col[...] * grad_tokens[257:258]

    def pixel_part():
        pixels = dot_nt(embed_grad[...], kern[...]).astype(BF16)
        part_e[0] = pixels[:128]
        part_e[1] = pixels[128:]

    def branch_part():
        for i in range(len(CUTS)):
            put_part(part_b, span(i), dot(activation[span(i)], w_down[...]))

    def final_output():
        for i, (lo, n) in enumerate(CUTS):
            rows = span(i)
            x = after[rows] + get_out(out_b, rows) + b_down
            if lo + n <= 256:
                output[lo + 2 : lo + n + 2] = live_col[rows] * x
            else:
                output[lo + 2 : 258] = live_col[lo:256] * x[: 256 - lo]
                output[0:2] = x[256 - lo : 258 - lo]

    def final_pixels():
        grad_patches[0:128] = out_e[0]
        grad_patches[128:256] = out_e[1]

    tasks = {
        "embed": embed,
        "epass": epass,
        "fillgate": fillgate,
        "tokens": tokens_norm,
        "attn": attention,
        "apart": attn_part,
        "ffn": feedforward,
        "gdown": grad_of_down,
        "gup": grad_of_up,
        "ln2b": norm_two_back,
        "gmix": mixed_back,
        "head": head_back,
        "npart": norm_part,
        "gattn": grad_of_attn,
        "sel": selection,
        "ln1b": norm_one_back,
        "table": table_grad,
        "sready": small_ready,
        "pix": pixel_part,
        "branch": branch_part,
        "outp": final_output,
        "pixout": final_pixels,
        "small": small,
        "a": sum_a,
        "b": sum_b,
        "c": sum_c,
        "d": sum_d,
        "e": sum_e,
    }
    for name, *args in ORDER:
        if name in pieces:
            steps = pieces[name].steps
            if steps:
                steps.pop(0)()
        elif args and isinstance(args[0], str):
            getattr(tasks[name], args[0])(*args[1:])
        else:
            tasks[name](*args)
    while any(piece.steps for piece in pieces.values()):
        for piece in pieces.values():
            if piece.steps:
                piece.steps.pop(0)()
    for one in (sum_a, sum_b, sum_c, sum_d, sum_e, etc):
        one.finish()


def layer(dp_count, width, operands):
    lines = dp_count // 2

    def piece(rows, lanes, parts):
        chunk = -(-rows // parts)
        chunk = -(-chunk // 16) * 16
        if parts == lines:
            return (lines, chunk, lanes)
        return (2, lines, chunk, lanes)

    pieces = []
    for name, kind in KINDS:
        parts = dp_count if kind is PairFirst else lines
        if name == "table0":
            pieces.append(piece(2 * width, NB * PIX // 2, parts))
        else:
            pieces.append(piece(4 * width, D // 2, parts))

    def piece_scratch(shape):
        if len(shape) == 4:
            return [low(*shape[1:]), low(*shape[1:]), low(2, *shape[1:]), vmem(*shape[2:])]
        return [low(2, *shape), vmem(*shape[1:]), low(*shape[1:]), low(*shape[1:])]

    half = D // 2
    pixel_lanes = BANDS * PIX

    def vmem(*shape, dtype=F32):
        return pltpu.VMEM(shape, dtype)

    def low(*shape):
        return pltpu.VMEM(shape, BF16)

    scratch = [
        low(4, 256, width),
        vmem(ROWS, D),
        vmem(ROWS, D),
        vmem(ROWS, 1),
        vmem(ROWS, D),
        vmem(ROWS, 1),
        vmem(ROWS, D),
        low(ROWS, D),
        low(ROWS, D),
        low(ROWS, width),
        low(ROWS, width),
        low(ROWS, width),
        vmem(width // HEAD_DIM, ROWS, ROWS),
        low(ROWS, width),
        low(ROWS, width),
        low(3, ROWS, width),
        low(ROWS, D),
        vmem(ROWS, D),
        low(ROWS, D),
        low(ROWS, D),
        vmem(ROWS, D),
        low(ROWS, D),
        vmem(ROWS, D),
        low(256, width),
        low(pixel_lanes, NB * PIX),
    ]
    scratch += [low(2, ROWS, half)] * 4 + [low(2, 128, pixel_lanes)]
    scratch += [low(5, ROWS, half)] * 4 + [low(5, 128, pixel_lanes)]
    scratch += [vmem(2, ROWS, half)] * 4 + [vmem(2, 128, pixel_lanes)]
    scratch.append([low(*shape) for shape in pieces])
    scratch.append([piece_scratch(shape) for shape in pieces])
    scratch += [vmem(16, D), vmem(16, D), vmem(lines, 16, D)]
    dma = pltpu.SemaphoreType.DMA
    scratch += [dma((5, 16)), dma((5, 16)), dma((len(pieces) + 1, 4 * lines + 1)), dma((len(pieces) + 1, 4 * lines + 1)), dma((3,)), dma((3,))]
    ref = pl.BlockSpec(memory_space=pltpu.VMEM)
    shapes = [
        jax.ShapeDtypeStruct((SEQ, D), F32),
        jax.ShapeDtypeStruct((256, pixel_lanes), F32),
        jax.ShapeDtypeStruct((16, D), F32),
        [jax.ShapeDtypeStruct(shape, BF16) for shape in pieces],
    ]
    output, grad_patches, smalls, wholes = pl.pallas_call(
        functools.partial(layer_kernel, lines, KINDS),
        out_shape=shapes,
        in_specs=[ref] * len(operands),
        out_specs=[ref] * 3 + [[ref] * len(pieces)],
        scratch_shapes=scratch,
        compiler_params=pltpu.CompilerParams(
            collective_id=0, has_side_effects=True, vmem_limit_bytes=62 * 1024 * 1024
        ),
        name="layer",
    )(*operands)
    wholes = {name: out.reshape(-1, out.shape[-1]) for (name, kind), out in zip(KINDS, wholes)}
    return output, grad_patches, smalls, wholes


def small_sum_kernel(axis, count, part, out, slots, sends, recvs):
    me = lax.axis_index(axis)
    peers = [{axis: lax.rem(me + k, count)} for k in range(1, count)]
    greet(peers)
    copies = []
    for k, peer in enumerate(peers):
        copy = remote(part, slots.at[me], sends.at[k], recvs.at[k], peer)
        copy.start()
        copies.append(copy)
    slots[me] = part[...]
    for copy in copies:
        copy.wait()
    total = slots[0]
    for k in range(1, count):
        total = total + slots[k]
    out[...] = total


def small_sum(part, axis, count, number):
    vmem = pl.BlockSpec(memory_space=pltpu.VMEM)
    return pl.pallas_call(
        functools.partial(small_sum_kernel, axis, count),
        out_shape=jax.ShapeDtypeStruct(part.shape, F32),
        in_specs=[vmem],
        out_specs=vmem,
        scratch_shapes=[
            pltpu.VMEM((count,) + part.shape, F32),
            pltpu.SemaphoreType.DMA((count - 1,)),
            pltpu.SemaphoreType.DMA((count - 1,)),
        ],
        compiler_params=pltpu.CompilerParams(collective_id=number, has_side_effects=True),
        name="small_sum_" + axis,
    )(part)


def local(
    dp_count,
    patches,
    wavelengths,
    band_ids,
    band_mask,
    sensor,
    lengths,
    visible,
    meta,
    w_hyper,
    b_hyper,
    w_gen,
    cls_token,
    w_meta,
    gain_one,
    shift_one,
    w_qkv,
    w_out,
    gain_two,
    shift_two,
    w_up,
    b_up,
    w_down,
    b_down,
    cotangent,
):
    highest = lax.Precision.HIGHEST
    width = w_gen.shape[0]
    features = sinus_waves(wavelengths, HYP)
    positions = grid_codes(visible, lengths, D, VIS_MAX)[0]
    hyper_pre = jnp.dot(features, w_hyper, precision=highest) + b_hyper
    hidden, hyper_pull = jax.vjp(gelu_exact, hyper_pre)
    hidden_low = hidden.astype(BF16)
    ids, mask = band_ids[sensor[0]], band_mask[sensor[0]]
    select = (ids[:, None] == jnp.arange(NB)[None, :]).astype(F32) * mask[:, None].astype(F32)
    chosen = jnp.dot(select.astype(BF16), hidden_low, preferred_element_type=F32).astype(BF16)
    kern = jnp.einsum("bh,dph->bpd", chosen, w_gen, preferred_element_type=F32).astype(BF16)
    kern = kern.reshape(BANDS * PIX, width)
    place = jnp.arange(ROWS)
    live = ((place < lengths[0]) | ((place >= 256) & (place < SEQ))).astype(F32)
    meta_row = jnp.dot(meta, w_meta, precision=highest)[0]
    rows_in = jnp.stack([gain_one, shift_one, gain_two, shift_two, b_down, cls_token, meta_row, meta_row])
    operands = (
        patches[0],
        kern,
        positions,
        rows_in,
        meta.reshape(-1, 1),
        live[None, :],
        live[:, None],
        jnp.pad(select.astype(BF16), ((0, 16 - BANDS), (0, 0))),
        w_qkv,
        w_out,
        w_up,
        b_up[None, :],
        w_down,
        cotangent[0],
    )
    output, grad_patches, smalls, wholes = layer(dp_count, width, operands)

    def joined(name):
        halves = [wholes[f"{name}{j}"][: 4 * width] for j in range(2)]
        return jnp.concatenate(halves, axis=1).astype(F32)

    grad_w_down, grad_w_up, attn = joined("down"), joined("up"), joined("attn")
    table = wholes["table0"][: 2 * width].reshape(2, width, NB // 2, PIX)
    low_halves = hidden_low.reshape(2, NB // 2, HYP)
    grad_w_gen = jnp.einsum("anh,adnp->dph", low_halves, table, preferred_element_type=F32)
    hidden_part = jnp.einsum("adnp,dph->anh", table, w_gen, preferred_element_type=F32)
    grad_hidden = small_sum(hidden_part.reshape(NB, HYP), "mp", 4, 1)
    grad_inner = hyper_pull(grad_hidden)[0]
    grad_w_hyper = jnp.dot(features.T, grad_inner, precision=highest)
    grad_b_hyper = jnp.sum(grad_inner, axis=0)
    return (
        output[None],
        grad_patches[None],
        grad_w_hyper,
        grad_b_hyper,
        grad_w_gen,
        smalls[4],
        smalls[8:16],
        smalls[0],
        smalls[1],
        attn[width : 4 * width].reshape(3, width, D),
        attn[:width],
        smalls[2],
        smalls[3],
        grad_w_up,
        smalls[6],
        grad_w_down,
        smalls[5],
    )


def solution(mesh):
    return jax.shard_map(
        functools.partial(local, mesh.shape["dp"]),
        mesh=mesh,
        in_specs=(
            P("dp", None, None),
            P(),
            P(),
            P(),
            P("dp"),
            P("dp"),
            P("dp", None),
            P("dp", None),
            P(),
            P(),
            P("mp", None, None),
            P(),
            P(),
            P(),
            P(),
            P(None, "mp", None),
            P("mp", None),
            P(),
            P(),
            P(None, "mp"),
            P("mp"),
            P("mp", None),
            P(),
            P("dp", None, None),
        ),
        out_specs=(
            P("dp", None, None),
            P("dp", None, None),
            P(),
            P(),
            P("mp", None, None),
            P(),
            P(),
            P(),
            P(),
            P(None, "mp", None),
            P("mp", None),
            P(),
            P(),
            P(None, "mp"),
            P("mp"),
            P("mp", None),
            P(),
        ),
        check_vma=False,
    )
```

```python
import functools
import math

import jax
import jax.numpy as jnp
from jax import lax
from jax.experimental import pallas as pl
from jax.experimental.pallas import tpu as pltpu
from jax.sharding import PartitionSpec as P

F32 = jnp.float32
BF16 = jnp.bfloat16
MESH = pl.DeviceIdType.MESH

D = 768
HEAD_DIM = 64
PIX = 64
HYP = 128
BANDS = 13
NB = 32
SENSORS = 4
VIS_MAX = 256
SEQ = 258


def sinus_waves(wavelengths, width):
    half_width = width // 2
    steps = jnp.arange(half_width, dtype=jnp.float32)
    freqs = jnp.exp(steps * (6.0 * math.log(2.0) / half_width))
    angles = wavelengths[:, None] * freqs[None, :]
    return jnp.concatenate([jnp.sin(angles), jnp.cos(angles)], axis=1)


def grid_codes(visible, lengths, width, most):
    short_side = math.isqrt(most)
    long_side = 2 * short_side
    sides = jnp.where(lengths == most, long_side, short_side).astype(jnp.int32)[:, None]
    grid_rows = (visible // sides).astype(jnp.float32)
    grid_cols = (visible % sides).astype(jnp.float32)
    quarter = width // 4
    omegas = jnp.exp(jnp.arange(quarter, dtype=jnp.float32) * (-math.log(10000.0) / quarter))
    row_angle = grid_rows[..., None] * omegas
    col_angle = grid_cols[..., None] * omegas
    return jnp.concatenate(
        [jnp.sin(row_angle), jnp.cos(row_angle), jnp.sin(col_angle), jnp.cos(col_angle)], axis=-1
    )


def gelu_exact(values):
    return jax.nn.gelu(values, approximate=False)


def remote(src, dst, send_sem, recv_sem, device):
    return pltpu.make_async_remote_copy(
        src_ref=src,
        dst_ref=dst,
        send_sem=send_sem,
        recv_sem=recv_sem,
        device_id=device,
        device_id_type=MESH,
    )


def greet(devices):
    barrier = pltpu.get_barrier_semaphore()
    for device in devices:
        pl.semaphore_signal(barrier, inc=1, device_id=device, device_id_type=MESH)
    pl.semaphore_wait(barrier, len(devices))


def mp_peers():
    place = lax.axis_index("mp")
    core = lax.rem(place, 2)
    return core, {"mp": place + 1 - 2 * core}, {"mp": lax.rem(place + 2, 4)}


class Sender:
    def __init__(self, sends, recvs):
        self.sends, self.recvs, self.copies = sends, recvs, []

    def go(self, number, src, dst, device):
        copy = remote(src, dst, self.sends.at[number], self.recvs.at[number], device)
        copy.start()
        self.copies.append(copy)
        return copy

    def finish(self):
        for copy in self.copies:
            copy.wait_send()


class MpSum(Sender):
    def __init__(self, part, slots, out, cuts, sends, recvs):
        super().__init__(sends, recvs)
        self.part, self.out, self.cuts = part, out, cuts
        self.pair_in, self.chip_sum, self.far_in, self.other_near, self.other_far = slots
        self.core, self.pair, self.far = mp_peers()
        self.first, self.second, self.third = {}, {}, {}

    def number(self, step, i):
        return step * len(self.cuts) + i

    def start(self, i):
        rows = pl.ds(*self.cuts[i])
        self.first[i] = self.go(
            self.number(0, i), self.part.at[1 - self.core, rows], self.pair_in.at[rows], self.pair
        )

    def relay(self, i):
        rows = pl.ds(*self.cuts[i])
        self.first[i].wait_recv()
        self.chip_sum[rows] = (
            self.part[self.core, rows].astype(F32) + self.pair_in[rows].astype(F32)
        ).astype(BF16)
        mine = self.chip_sum.at[rows]
        self.second[i] = (
            self.go(self.number(1, i), mine, self.far_in.at[rows], self.far),
            self.go(self.number(2, i), mine, self.other_near.at[rows], self.pair),
        )

    def forward(self, i):
        rows = pl.ds(*self.cuts[i])
        self.second[i][0].wait_recv()
        self.third[i] = self.go(
            self.number(3, i), self.far_in.at[rows], self.other_far.at[rows], self.pair
        )
        self.out[self.core, rows] = self.chip_sum[rows].astype(F32) + self.far_in[rows].astype(F32)

    def total(self, i):
        rows = pl.ds(*self.cuts[i])
        self.second[i][1].wait_recv()
        self.third[i].wait_recv()
        self.out[1 - self.core, rows] = self.other_near[rows].astype(F32) + self.other_far[
            rows
        ].astype(F32)


class DpPlace:
    def __init__(self, lines):
        place = lax.axis_index("dp")
        self.lines = lines
        self.inner = lax.rem(place, 2)
        self.outer = place // 2
        self.pair = {"dp": self.outer * 2 + 1 - self.inner}

    def peer(self, k):
        return {"dp": lax.rem(self.outer + k, self.lines) * 2 + self.inner}


class Chain:
    def __init__(self, place, sends, recvs):
        self.place, self.sends, self.recvs = place, sends, recvs
        self.ends = []
        self.low = place.outer < (place.lines + 1) // 2
        self.depth = jnp.where(self.low, place.outer, place.lines - 1 - place.outer)

    def copy(self, number, src, dst, device):
        return remote(src, dst, self.sends.at[number], self.recvs.at[number], device)

    def start(self, copy, cond=None):
        if cond is None:
            copy.start()
        else:
            pl.when(cond)(copy.start)
        self.ends.append((copy, cond))

    def next_to(self, up):
        place = self.place
        outer = jnp.where(up, place.outer + 1, place.outer - 1)
        outer = jnp.clip(outer, 0, place.lines - 1)
        return {"dp": outer * 2 + place.inner}

    def step(self):
        if self.steps:
            self.steps.pop(0)()

    def finish(self):
        for copy, cond in self.ends:
            if cond is None:
                copy.wait_send()
            else:
                pl.when(cond)(copy.wait_send)

    def hop(self, flow, i, outward):
        lines = self.place.lines
        up = self.low if outward else jnp.logical_not(self.low)
        way = jnp.where(up, 0, 1)
        chunk = jnp.where(up, lines - 1 - i, i)
        slot = flow.at[way, chunk]
        return slot, chunk, self.copy(way * lines + chunk, slot, slot, self.next_to(up))

    def out(self, own, flow):
        for i in range(self.place.lines - 1):
            slot, chunk, copy = self.hop(flow, i, True)

            @pl.when(self.depth == 0)
            def _(slot=slot, chunk=chunk):
                slot[...] = own[chunk]

            self.start(copy, self.depth == 0)

    def on(self, own, flow, i, outward):
        slot, chunk, copy = self.hop(flow, i, outward)
        inner = i < self.place.lines - 1 - self.depth if outward else i < self.depth
        active = jnp.logical_and(self.depth > 0, inner)

        @pl.when(active)
        def _():
            copy.wait_recv()
            slot[...] = (slot[...].astype(F32) + own[chunk].astype(F32)).astype(BF16)

        self.start(copy, active)

    def sum_steps(self, own, flow):
        lines = self.place.lines
        steps = [functools.partial(self.out, own, flow)]
        for i in range(lines - 2):
            steps.append(functools.partial(self.on, own, flow, i, True))
            if i < (lines + 1) // 2 - 1:
                steps.append(functools.partial(self.on, own, flow, i, False))
        return steps

    def sum_end(self, own, flow, total):
        lines, z = self.place.lines, self.place.outer
        total[...] = own[z].astype(F32)
        for way, cond in ((0, z > 0), (1, z < lines - 1)):
            slot = flow.at[way, z]
            copy = self.copy(way * lines + z, slot, slot, self.next_to(z > 0))

            @pl.when(cond)
            def _(slot=slot, copy=copy):
                copy.wait_recv()
                total[...] += slot[...].astype(F32)

    def spread_start(self, whole, base):
        lines, z = self.place.lines, self.place.outer
        mine = whole.at[z]
        self.start(self.copy(base + z, mine, mine, self.next_to(True)), z < lines - 1)
        self.start(self.copy(base + z, mine, mine, self.next_to(False)), z > 0)

    def spread_step(self, whole, base, r, then=None):
        lines, z = self.place.lines, self.place.outer
        for up, chunk, cond, more in (
            (True, z - r, z - r >= 0, z < lines - 1),
            (False, z + r, z + r < lines, z > 0),
        ):
            chunk = jnp.clip(chunk, 0, lines - 1)
            slot = whole.at[chunk]
            copy = self.copy(base + chunk, slot, slot, self.next_to(up))
            pl.when(cond)(copy.wait_recv)
            self.start(copy, jnp.logical_and(cond, more))
            if then is not None:
                then(chunk, slot, cond)


class PairFirst(Chain):
    def __init__(self, place, grad, scratch, whole, sends, recvs):
        super().__init__(place, sends, recvs)
        self.grad, self.whole = grad, whole.at[place.inner]
        self.pair_in, self.half, self.flow, self.total = scratch
        lines = place.lines
        steps = [self.pair_start, self.pair_end] + self.sum_steps(self.half, self.flow)
        steps.append(self.line_end)
        for r in range(1, lines):
            steps.append(functools.partial(self.spread_step, self.whole, 2 * lines, r, self.to_pair))
        steps.append(self.end)
        self.steps = steps

    def pair_start(self):
        place = self.place
        copy = self.copy(4 * place.lines, self.grad.at[1 - place.inner], self.pair_in, place.pair)
        self.first = copy
        self.start(copy)

    def pair_end(self):
        self.first.wait_recv()
        for z in range(self.place.lines):
            self.half[z] = (
                self.grad[self.place.inner, z].astype(F32) + self.pair_in[z].astype(F32)
            ).astype(BF16)

    def to_pair(self, chunk, slot, cond=None):
        self.start(self.copy(3 * self.place.lines + chunk, slot, slot, self.place.pair), cond)

    def line_end(self):
        z = self.place.outer
        self.sum_end(self.half, self.flow, self.total)
        self.whole[z] = self.total[...].astype(BF16)
        self.spread_start(self.whole, 2 * self.place.lines)
        self.to_pair(z, self.whole.at[z])

    def end(self):
        for z in range(self.place.lines):
            slot = self.whole.at[z]
            self.copy(3 * self.place.lines + z, slot, slot, self.place.pair).wait_recv()
        self.finish()


class LineFirst(Chain):
    def __init__(self, place, grad, scratch, whole, sends, recvs):
        super().__init__(place, sends, recvs)
        self.grad, self.whole = grad, whole
        self.flow, self.total, self.mine, self.pair_in = scratch
        lines = place.lines
        steps = self.sum_steps(self.grad, self.flow)
        steps += [self.pair_start, self.pair_end]
        for r in range(1, lines):
            steps.append(functools.partial(self.spread_step, self.whole, 2 * lines, r))
        steps.append(self.finish)
        self.steps = steps

    def pair_start(self):
        self.sum_end(self.grad, self.flow, self.total)
        self.mine[...] = self.total[...].astype(BF16)
        copy = self.copy(4 * self.place.lines, self.mine, self.pair_in, self.place.pair)
        self.first = copy
        self.start(copy)

    def pair_end(self):
        self.first.wait_recv()
        self.whole[self.place.outer] = (
            self.mine[...].astype(F32) + self.pair_in[...].astype(F32)
        ).astype(BF16)
        self.spread_start(self.whole, 2 * self.place.lines)


class SmallSum(Sender):
    def __init__(self, place, part, pair_in, line_in, out, sends, recvs):
        super().__init__(sends, recvs)
        self.place, self.part, self.pair_in, self.line_in, self.out = place, part, pair_in, line_in, out

    def start(self):
        self.first = self.go(0, self.part, self.pair_in, self.place.pair)

    def relay(self):
        place, lines = self.place, self.place.lines
        self.first.wait_recv()
        self.line_in[place.outer] = self.part[...] + self.pair_in[...]
        mine = self.line_in.at[place.outer]
        self.second = [self.go(k, mine, mine, place.peer(k)) for k in range(1, lines)]

    def total(self):
        for copy in self.second:
            copy.wait_recv()
        total = self.line_in[0]
        for z in range(1, self.place.lines):
            total = total + self.line_in[z]
        self.out[...] = total
        self.finish()


def dot(left, right):
    return jnp.dot(left, right, preferred_element_type=F32)


def dot_nt(left, right):
    return lax.dot_general(left, right, (((1,), (1,)), ((), ())), preferred_element_type=F32)


def dot_tn(left, right):
    return lax.dot_general(left, right, (((0,), (0,)), ((), ())), preferred_element_type=F32)


def row_mean(values):
    return jnp.mean(values, axis=-1, keepdims=True)


def col_sum(values):
    return jnp.sum(values, axis=0, keepdims=True)


ROWS = 272
CUTS = [(0, 64), (64, 64), (128, 64), (192, 80)]
PIXEL_CUTS = [(0, 208), (208, 208)]


KINDS = (
    ("down0", PairFirst),
    ("down1", PairFirst),
    ("up0", PairFirst),
    ("up1", LineFirst),
    ("attn0", PairFirst),
    ("attn1", PairFirst),
    ("table0", PairFirst),
)


def layer_kernel(
    lines,
    kinds,
    patches,
    kern,
    positions,
    rows_in,
    meta_col,
    live_row,
    live_col,
    select,
    w_qkv,
    w_out,
    w_up,
    b_up,
    w_down,
    cotangent,
    output,
    grad_patches,
    smalls,
    wholes,
    embeds,
    tokens,
    xhat_one,
    rstd_one,
    xhat_two,
    rstd_two,
    after,
    normed,
    normed_two,
    queries,
    keys,
    values,
    probs,
    mixed,
    grad_mixed,
    grad_qkv,
    branch_grad,
    gate_grad,
    activation,
    grad_pre,
    grad_after,
    after_low,
    grad_tokens,
    embed_grad,
    spread,
    part_a,
    part_b,
    part_c,
    part_d,
    part_e,
    slots_a,
    slots_b,
    slots_c,
    slots_d,
    slots_e,
    out_a,
    out_b,
    out_c,
    out_d,
    out_e,
    grads,
    slots,
    small_part,
    small_pair,
    small_line,
    mp_sends,
    mp_recvs,
    dp_sends,
    dp_recvs,
    etc_sends,
    etc_recvs,
):
    core, pair, far = mp_peers()
    place = DpPlace(lines)
    greet([pair, far, place.pair] + [place.peer(k) for k in range(1, lines)])
    me = lax.axis_index("mp")
    width = w_out.shape[0]
    heads = width // HEAD_DIM
    full = D

    def mp_sum(part, slots, out, cuts, number):
        return MpSum(
            part,
            [slots.at[k] for k in range(5)],
            out,
            cuts,
            mp_sends.at[number],
            mp_recvs.at[number],
        )

    sum_a = mp_sum(part_a, slots_a, out_a, CUTS, 0)
    sum_b = mp_sum(part_b, slots_b, out_b, CUTS, 1)
    sum_c = mp_sum(part_c, slots_c, out_c, CUTS, 2)
    sum_d = mp_sum(part_d, slots_d, out_d, CUTS, 3)
    sum_e = mp_sum(part_e, slots_e, out_e, PIXEL_CUTS, 4)

    pieces = []
    for number, (name, kind) in enumerate(kinds):
        pieces.append(
            kind(
                place,
                grads[number],
                slots[number],
                wholes[number],
                dp_sends.at[number],
                dp_recvs.at[number],
            )
        )
    small = SmallSum(place, small_part, small_pair, small_line, smalls, dp_sends.at[len(kinds)], dp_recvs.at[len(kinds)])

    def put_piece(grad, first_row, block):
        rows = grad.shape[-2]
        for k in range(0, block.shape[0], rows):
            chunk = (first_row + k) // rows
            spot = (chunk,) if len(grad.shape) == 3 else (chunk // lines, chunk % lines)
            grad[spot] = block[k : k + rows].astype(BF16)

    gain_one, shift_one = rows_in[0:1], rows_in[1:2]
    gain_two, shift_two = rows_in[2:3], rows_in[3:4]
    b_down = rows_in[4:5]
    lane_head = lax.broadcasted_iota(jnp.int32, (1, width), 1) // HEAD_DIM
    head_masks = [(lane_head == h).astype(F32).astype(BF16) for h in range(heads)]

    etc = Sender(etc_sends, etc_recvs)
    kept = {}

    def embed():
        embeds[me] = dot_tn(patches[...], kern[...]).astype(BF16)
        mine = embeds.at[me]
        kept["pair"] = etc.go(0, mine, mine, pair)
        kept["far"] = etc.go(1, mine, mine, far)

    def epass():
        kept["far"].wait_recv()
        got = embeds.at[lax.rem(me + 2, 4)]
        kept["passed"] = etc.go(2, got, got, pair)

    def fillgate():
        branch_grad[0:256] = (live_col[0:256] * cotangent[2:258]).astype(BF16)
        branch_grad[256:272] = jnp.concatenate(
            [cotangent[0:2], jnp.zeros((14, full), F32)], axis=0
        ).astype(BF16)
        small_part[...] = jnp.zeros_like(small_part)
        small_part[5:6] = col_sum(branch_grad[...].astype(F32))
        gate_grad[...] = dot_nt(branch_grad[...], w_down[...])

    def tokens_norm():
        kept["pair"].wait_recv()
        kept["passed"].wait_recv()
        for lo, n in CUTS:
            hi = min(lo + n, 256)
            for i in range(4):
                cols = slice(i * width, (i + 1) * width)
                tokens[lo:hi, cols] = embeds[i, lo:hi].astype(F32)
            tokens[lo:hi] += positions[lo:hi]
            if lo + n > 256:
                tokens[256:272] = jnp.concatenate([rows_in[5:7], jnp.zeros((14, full), F32)], axis=0)
            rows = slice(lo, lo + n)
            x = tokens[rows]
            centred = x - row_mean(x)
            rstd = lax.rsqrt(row_mean(centred * centred) + 1e-05)
            rstd_one[rows] = rstd
            xhat = centred * rstd
            xhat_one[rows] = xhat
            normed[rows] = (xhat * gain_one + shift_one).astype(BF16)

    def attention():
        queries[...] = dot_nt(normed[...], w_qkv[0]).astype(BF16)
        keys[...] = dot_nt(normed[...], w_qkv[1]).astype(BF16)
        values[...] = dot_nt(normed[...], w_qkv[2]).astype(BF16)
        live_keys = live_row[...] > 0
        total = None
        for h in range(heads):
            raw = dot_nt(queries[...] * head_masks[h], keys[...]) * 0.125
            raw = jnp.where(live_keys, raw, -1000000000.0)
            expo = jnp.exp(raw - jnp.max(raw, axis=-1, keepdims=True))
            prob = expo / jnp.sum(expo, axis=-1, keepdims=True)
            probs[h] = prob
            term = dot(prob.astype(BF16), values[...] * head_masks[h])
            total = term if total is None else total + term
        mixed[...] = total.astype(BF16)

    def put_part(part, rows, block):
        half = block.shape[1] // 2
        part[0, rows] = block[:, :half].astype(BF16)
        part[1, rows] = block[:, half:].astype(BF16)

    def get_out(out, rows):
        return jnp.concatenate([out[0, rows], out[1, rows]], axis=1)

    def span(i):
        lo, n = CUTS[i]
        return slice(lo, lo + n)

    def attn_part(i):
        put_part(part_a, span(i), dot(mixed[span(i)], w_out[...]))

    def feedforward(i):
        rows = span(i)
        x = tokens[rows] + get_out(out_a, rows)
        after[rows] = x
        centred = x - row_mean(x)
        rstd = lax.rsqrt(row_mean(centred * centred) + 1e-05)
        rstd_two[rows] = rstd
        xhat = centred * rstd
        xhat_two[rows] = xhat
        normed_two[rows] = (xhat * gain_two + shift_two).astype(BF16)
        gate = dot(normed_two[rows], w_up[...]) + b_up[...]
        cdf = 0.5 + 0.5 * lax.erf(gate * (2.0**-0.5))
        activation[rows] = (gate * cdf).astype(BF16)
        pdf = jnp.exp(-0.5 * gate * gate) * ((2.0 * math.pi) ** -0.5)
        grad_pre[rows] = (gate_grad[rows] * (cdf + gate * pdf)).astype(BF16)
        put_part(part_c, rows, dot_nt(grad_pre[rows], w_up[...]))

    half = full // 2

    def grad_of_down(j):
        cols = slice(j * half, (j + 1) * half)
        put_piece(pieces[j].grad, 0, dot_tn(activation[...], branch_grad[:, cols]))

    def grad_of_up(j):
        cols = slice(j * half, (j + 1) * half)
        put_piece(pieces[2 + j].grad, 0, dot_tn(normed_two[...], grad_pre[:, cols]))
        if j == 1:
            small_part[6:7] = col_sum(grad_pre[...].astype(F32))

    def norm_two_back(i):
        rows = span(i)
        lo, n = CUTS[i]
        dy = get_out(out_c, rows)
        xhat = xhat_two[rows]
        small_part[2:3] += col_sum(dy * xhat)
        small_part[3:4] += col_sum(dy)
        e = dy * gain_two
        dx = rstd_two[rows] * (e - row_mean(e) - xhat * row_mean(e * xhat))
        if lo + n <= 256:
            grad_out = live_col[rows] * cotangent[lo + 2 : lo + n + 2]
        else:
            grad_out = jnp.concatenate(
                [live_col[lo:256] * cotangent[lo + 2 : 258], cotangent[0:2], jnp.zeros((14, full), F32)],
                axis=0,
            )
        grad_x = dx + grad_out
        grad_after[rows] = grad_x
        after_low[rows] = grad_x.astype(BF16)

    def mixed_back():
        grad_mixed[...] = dot_nt(after_low[...], w_out[...]).astype(BF16)
        kept["parts"] = [None, None, None]

    def head_back(h):
        mixed_h = grad_mixed[...] * head_masks[h]
        grad_probs = dot_nt(mixed_h, values[...])
        prob = probs[h]
        scores = prob * (grad_probs - jnp.sum(grad_probs * prob, axis=-1, keepdims=True))
        scores = scores.astype(BF16)
        terms = [
            dot(scores, keys[...] * head_masks[h]),
            dot_tn(scores, queries[...] * head_masks[h]),
            dot_tn(prob.astype(BF16), mixed_h),
        ]
        kept["parts"] = [t if p is None else p + t for p, t in zip(kept["parts"], terms)]
        if h == heads - 1:
            for t, scale in enumerate((0.125, 0.125, 1.0)):
                grad_qkv[t] = (kept["parts"][t] * scale).astype(BF16)

    def norm_part(i):
        rows = span(i)
        block = dot(grad_qkv[0, rows], w_qkv[0])
        block = block + dot(grad_qkv[1, rows], w_qkv[1])
        put_part(part_d, rows, block + dot(grad_qkv[2, rows], w_qkv[2]))

    def grad_of_attn(j):
        cols = slice(j * half, (j + 1) * half)
        grad = pieces[4 + j].grad
        put_piece(grad, 0, dot_tn(mixed[...], after_low[:, cols]))
        for t in range(3):
            put_piece(grad, (t + 1) * width, dot_tn(grad_qkv[t], normed[:, cols]))

    wide = NB * PIX

    def selection():
        band = lax.broadcasted_iota(jnp.int32, (BANDS * PIX, 16), 0) // PIX
        slot = lax.broadcasted_iota(jnp.int32, (BANDS * PIX, 16), 1)
        row_select = dot((band == slot).astype(F32).astype(BF16), select[...]).astype(BF16)
        table_band = lax.broadcasted_iota(jnp.int32, (NB, wide), 0)
        table_lane = lax.broadcasted_iota(jnp.int32, (NB, wide), 1) // PIX
        widen = (table_band == table_lane).astype(F32).astype(BF16)
        for b in range(BANDS):
            rows = slice(b * PIX, (b + 1) * PIX)
            spot = lax.broadcasted_iota(jnp.int32, (PIX, wide), 0)
            lane = lax.rem(lax.broadcasted_iota(jnp.int32, (PIX, wide), 1), PIX)
            block = dot(row_select[rows], widen)
            spread[rows] = jnp.where(spot == lane, block, 0.0).astype(BF16)

    def norm_one_back(i):
        rows = span(i)
        dy = get_out(out_d, rows)
        xhat = xhat_one[rows]
        small_part[0:1] += col_sum(dy * xhat)
        small_part[1:2] += col_sum(dy)
        e = dy * gain_one
        dx = rstd_one[rows] * (e - row_mean(e) - xhat * row_mean(e * xhat))
        grad_tokens[rows] = grad_after[rows] + dx

    def table_grad():
        for i in range(4):

            @pl.when(me == i)
            def _():
                embed_grad[...] = grad_tokens[0:256, i * width : (i + 1) * width].astype(BF16)

        grad_kern = dot(patches[...], embed_grad[...]).astype(BF16)
        table = dot_tn(grad_kern, spread[...])
        put_piece(pieces[6].grad, 0, table[:, : wide // 2])
        put_piece(pieces[6].grad, width, table[:, wide // 2 :])

    def small_ready():
        small_part[4:5] = grad_tokens[256:257]
        small_part[8:16] = meta_col[...] * grad_tokens[257:258]

    def pixel_part():
        pixels = dot_nt(kern[...], embed_grad[...]).astype(BF16)
        part_e[0] = pixels[: BANDS * PIX // 2]
        part_e[1] = pixels[BANDS * PIX // 2 :]

    def branch_part():
        for i in range(len(CUTS)):
            put_part(part_b, span(i), dot(activation[span(i)], w_down[...]))

    def final_output():
        for i, (lo, n) in enumerate(CUTS):
            rows = span(i)
            x = after[rows] + get_out(out_b, rows) + b_down
            if lo + n <= 256:
                output[lo + 2 : lo + n + 2] = live_col[rows] * x
            else:
                output[lo + 2 : 258] = live_col[lo:256] * x[: 256 - lo]
                output[0:2] = x[256 - lo : 258 - lo]

    def final_pixels():
        grad_patches[: BANDS * PIX // 2] = out_e[0]
        grad_patches[BANDS * PIX // 2 :] = out_e[1]

    down0, down1, up0, up1, attn0, attn1, table0 = pieces
    order = [
        embed,
        fillgate,
        selection,
        epass,
        tokens_norm,
        attention,
        (attn_part, 0),
        (sum_a.start, 0),
        (attn_part, 1),
        (sum_a.start, 1),
        (attn_part, 2),
        (sum_a.start, 2),
        (attn_part, 3),
        (sum_a.start, 3),
        (sum_a.relay, 0),
        (sum_a.relay, 1),
        (sum_a.relay, 2),
        (sum_a.relay, 3),
        (sum_a.forward, 0),
        (sum_a.forward, 1),
        (sum_a.total, 0),
        (feedforward, 0),
        (sum_a.total, 1),
        (sum_a.forward, 2),
        (sum_c.start, 0),
        (feedforward, 1),
        (sum_a.forward, 3),
        (sum_a.total, 2),
        (sum_c.relay, 0),
        (sum_c.start, 1),
        (feedforward, 2),
        (sum_a.total, 3),
        (sum_c.start, 2),
        (feedforward, 3),
        (sum_c.relay, 1),
        (sum_c.relay, 2),
        (sum_c.forward, 0),
        (sum_c.start, 3),
        (grad_of_down, 0),
        (grad_of_down, 1),
        down0.step,
        (sum_c.total, 0),
        down1.step,
        (sum_c.relay, 3),
        (grad_of_up, 0),
        up0.step,
        (sum_c.forward, 1),
        (grad_of_up, 1),
        up1.step,
        (sum_c.forward, 2),
        (norm_two_back, 0),
        (sum_c.total, 1),
        (norm_two_back, 1),
        (sum_c.total, 2),
        (sum_c.forward, 3),
        (norm_two_back, 2),
        branch_part,
        (sum_c.total, 3),
        (norm_two_back, 3),
        mixed_back,
        (head_back, 0),
        down0.step,
        down0.step,
        up1.step,
        (head_back, 1),
        (head_back, 2),
        (norm_part, 0),
        (sum_d.start, 0),
        (norm_part, 1),
        (sum_d.start, 1),
        (norm_part, 2),
        (sum_d.start, 2),
        (norm_part, 3),
        (sum_d.start, 3),
        (grad_of_attn, 0),
        (sum_d.relay, 0),
        (sum_d.relay, 1),
        (sum_d.relay, 2),
        down1.step,
        (sum_d.relay, 3),
        down0.step,
        down1.step,
        up1.step,
        up1.step,
        attn0.step,
        (grad_of_attn, 1),
        attn1.step,
        (sum_b.start, 0),
        (sum_b.start, 1),
        (sum_b.start, 2),
        (sum_b.start, 3),
        (sum_d.forward, 0),
        (sum_b.relay, 0),
        (sum_b.relay, 1),
        (sum_b.relay, 2),
        (sum_d.forward, 1),
        down0.step,
        down0.step,
        (sum_b.relay, 3),
        (sum_d.total, 0),
        (norm_one_back, 0),
        (sum_d.forward, 2),
        down1.step,
        (sum_d.total, 1),
        (norm_one_back, 1),
        (sum_d.forward, 3),
        up0.step,
        (sum_d.total, 2),
        up0.step,
        (norm_one_back, 2),
        up1.step,
        (sum_d.total, 3),
        (norm_one_back, 3),
        table_grad,
        down0.step,
        table0.step,
        down1.step,
        down1.step,
        up0.step,
        small_ready,
        small.start,
        pixel_part,
        (sum_e.start, 0),
        (sum_e.start, 1),
        (sum_b.forward, 0),
        (sum_b.forward, 1),
        (sum_b.forward, 2),
        (sum_b.forward, 3),
        attn0.step,
        attn0.step,
        (sum_e.relay, 0),
        (sum_e.relay, 1),
        (sum_b.total, 0),
        (sum_b.total, 1),
        (sum_b.total, 2),
        (sum_b.total, 3),
        final_output,
        down0.step,
        down1.step,
        attn0.step,
        up0.step,
        up0.step,
        (sum_e.forward, 0),
        attn1.step,
        down0.step,
        attn1.step,
        (sum_e.total, 0),
        (sum_e.forward, 1),
        (sum_e.total, 1),
        down1.step,
        final_pixels,
        up1.step,
        attn0.step,
        attn0.step,
        attn1.step,
        down0.step,
        up0.step,
        down1.step,
        up1.step,
        attn0.step,
        attn1.step,
        attn1.step,
        table0.step,
        table0.step,
        small.relay,
        down1.step,
        up0.step,
        up1.step,
        table0.step,
        attn0.step,
        attn1.step,
        down0.step,
        small.total,
        up0.step,
        table0.step,
        table0.step,
        down1.step,
        up1.step,
        up1.step,
        attn0.step,
        attn1.step,
        up0.step,
        table0.step,
        attn0.step,
        attn1.step,
        up0.step,
        table0.step,
        attn1.step,
        attn0.step,
        table0.step,
        attn1.step,
        table0.step,
        table0.step,
    ]
    for item in order:
        if isinstance(item, tuple):
            item[0](*item[1:])
        else:
            item()
    while any(piece.steps for piece in pieces):
        for piece in pieces:
            piece.step()
    for one in (sum_a, sum_b, sum_c, sum_d, sum_e, etc):
        one.finish()


def layer(dp_count, width, operands):
    lines = dp_count // 2

    def piece(rows, lanes, parts):
        chunk = -(-rows // parts)
        chunk = -(-chunk // 16) * 16
        if parts == lines:
            return (lines, chunk, lanes)
        return (2, lines, chunk, lanes)

    pieces = []
    for name, kind in KINDS:
        parts = dp_count if kind is PairFirst else lines
        if name == "table0":
            pieces.append(piece(2 * width, NB * PIX // 2, parts))
        else:
            pieces.append(piece(4 * width, D // 2, parts))

    def piece_scratch(shape):
        if len(shape) == 4:
            return [low(*shape[1:]), low(*shape[1:]), low(2, *shape[1:]), vmem(*shape[2:])]
        return [low(2, *shape), vmem(*shape[1:]), low(*shape[1:]), low(*shape[1:])]

    half = D // 2
    pixel_lanes = BANDS * PIX

    def vmem(*shape, dtype=F32):
        return pltpu.VMEM(shape, dtype)

    def low(*shape):
        return pltpu.VMEM(shape, BF16)

    scratch = [
        low(4, 256, width),
        vmem(ROWS, D),
        vmem(ROWS, D),
        vmem(ROWS, 1),
        vmem(ROWS, D),
        vmem(ROWS, 1),
        vmem(ROWS, D),
        low(ROWS, D),
        low(ROWS, D),
        low(ROWS, width),
        low(ROWS, width),
        low(ROWS, width),
        vmem(width // HEAD_DIM, ROWS, ROWS),
        low(ROWS, width),
        low(ROWS, width),
        low(3, ROWS, width),
        low(ROWS, D),
        vmem(ROWS, D),
        low(ROWS, D),
        low(ROWS, D),
        vmem(ROWS, D),
        low(ROWS, D),
        vmem(ROWS, D),
        low(256, width),
        low(pixel_lanes, NB * PIX),
    ]
    scratch += [low(2, ROWS, half)] * 4 + [low(2, pixel_lanes // 2, 256)]
    scratch += [low(5, ROWS, half)] * 4 + [low(5, pixel_lanes // 2, 256)]
    scratch += [vmem(2, ROWS, half)] * 4 + [vmem(2, pixel_lanes // 2, 256)]
    scratch.append([low(*shape) for shape in pieces])
    scratch.append([piece_scratch(shape) for shape in pieces])
    scratch += [vmem(16, D), vmem(16, D), vmem(lines, 16, D)]
    dma = pltpu.SemaphoreType.DMA
    scratch += [dma((5, 16)), dma((5, 16)), dma((len(pieces) + 1, 4 * lines + 1)), dma((len(pieces) + 1, 4 * lines + 1)), dma((3,)), dma((3,))]
    ref = pl.BlockSpec(memory_space=pltpu.VMEM)
    shapes = [
        jax.ShapeDtypeStruct((SEQ, D), F32),
        jax.ShapeDtypeStruct((pixel_lanes, 256), F32),
        jax.ShapeDtypeStruct((16, D), F32),
        [jax.ShapeDtypeStruct(shape, BF16) for shape in pieces],
    ]
    output, grad_patches, smalls, wholes = pl.pallas_call(
        functools.partial(layer_kernel, lines, KINDS),
        out_shape=shapes,
        in_specs=[ref] * len(operands),
        out_specs=[ref] * 3 + [[ref] * len(pieces)],
        scratch_shapes=scratch,
        compiler_params=pltpu.CompilerParams(
            collective_id=0, has_side_effects=True, vmem_limit_bytes=62 * 1024 * 1024
        ),
        name="layer",
    )(*operands)
    wholes = {name: out.reshape(-1, out.shape[-1]) for (name, kind), out in zip(KINDS, wholes)}
    return output, grad_patches, smalls, wholes


def small_sum_kernel(axis, count, part, out, slots, sends, recvs):
    me = lax.axis_index(axis)
    peers = [{axis: lax.rem(me + k, count)} for k in range(1, count)]
    greet(peers)
    copies = []
    for k, peer in enumerate(peers):
        copy = remote(part, slots.at[me], sends.at[k], recvs.at[k], peer)
        copy.start()
        copies.append(copy)
    slots[me] = part[...]
    for copy in copies:
        copy.wait()
    total = slots[0]
    for k in range(1, count):
        total = total + slots[k]
    out[...] = total


def small_sum(part, axis, count, number):
    vmem = pl.BlockSpec(memory_space=pltpu.VMEM)
    return pl.pallas_call(
        functools.partial(small_sum_kernel, axis, count),
        out_shape=jax.ShapeDtypeStruct(part.shape, F32),
        in_specs=[vmem],
        out_specs=vmem,
        scratch_shapes=[
            pltpu.VMEM((count,) + part.shape, F32),
            pltpu.SemaphoreType.DMA((count - 1,)),
            pltpu.SemaphoreType.DMA((count - 1,)),
        ],
        compiler_params=pltpu.CompilerParams(collective_id=number, has_side_effects=True),
        name="small_sum_" + axis,
    )(part)


def local(
    dp_count,
    patches,
    wavelengths,
    band_ids,
    band_mask,
    sensor,
    lengths,
    visible,
    meta,
    w_hyper,
    b_hyper,
    w_gen,
    cls_token,
    w_meta,
    gain_one,
    shift_one,
    w_qkv,
    w_out,
    gain_two,
    shift_two,
    w_up,
    b_up,
    w_down,
    b_down,
    cotangent,
):
    highest = lax.Precision.HIGHEST
    width = w_gen.shape[0]
    features = sinus_waves(wavelengths, HYP)
    positions = grid_codes(visible, lengths, D, VIS_MAX)[0]
    hyper_pre = jnp.dot(features, w_hyper, precision=highest) + b_hyper
    hidden, hyper_pull = jax.vjp(gelu_exact, hyper_pre)
    hidden_low = hidden.astype(BF16)
    ids, mask = band_ids[sensor[0]], band_mask[sensor[0]]
    select = (ids[:, None] == jnp.arange(NB)[None, :]).astype(F32) * mask[:, None].astype(F32)
    chosen = jnp.dot(select.astype(BF16), hidden_low, preferred_element_type=F32).astype(BF16)
    kern = jnp.einsum("bh,dph->bpd", chosen, w_gen, preferred_element_type=F32).astype(BF16)
    kern = kern.reshape(BANDS * PIX, width)
    place = jnp.arange(ROWS)
    live = ((place < lengths[0]) | ((place >= 256) & (place < SEQ))).astype(F32)
    meta_row = jnp.dot(meta, w_meta, precision=highest)[0]
    rows_in = jnp.stack([gain_one, shift_one, gain_two, shift_two, b_down, cls_token, meta_row, meta_row])
    operands = (
        patches[0].T,
        kern,
        positions,
        rows_in,
        meta.reshape(-1, 1),
        live[None, :],
        live[:, None],
        jnp.pad(select.astype(BF16), ((0, 16 - BANDS), (0, 0))),
        w_qkv,
        w_out,
        w_up,
        b_up[None, :],
        w_down,
        cotangent[0],
    )
    output, grad_patches, smalls, wholes = layer(dp_count, width, operands)

    def joined(name):
        halves = [wholes[f"{name}{j}"][: 4 * width] for j in range(2)]
        return jnp.concatenate(halves, axis=1).astype(F32)

    grad_w_down, grad_w_up, attn = joined("down"), joined("up"), joined("attn")
    table = wholes["table0"][: 2 * width].reshape(2, width, NB // 2, PIX)
    low_halves = hidden_low.reshape(2, NB // 2, HYP)
    grad_w_gen = jnp.einsum("anh,adnp->dph", low_halves, table, preferred_element_type=F32)
    hidden_part = jnp.einsum("adnp,dph->anh", table, w_gen, preferred_element_type=F32)
    grad_hidden = small_sum(hidden_part.reshape(NB, HYP), "mp", 4, 1)
    grad_inner = hyper_pull(grad_hidden)[0]
    grad_w_hyper = jnp.dot(features.T, grad_inner, precision=highest)
    grad_b_hyper = jnp.sum(grad_inner, axis=0)
    return (
        output[None],
        grad_patches.T[None],
        grad_w_hyper,
        grad_b_hyper,
        grad_w_gen,
        smalls[4],
        smalls[8:16],
        smalls[0],
        smalls[1],
        attn[width : 4 * width].reshape(3, width, D),
        attn[:width],
        smalls[2],
        smalls[3],
        grad_w_up,
        smalls[6],
        grad_w_down,
        smalls[5],
    )


def solution(mesh):
    return jax.shard_map(
        functools.partial(local, mesh.shape["dp"]),
        mesh=mesh,
        in_specs=(
            P("dp", None, None),
            P(),
            P(),
            P(),
            P("dp"),
            P("dp"),
            P("dp", None),
            P("dp", None),
            P(),
            P(),
            P("mp", None, None),
            P(),
            P(),
            P(),
            P(),
            P(None, "mp", None),
            P("mp", None),
            P(),
            P(),
            P(None, "mp"),
            P("mp"),
            P("mp", None),
            P(),
            P("dp", None, None),
        ),
        out_specs=(
            P("dp", None, None),
            P("dp", None, None),
            P(),
            P(),
            P("mp", None, None),
            P(),
            P(),
            P(),
            P(),
            P(None, "mp", None),
            P("mp", None),
            P(),
            P(),
            P(None, "mp"),
            P("mp"),
            P("mp", None),
            P(),
        ),
        check_vma=False,
    )
```

```python
import functools
import math

import jax
import jax.numpy as jnp
from jax import lax
from jax.experimental import pallas as pl
from jax.experimental.pallas import tpu as pltpu
from jax.sharding import PartitionSpec as P

F32 = jnp.float32
BF16 = jnp.bfloat16
MESH = pl.DeviceIdType.MESH

D = 768
HEAD_DIM = 64
PIX = 64
HYP = 128
BANDS = 13
NB = 32
SENSORS = 4
VIS_MAX = 256
SEQ = 258


def sinus_waves(wavelengths, width):
    half_width = width // 2
    steps = jnp.arange(half_width, dtype=jnp.float32)
    freqs = jnp.exp(steps * (6.0 * math.log(2.0) / half_width))
    angles = wavelengths[:, None] * freqs[None, :]
    return jnp.concatenate([jnp.sin(angles), jnp.cos(angles)], axis=1)


def grid_codes(visible, lengths, width, most):
    short_side = math.isqrt(most)
    long_side = 2 * short_side
    sides = jnp.where(lengths == most, long_side, short_side).astype(jnp.int32)[:, None]
    grid_rows = (visible // sides).astype(jnp.float32)
    grid_cols = (visible % sides).astype(jnp.float32)
    quarter = width // 4
    omegas = jnp.exp(jnp.arange(quarter, dtype=jnp.float32) * (-math.log(10000.0) / quarter))
    row_angle = grid_rows[..., None] * omegas
    col_angle = grid_cols[..., None] * omegas
    return jnp.concatenate(
        [jnp.sin(row_angle), jnp.cos(row_angle), jnp.sin(col_angle), jnp.cos(col_angle)], axis=-1
    )


def gelu_exact(values):
    return jax.nn.gelu(values, approximate=False)


def remote(src, dst, send_sem, recv_sem, device):
    return pltpu.make_async_remote_copy(
        src_ref=src,
        dst_ref=dst,
        send_sem=send_sem,
        recv_sem=recv_sem,
        device_id=device,
        device_id_type=MESH,
    )


def greet(devices):
    barrier = pltpu.get_barrier_semaphore()
    for device in devices:
        pl.semaphore_signal(barrier, inc=1, device_id=device, device_id_type=MESH)
    pl.semaphore_wait(barrier, len(devices))


def mp_peers():
    place = lax.axis_index("mp")
    core = lax.rem(place, 2)
    return core, {"mp": place + 1 - 2 * core}, {"mp": lax.rem(place + 2, 4)}


class Sender:
    def __init__(self, sends, recvs):
        self.sends, self.recvs, self.copies = sends, recvs, []

    def go(self, number, src, dst, device):
        copy = remote(src, dst, self.sends.at[number], self.recvs.at[number], device)
        copy.start()
        self.copies.append(copy)
        return copy

    def finish(self):
        for copy in self.copies:
            copy.wait_send()


class MpSum(Sender):
    def __init__(self, part, slots, out, cuts, sends, recvs):
        super().__init__(sends, recvs)
        self.part, self.out, self.cuts = part, out, cuts
        self.pair_in, self.chip_sum, self.far_in, self.other_near, self.other_far = slots
        self.core, self.pair, self.far = mp_peers()
        self.first, self.second, self.third = {}, {}, {}

    def number(self, step, i):
        return step * len(self.cuts) + i

    def start(self, i):
        rows = pl.ds(*self.cuts[i])
        self.first[i] = self.go(
            self.number(0, i), self.part.at[1 - self.core, rows], self.pair_in.at[rows], self.pair
        )

    def relay(self, i):
        rows = pl.ds(*self.cuts[i])
        self.first[i].wait_recv()
        self.chip_sum[rows] = (
            self.part[self.core, rows].astype(F32) + self.pair_in[rows].astype(F32)
        ).astype(BF16)
        mine = self.chip_sum.at[rows]
        self.second[i] = (
            self.go(self.number(1, i), mine, self.far_in.at[rows], self.far),
            self.go(self.number(2, i), mine, self.other_near.at[rows], self.pair),
        )

    def forward(self, i):
        rows = pl.ds(*self.cuts[i])
        self.second[i][0].wait_recv()
        self.third[i] = self.go(
            self.number(3, i), self.far_in.at[rows], self.other_far.at[rows], self.pair
        )
        self.out[self.core, rows] = self.chip_sum[rows].astype(F32) + self.far_in[rows].astype(F32)

    def total(self, i):
        rows = pl.ds(*self.cuts[i])
        self.second[i][1].wait_recv()
        self.third[i].wait_recv()
        self.out[1 - self.core, rows] = self.other_near[rows].astype(F32) + self.other_far[
            rows
        ].astype(F32)


class DpPlace:
    def __init__(self, lines):
        place = lax.axis_index("dp")
        self.lines = lines
        self.inner = lax.rem(place, 2)
        self.outer = place // 2
        self.pair = {"dp": self.outer * 2 + 1 - self.inner}

    def peer(self, k):
        return {"dp": lax.rem(self.outer + k, self.lines) * 2 + self.inner}


class Chain:
    def __init__(self, place, sends, recvs):
        self.place, self.sends, self.recvs = place, sends, recvs
        self.ends = []
        self.low = place.outer < (place.lines + 1) // 2
        self.depth = jnp.where(self.low, place.outer, place.lines - 1 - place.outer)

    def copy(self, number, src, dst, device):
        return remote(src, dst, self.sends.at[number], self.recvs.at[number], device)

    def start(self, copy, cond=None):
        if cond is None:
            copy.start()
        else:
            pl.when(cond)(copy.start)
        self.ends.append((copy, cond))

    def next_to(self, up):
        place = self.place
        outer = jnp.where(up, place.outer + 1, place.outer - 1)
        outer = jnp.clip(outer, 0, place.lines - 1)
        return {"dp": outer * 2 + place.inner}

    def step(self):
        if self.steps:
            self.steps.pop(0)()

    def drain(self):
        while self.steps:
            self.step()

    def finish(self):
        for copy, cond in self.ends:
            if cond is None:
                copy.wait_send()
            else:
                pl.when(cond)(copy.wait_send)

    def hop(self, flow, i, outward):
        lines = self.place.lines
        up = self.low if outward else jnp.logical_not(self.low)
        way = jnp.where(up, 0, 1)
        chunk = jnp.where(up, lines - 1 - i, i)
        slot = flow.at[way, chunk]
        return slot, chunk, self.copy(way * lines + chunk, slot, slot, self.next_to(up))

    def out(self, own, flow):
        for i in range(self.place.lines - 1):
            slot, chunk, copy = self.hop(flow, i, True)

            @pl.when(self.depth == 0)
            def _(slot=slot, chunk=chunk):
                slot[...] = own[chunk]

            self.start(copy, self.depth == 0)

    def on(self, own, flow, i, outward):
        slot, chunk, copy = self.hop(flow, i, outward)
        inner = i < self.place.lines - 1 - self.depth if outward else i < self.depth
        active = jnp.logical_and(self.depth > 0, inner)

        @pl.when(active)
        def _():
            copy.wait_recv()
            slot[...] = (slot[...].astype(F32) + own[chunk].astype(F32)).astype(BF16)

        self.start(copy, active)

    def sum_steps(self, own, flow):
        lines = self.place.lines
        steps = [functools.partial(self.out, own, flow)]
        for i in range(lines - 2):
            steps.append(functools.partial(self.on, own, flow, i, True))
            if i < (lines + 1) // 2 - 1:
                steps.append(functools.partial(self.on, own, flow, i, False))
        return steps

    def sum_end(self, own, flow, total):
        lines, z = self.place.lines, self.place.outer
        total[...] = own[z].astype(F32)
        for way, cond in ((0, z > 0), (1, z < lines - 1)):
            slot = flow.at[way, z]
            copy = self.copy(way * lines + z, slot, slot, self.next_to(z > 0))

            @pl.when(cond)
            def _(slot=slot, copy=copy):
                copy.wait_recv()
                total[...] += slot[...].astype(F32)

    def spread_start(self, whole, base):
        lines, z = self.place.lines, self.place.outer
        mine = whole.at[z]
        self.start(self.copy(base + z, mine, mine, self.next_to(True)), z < lines - 1)
        self.start(self.copy(base + z, mine, mine, self.next_to(False)), z > 0)

    def spread_step(self, whole, base, r, then=None):
        lines, z = self.place.lines, self.place.outer
        for up, chunk, cond, more in (
            (True, z - r, z - r >= 0, z < lines - 1),
            (False, z + r, z + r < lines, z > 0),
        ):
            chunk = jnp.clip(chunk, 0, lines - 1)
            slot = whole.at[chunk]
            copy = self.copy(base + chunk, slot, slot, self.next_to(up))
            pl.when(cond)(copy.wait_recv)
            self.start(copy, jnp.logical_and(cond, more))
            if then is not None:
                then(chunk, slot, cond)


class PairFirst(Chain):
    def __init__(self, place, grad, scratch, whole, sends, recvs):
        super().__init__(place, sends, recvs)
        self.grad, self.whole = grad, whole.at[place.inner]
        self.pair_in, self.half, self.flow, self.total = scratch
        lines = place.lines
        steps = [self.pair_start, self.pair_end] + self.sum_steps(self.half, self.flow)
        steps.append(self.line_end)
        for r in range(1, lines):
            steps.append(functools.partial(self.spread_step, self.whole, 2 * lines, r, self.to_pair))
        steps.append(self.end)
        self.steps = steps

    def pair_start(self):
        place = self.place
        copy = self.copy(4 * place.lines, self.grad.at[1 - place.inner], self.pair_in, place.pair)
        self.first = copy
        self.start(copy)

    def pair_end(self):
        self.first.wait_recv()
        for z in range(self.place.lines):
            self.half[z] = (
                self.grad[self.place.inner, z].astype(F32) + self.pair_in[z].astype(F32)
            ).astype(BF16)

    def to_pair(self, chunk, slot, cond=None):
        self.start(self.copy(3 * self.place.lines + chunk, slot, slot, self.place.pair), cond)

    def line_end(self):
        z = self.place.outer
        self.sum_end(self.half, self.flow, self.total)
        self.whole[z] = self.total[...].astype(BF16)
        self.spread_start(self.whole, 2 * self.place.lines)
        self.to_pair(z, self.whole.at[z])

    def end(self):
        for z in range(self.place.lines):
            slot = self.whole.at[z]
            self.copy(3 * self.place.lines + z, slot, slot, self.place.pair).wait_recv()
        self.finish()


class LineFirst(Chain):
    def __init__(self, place, grad, scratch, whole, sends, recvs):
        super().__init__(place, sends, recvs)
        self.grad, self.whole = grad, whole
        self.flow, self.total, self.mine, self.pair_in = scratch
        lines = place.lines
        steps = self.sum_steps(self.grad, self.flow)
        steps += [self.pair_start, self.pair_end]
        for r in range(1, lines):
            steps.append(functools.partial(self.spread_step, self.whole, 2 * lines, r))
        steps.append(self.finish)
        self.steps = steps

    def pair_start(self):
        self.sum_end(self.grad, self.flow, self.total)
        self.mine[...] = self.total[...].astype(BF16)
        copy = self.copy(4 * self.place.lines, self.mine, self.pair_in, self.place.pair)
        self.first = copy
        self.start(copy)

    def pair_end(self):
        self.first.wait_recv()
        self.whole[self.place.outer] = (
            self.mine[...].astype(F32) + self.pair_in[...].astype(F32)
        ).astype(BF16)
        self.spread_start(self.whole, 2 * self.place.lines)


class LineGather(Chain):
    def __init__(self, place, bank, sends, recvs, share=None):
        super().__init__(place, sends, recvs)
        self.bank, self.share = bank, share
        lines = place.lines
        self.mine = bank.at[place.inner]
        steps = [self.begin]
        for r in range(1, lines):
            steps.append(functools.partial(self.spread_step, self.mine, 0, r, self.hand_on))
        self.steps = steps + [self.from_pair, self.end]

    def hand_on(self, chunk, slot, cond=None):
        lines = self.place.lines
        self.start(self.copy(lines + chunk, slot, slot, self.place.pair), cond)
        self.to_core(self.place.inner * lines + chunk, slot, cond)

    def to_core(self, number, slot, cond=None):
        if self.share is not None:
            device, sends, recvs = self.share[:3]
            self.start(remote(slot, slot, sends.at[number], recvs.at[number], device), cond)

    def begin(self):
        z = self.place.outer
        self.spread_start(self.mine, 0)
        self.hand_on(z, self.mine.at[z])

    def from_pair(self):
        lines, other = self.place.lines, 1 - self.place.inner
        for z in range(lines):
            slot = self.bank.at[other, z]
            self.copy(lines + z, slot, slot, self.place.pair).wait_recv()
            self.to_core(other * lines + z, slot)

    def end(self):
        if self.share is not None:
            device, sends, recvs, there = self.share
            for i in range(2):
                for z in range(self.place.lines):
                    number, slot = i * self.place.lines + z, there.at[i, z]
                    remote(slot, slot, sends.at[number], recvs.at[number], device).wait_recv()
        self.finish()


class SmallSum(Sender):
    def __init__(self, place, part, pair_in, line_in, out, sends, recvs):
        super().__init__(sends, recvs)
        self.place, self.part, self.pair_in, self.line_in, self.out = place, part, pair_in, line_in, out

    def start(self):
        self.first = self.go(0, self.part, self.pair_in, self.place.pair)

    def relay(self):
        place, lines = self.place, self.place.lines
        self.first.wait_recv()
        self.line_in[place.outer] = self.part[...] + self.pair_in[...]
        mine = self.line_in.at[place.outer]
        self.second = [self.go(k, mine, mine, place.peer(k)) for k in range(1, lines)]

    def total(self):
        for copy in self.second:
            copy.wait_recv()
        total = self.line_in[0]
        for z in range(1, self.place.lines):
            total = total + self.line_in[z]
        self.out[...] = total
        self.finish()


class MpSmall(Sender):
    def __init__(self, part, slots, out, sends, recvs):
        super().__init__(sends, recvs)
        self.part, self.slots, self.out = part, slots, out
        core, pair, far = mp_peers()
        self.peers = [pair, far, {"mp": far["mp"] + 1 - 2 * core}]

    def begin(self):
        me = lax.axis_index("mp")
        self.slots[me] = self.part[...]
        for k, peer in enumerate(self.peers):
            self.go(k, self.part, self.slots.at[me], peer)

    def total(self):
        for copy in self.copies:
            copy.wait_recv()
        total = self.slots[0]
        for k in range(1, 4):
            total = total + self.slots[k]
        self.out[...] = total


def dot(left, right):
    return jnp.dot(left, right, preferred_element_type=F32)


def dot_nt(left, right):
    return lax.dot_general(left, right, (((1,), (1,)), ((), ())), preferred_element_type=F32)


def dot_tn(left, right):
    return lax.dot_general(left, right, (((0,), (0,)), ((), ())), preferred_element_type=F32)


def row_mean(values):
    return jnp.mean(values, axis=-1, keepdims=True)


def col_sum(values):
    return jnp.sum(values, axis=0, keepdims=True)


ROWS = 272
CUTS = [(0, 64), (64, 64), (128, 64), (192, 80)]
GROUP = 8
SLOTS = 16
PIXEL_CUTS = [(0, 208), (208, 208)]


KINDS = (
    ("down0", LineFirst),
    ("down1", PairFirst),
    ("up0", PairFirst),
    ("up1", LineFirst),
    ("attn0", PairFirst),
    ("attn1", PairFirst),
)


def layer_kernel(
    lines,
    kinds,
    far_patches,
    hidden,
    far_w_table,
    far_positions,
    rows_in,
    meta_col,
    live_row,
    live_col,
    select,
    far_w_qkv,
    far_w_out,
    far_w_up,
    b_up,
    far_w_down,
    far_cotangent,
    far_output,
    far_grad_patches,
    smalls,
    hidden_grad,
    grad_gen,
    far_wholes,
    embeds,
    tokens,
    xhat_one,
    rstd_one,
    xhat_two,
    rstd_two,
    after,
    normed,
    normed_two,
    queries,
    keys,
    values,
    probs,
    mixed,
    grad_mixed,
    grad_qkv,
    branch_grad,
    gate_grad,
    activation,
    grad_pre,
    after_low,
    bank,
    embed_bank,
    spots,
    kern,
    picks,
    kern_grads,
    table,
    gen_out,
    hidden_part,
    hidden_slots,
    part_a,
    part_b,
    part_c,
    part_d,
    part_e,
    slots_a,
    slots_b,
    slots_c,
    slots_d,
    slots_e,
    out_a,
    out_b,
    out_c,
    out_d,
    out_e,
    grads,
    slots,
    small_part,
    small_pair,
    small_line,
    mp_sends,
    mp_recvs,
    dp_sends,
    dp_recvs,
    etc_sends,
    etc_recvs,
    share_sends,
    share_recvs,
    out_sem,
    patches,
    w_table,
    positions,
    w_qkv,
    w_out,
    w_up,
    w_down,
    cotangent,
    output,
    grad_patches,
    wholes,
    in_sems,
    end_sems,
):
    core, pair, far = mp_peers()
    place = DpPlace(lines)
    loads = {}
    for number, (src, dst) in enumerate(
        (
            (far_w_table, w_table),
            (far_patches, patches),
            (far_cotangent, cotangent),
            (far_w_down, w_down),
            (far_positions, positions),
            (far_w_qkv, w_qkv),
            (far_w_out, w_out),
            (far_w_up, w_up),
        )
    ):
        loads[number] = pltpu.make_async_copy(src, dst, in_sems.at[number])
        loads[number].start()

    def need(number):
        if number in loads:
            loads.pop(number).wait()

    stores = []

    def keep(src, dst):
        stores.append(pltpu.make_async_copy(src, dst, end_sems.at[len(stores)]))
        stores[-1].start()

    cross = {"mp": far["mp"] + 1 - 2 * core}
    greet([pair, far, cross, place.pair] + [place.peer(k) for k in range(1, lines)])
    me = lax.axis_index("mp")
    width = w_out.shape[0]
    heads = width // HEAD_DIM
    full = D

    def mp_sum(part, slots, out, cuts, number):
        return MpSum(
            part,
            [slots.at[k] for k in range(5)],
            out,
            cuts,
            mp_sends.at[number],
            mp_recvs.at[number],
        )

    sum_a = mp_sum(part_a, slots_a, out_a, CUTS, 0)
    sum_b = mp_sum(part_b, slots_b, out_b, CUTS, 1)
    sum_c = mp_sum(part_c, slots_c, out_c, CUTS, 2)
    sum_d = mp_sum(part_d, slots_d, out_d, CUTS, 3)
    sum_e = mp_sum(part_e, slots_e, out_e, PIXEL_CUTS, 4)

    pieces = []
    for number, (name, kind) in enumerate(kinds):
        pieces.append(
            kind(
                place,
                grads[number],
                slots[number],
                wholes[number],
                dp_sends.at[number],
                dp_recvs.at[number],
            )
        )
    count = len(kinds)
    early = LineGather(
        place,
        bank.at[core],
        dp_sends.at[count + 1],
        dp_recvs.at[count + 1],
        (pair, share_sends, share_recvs, bank.at[1 - core]),
    )
    late = LineGather(place, embed_bank, dp_sends.at[count + 2], dp_recvs.at[count + 2])
    hidden_sum = MpSmall(hidden_part, hidden_slots, hidden_grad, etc_sends.at[pl.ds(3, 3)], etc_recvs.at[pl.ds(3, 3)])
    small = SmallSum(place, small_part, small_pair, small_line, smalls, dp_sends.at[len(kinds)], dp_recvs.at[len(kinds)])

    def put_piece(grad, first_row, block):
        rows = grad.shape[-2]
        for k in range(0, block.shape[0], rows):
            chunk = (first_row + k) // rows
            spot = (chunk,) if len(grad.shape) == 3 else (chunk // lines, chunk % lines)
            grad[spot] = block[k : k + rows].astype(BF16)

    gain_one, shift_one = rows_in[0:1], rows_in[1:2]
    gain_two, shift_two = rows_in[2:3], rows_in[3:4]
    b_down = rows_in[4:5]
    lane_head = lax.broadcasted_iota(jnp.int32, (1, width), 1) // HEAD_DIM
    head_masks = [(lane_head == h).astype(F32).astype(BF16) for h in range(heads)]

    grad_after, grad_tokens = gate_grad, tokens
    etc = Sender(etc_sends, etc_recvs)
    kept = {}

    def iota(rows, lanes, dim):
        return lax.broadcasted_iota(jnp.int32, (rows, lanes), dim)

    def blocks(block, rows, lanes):
        tall = jnp.concatenate([block] * GROUP, axis=0)
        wide = jnp.concatenate([tall] * GROUP, axis=1)
        on = iota(*wide.shape, 0) // rows == iota(*wide.shape, 1) // lanes
        return jnp.where(on, wide.astype(F32), 0.0).astype(BF16)

    pixels = BANDS * PIX
    part_rows = PIX // GROUP // 2
    group_rows = GROUP * SLOTS

    def w_group(g):
        return w_table[:, g * GROUP * HYP : (g + 1) * GROUP * HYP]

    def make_kern():
        need(0)
        row, col = iota(PIX * SLOTS, pixels, 0), iota(PIX * SLOTS, pixels, 1)
        want = lax.rem(row, SLOTS) * PIX + row // SLOTS
        spots[...] = (col == want).astype(F32).astype(BF16)
        chosen = dot(select[...], hidden[...]).astype(BF16)
        wide = blocks(chosen, SLOTS, HYP)
        for g in range(PIX // GROUP):
            kern_grads[g, 0:group_rows] = dot_nt(wide, w_group(g)).astype(BF16)
        rows = jnp.concatenate([kern_grads[g, 0:group_rows] for g in range(PIX // GROUP)], axis=0)
        kern[...] = dot_tn(spots[...], rows).astype(BF16)

    def fill_bank():
        need(1)
        half_rows = PIX * SLOTS // 2
        for c in range(2):

            @pl.when(core == c)
            def _():
                rows = dot(spots[c * half_rows : (c + 1) * half_rows], patches[...])
                bank[c, place.inner, place.outer, 0:half_rows] = rows.astype(BF16)
                bank[c, place.inner, place.outer, half_rows : half_rows + SLOTS, 0:128] = jnp.concatenate(
                    [select[...].astype(F32), jnp.zeros((SLOTS, 128 - NB), F32)], axis=1
                ).astype(BF16)
                bank[c, place.inner, place.outer, half_rows : half_rows + SLOTS, 128:256] = jnp.zeros(
                    (SLOTS, 128), BF16
                )

    def make_picks():
        half_rows = PIX * SLOTS // 2
        for c in range(2 * lines):
            mine = bank[0, c // lines, c % lines, half_rows : half_rows + SLOTS, 0:128]
            picks[c * group_rows : (c + 1) * group_rows] = blocks(mine[:, 0:NB], SLOTS, NB)

    def kern_grad(c):
        block = embed_bank[c // lines, c % lines]
        for h in range(2):
            rows = dot(bank[h, c // lines, c % lines, 0 : PIX * SLOTS // 2], block).astype(BF16)
            for k in range(part_rows):
                kern_grads[h * part_rows + k, c * group_rows : (c + 1) * group_rows] = rows[
                    k * group_rows : (k + 1) * group_rows
                ]

    def kern_grad_half(i):
        for c in range(i * lines, (i + 1) * lines):
            kern_grad(c)

    def table_part(g):
        got = dot_tn(kern_grads[g], picks[...]).astype(BF16)
        table[g * width : (g + 1) * width] = got
        grads_g = dot(got, kept["hidden"])
        if g >= 2:
            kept[g - 2].wait()
        for k in range(GROUP):
            gen_out[g % 2, pl.ds(k, width, stride=GROUP), :] = grads_g[:, k * HYP : (k + 1) * HYP]
        kept[g] = pltpu.make_async_copy(
            gen_out.at[g % 2].reshape(width, GROUP, HYP),
            grad_gen.at[:, pl.ds(g * GROUP, GROUP), :],
            out_sem.at[g % 2],
        )
        kept[g].start()

    def table_start():
        kept["hidden"] = blocks(hidden[...], NB, HYP)

    def hidden_grads():
        flat = jnp.concatenate([w_group(g) for g in range(PIX // GROUP)], axis=0)
        every = dot_tn(table[...], flat)
        total = every[0:NB, 0:HYP]
        for k in range(1, GROUP):
            total = total + every[k * NB : (k + 1) * NB, k * HYP : (k + 1) * HYP]
        hidden_part[...] = total

    def embed():
        need(1)
        embeds[me] = dot_tn(patches[...], kern[...]).astype(BF16)
        mine = embeds.at[me]
        kept["pair"] = etc.go(0, mine, mine, pair)
        kept["far"] = etc.go(1, mine, mine, far)

    def epass():
        kept["far"].wait_recv()
        got = embeds.at[lax.rem(me + 2, 4)]
        kept["passed"] = etc.go(2, got, got, pair)

    def fillgate():
        need(2)
        need(3)
        branch_grad[0:256] = (live_col[0:256] * cotangent[2:258]).astype(BF16)
        branch_grad[256:272] = jnp.concatenate(
            [cotangent[0:2], jnp.zeros((14, full), F32)], axis=0
        ).astype(BF16)
        small_part[...] = jnp.zeros_like(small_part)
        small_part[5:6] = col_sum(branch_grad[...].astype(F32))
        gate_grad[...] = dot_nt(branch_grad[...], w_down[...])

    def tokens_norm():
        need(4)
        kept["pair"].wait_recv()
        kept["passed"].wait_recv()
        for lo, n in CUTS:
            hi = min(lo + n, 256)
            for i in range(4):
                cols = slice(i * width, (i + 1) * width)
                tokens[lo:hi, cols] = embeds[i, lo:hi].astype(F32)
            tokens[lo:hi] += positions[lo:hi]
            if lo + n > 256:
                tokens[256:272] = jnp.concatenate([rows_in[5:7], jnp.zeros((14, full), F32)], axis=0)
            rows = slice(lo, lo + n)
            x = tokens[rows]
            centred = x - row_mean(x)
            rstd = lax.rsqrt(row_mean(centred * centred) + 1e-05)
            rstd_one[rows] = rstd
            xhat = centred * rstd
            xhat_one[rows] = xhat
            normed[rows] = (xhat * gain_one + shift_one).astype(BF16)

    def attention():
        need(5)
        queries[...] = dot_nt(normed[...], w_qkv[0]).astype(BF16)
        keys[...] = dot_nt(normed[...], w_qkv[1]).astype(BF16)
        values[...] = dot_nt(normed[...], w_qkv[2]).astype(BF16)
        live_keys = live_row[...] > 0
        total = None
        for h in range(heads):
            raw = dot_nt(queries[...] * head_masks[h], keys[...]) * 0.125
            raw = jnp.where(live_keys, raw, -1000000000.0)
            expo = jnp.exp(raw - jnp.max(raw, axis=-1, keepdims=True))
            prob = expo / jnp.sum(expo, axis=-1, keepdims=True)
            probs[h] = prob
            term = dot(prob.astype(BF16), values[...] * head_masks[h])
            total = term if total is None else total + term
        mixed[...] = total.astype(BF16)

    def put_part(part, rows, block):
        half = block.shape[1] // 2
        part[0, rows] = block[:, :half].astype(BF16)
        part[1, rows] = block[:, half:].astype(BF16)

    def get_out(out, rows):
        return jnp.concatenate([out[0, rows], out[1, rows]], axis=1)

    def span(i):
        lo, n = CUTS[i]
        return slice(lo, lo + n)

    def attn_part(i):
        need(6)
        put_part(part_a, span(i), dot(mixed[span(i)], w_out[...]))

    def feedforward(i):
        need(7)
        rows = span(i)
        x = tokens[rows] + get_out(out_a, rows)
        after[rows] = x
        centred = x - row_mean(x)
        rstd = lax.rsqrt(row_mean(centred * centred) + 1e-05)
        rstd_two[rows] = rstd
        xhat = centred * rstd
        xhat_two[rows] = xhat
        normed_two[rows] = (xhat * gain_two + shift_two).astype(BF16)
        gate = dot(normed_two[rows], w_up[...]) + b_up[...]
        cdf = 0.5 + 0.5 * lax.erf(gate * (2.0**-0.5))
        activation[rows] = (gate * cdf).astype(BF16)
        pdf = jnp.exp(-0.5 * gate * gate) * ((2.0 * math.pi) ** -0.5)
        grad_pre[rows] = (gate_grad[rows] * (cdf + gate * pdf)).astype(BF16)
        put_part(part_c, rows, dot_nt(grad_pre[rows], w_up[...]))

    half = full // 2

    def grad_of_down(j):
        cols = slice(j * half, (j + 1) * half)
        put_piece(pieces[j].grad, 0, dot_tn(activation[...], branch_grad[:, cols]))

    def grad_of_up(j):
        cols = slice(j * half, (j + 1) * half)
        put_piece(pieces[2 + j].grad, 0, dot_tn(normed_two[...], grad_pre[:, cols]))
        if j == 1:
            small_part[6:7] = col_sum(grad_pre[...].astype(F32))

    def norm_two_back(i):
        rows = span(i)
        lo, n = CUTS[i]
        dy = get_out(out_c, rows)
        xhat = xhat_two[rows]
        small_part[2:3] += col_sum(dy * xhat)
        small_part[3:4] += col_sum(dy)
        e = dy * gain_two
        dx = rstd_two[rows] * (e - row_mean(e) - xhat * row_mean(e * xhat))
        if lo + n <= 256:
            grad_out = live_col[rows] * cotangent[lo + 2 : lo + n + 2]
        else:
            grad_out = jnp.concatenate(
                [live_col[lo:256] * cotangent[lo + 2 : 258], cotangent[0:2], jnp.zeros((14, full), F32)],
                axis=0,
            )
        grad_x = dx + grad_out
        grad_after[rows] = grad_x
        after_low[rows] = grad_x.astype(BF16)

    def mixed_back():
        grad_mixed[...] = dot_nt(after_low[...], w_out[...]).astype(BF16)
        kept["parts"] = [None, None, None]

    def head_back(h):
        mixed_h = grad_mixed[...] * head_masks[h]
        grad_probs = dot_nt(mixed_h, values[...])
        prob = probs[h]
        scores = prob * (grad_probs - jnp.sum(grad_probs * prob, axis=-1, keepdims=True))
        scores = scores.astype(BF16)
        terms = [
            dot(scores, keys[...] * head_masks[h]),
            dot_tn(scores, queries[...] * head_masks[h]),
            dot_tn(prob.astype(BF16), mixed_h),
        ]
        kept["parts"] = [t if p is None else p + t for p, t in zip(kept["parts"], terms)]
        if h == heads - 1:
            for t, scale in enumerate((0.125, 0.125, 1.0)):
                grad_qkv[t] = (kept["parts"][t] * scale).astype(BF16)

    def norm_part(i):
        rows = span(i)
        block = dot(grad_qkv[0, rows], w_qkv[0])
        block = block + dot(grad_qkv[1, rows], w_qkv[1])
        put_part(part_d, rows, block + dot(grad_qkv[2, rows], w_qkv[2]))

    def grad_of_attn(j):
        cols = slice(j * half, (j + 1) * half)
        grad = pieces[4 + j].grad
        put_piece(grad, 0, dot_tn(mixed[...], after_low[:, cols]))
        for t in range(3):
            put_piece(grad, (t + 1) * width, dot_tn(grad_qkv[t], normed[:, cols]))

    def norm_one_back(i):
        rows = span(i)
        dy = get_out(out_d, rows)
        xhat = xhat_one[rows]
        small_part[0:1] += col_sum(dy * xhat)
        small_part[1:2] += col_sum(dy)
        e = dy * gain_one
        dx = rstd_one[rows] * (e - row_mean(e) - xhat * row_mean(e * xhat))
        grad_tokens[rows] = grad_after[rows] + dx

    def embed_grads():
        for i in range(4):

            @pl.when(me == i)
            def _():
                embed_bank[place.inner, place.outer] = grad_tokens[0:256, i * width : (i + 1) * width].astype(BF16)

    def small_ready():
        small_part[4:5] = grad_tokens[256:257]
        small_part[8:16] = meta_col[...] * grad_tokens[257:258]

    def pixel_part():
        pixels = dot_nt(kern[...], embed_bank[place.inner, place.outer]).astype(BF16)
        part_e[0] = pixels[: BANDS * PIX // 2]
        part_e[1] = pixels[BANDS * PIX // 2 :]

    def branch_part():
        need(3)
        for i in range(len(CUTS)):
            put_part(part_b, span(i), dot(activation[span(i)], w_down[...]))

    def final_output():
        for i, (lo, n) in enumerate(CUTS):
            rows = span(i)
            x = after[rows] + get_out(out_b, rows) + b_down
            if lo + n <= 256:
                output[lo + 2 : lo + n + 2] = live_col[rows] * x
            else:
                output[lo + 2 : 258] = live_col[lo:256] * x[: 256 - lo]
                output[0:2] = x[256 - lo : 258 - lo]
        keep(output, far_output)

    def final_pixels():
        grad_patches[: BANDS * PIX // 2] = out_e[0]
        grad_patches[BANDS * PIX // 2 :] = out_e[1]
        keep(grad_patches, far_grad_patches)

    down0, down1, up0, up1, attn0, attn1 = pieces
    order = [
        make_kern,
        embed,
        fill_bank,
        early.step,
        epass,
        tokens_norm,
        attention,
        (attn_part, 0),
        (sum_a.start, 0),
        (attn_part, 3),
        (sum_a.start, 3),
        (attn_part, 2),
        early.step,
        (attn_part, 1),
        (sum_a.relay, 0),
        (sum_a.start, 1),
        fillgate,
        (sum_a.relay, 3),
        (sum_a.start, 2),
        (sum_a.relay, 1),
        (sum_a.relay, 2),
        (sum_a.forward, 0),
        (sum_a.total, 0),
        (sum_a.forward, 3),
        (feedforward, 0),
        (sum_c.start, 0),
        (sum_a.forward, 1),
        (sum_a.total, 3),
        (feedforward, 3),
        (sum_c.start, 3),
        (sum_a.forward, 2),
        (sum_c.relay, 0),
        (sum_a.total, 1),
        (feedforward, 1),
        (sum_c.start, 1),
        (sum_c.relay, 3),
        (sum_a.total, 2),
        (feedforward, 2),
        (grad_of_up, 1),
        up1.step,
        (sum_c.start, 2),
        (sum_c.relay, 1),
        (grad_of_up, 0),
        (sum_c.forward, 0),
        up0.step,
        (grad_of_down, 1),
        (sum_c.relay, 2),
        branch_part,
        (sum_c.forward, 3),
        (sum_c.forward, 1),
        down1.step,
        up1.step,
        (sum_c.forward, 2),
        (sum_c.total, 3),
        (sum_c.total, 0),
        (grad_of_down, 0),
        (sum_c.total, 1),
        (norm_two_back, 0),
        (norm_two_back, 1),
        (sum_c.total, 2),
        (norm_two_back, 2),
        (norm_two_back, 3),
        mixed_back,
        early.step,
        (head_back, 0),
        (head_back, 1),
        (head_back, 2),
        (norm_part, 2),
        (sum_b.start, 3),
        up0.step,
        up0.step,
        (norm_part, 0),
        (norm_part, 3),
        (sum_d.start, 2),
        up1.step,
        (sum_d.start, 0),
        (sum_b.relay, 3),
        (sum_b.start, 1),
        (sum_d.relay, 2),
        (sum_d.start, 3),
        (norm_part, 1),
        (sum_d.start, 1),
        (grad_of_attn, 0),
        down0.step,
        up0.step,
        up1.step,
        (sum_d.relay, 3),
        (sum_d.forward, 2),
        (sum_d.relay, 0),
        (sum_d.total, 2),
        up0.step,
        up0.step,
        (sum_d.relay, 1),
        (grad_of_attn, 1),
        attn0.step,
        (sum_b.relay, 1),
        down0.step,
        (sum_d.forward, 3),
        attn1.step,
        (sum_d.forward, 0),
        (sum_d.forward, 1),
        (sum_d.total, 3),
        (sum_d.total, 0),
        up1.step,
        (norm_one_back, 0),
        (norm_one_back, 3),
        early.step,
        (sum_d.total, 1),
        (norm_one_back, 2),
        (sum_b.start, 0),
        (sum_b.forward, 1),
        (norm_one_back, 1),
        embed_grads,
        down1.step,
        (sum_b.forward, 3),
        late.step,
        pixel_part,
        down1.step,
        small_ready,
        up0.step,
        (sum_b.start, 2),
        (sum_b.total, 1),
        (sum_e.start, 1),
        down0.step,
        down0.step,
        attn0.step,
        attn0.step,
        small.start,
        down1.step,
        late.step,
        down1.step,
        table_start,
        down1.step,
        up0.step,
        late.step,
        (sum_e.relay, 1),
        (sum_b.relay, 2),
        attn0.step,
        down1.step,
        (sum_e.start, 0),
        attn1.step,
        (sum_b.total, 3),
        up1.step,
        (sum_b.relay, 0),
        late.step,
        attn0.step,
        attn0.step,
        down0.step,
        attn1.step,
        down1.step,
        attn1.step,
        attn0.step,
        up0.step,
        (sum_e.relay, 0),
        early.step,
        attn1.step,
        small.relay,
        early.drain,
        attn0.step,
        late.step,
        late.drain,
        (sum_b.forward, 0),
        (sum_b.forward, 2),
        make_picks,
        (kern_grad_half, 0),
        (kern_grad_half, 1),
        (sum_b.total, 0),
        attn1.step,
        up1.step,
        (sum_e.forward, 1),
        (table_part, 0),
        attn1.step,
        (table_part, 1),
        (table_part, 2),
        down0.step,
        up1.step,
        (table_part, 3),
        down1.step,
        (table_part, 4),
        attn1.step,
        (sum_e.forward, 0),
        up0.step,
        down1.step,
        (table_part, 5),
        (sum_b.total, 2),
        final_output,
        up0.step,
        (table_part, 6),
        attn0.step,
        attn1.step,
        (table_part, 7),
        hidden_grads,
        (sum_e.total, 0),
        (sum_e.total, 1),
        down0.step,
        small.total,
        attn1.step,
        up1.step,
        attn0.step,
        up1.step,
        final_pixels,
        down1.step,
        hidden_sum.begin,
        down0.step,
        attn1.step,
        hidden_sum.total,
        attn0.step,
        down0.step,
        down0.step,
    ]
    def send_out(number):
        keep(wholes[number], far_wholes[number])

    for number, piece in enumerate(pieces):
        piece.steps.append(functools.partial(send_out, number))
    for item in order:
        if isinstance(item, tuple):
            item[0](*item[1:])
        else:
            item()
    for piece in pieces:
        piece.drain()
    for copy in stores:
        copy.wait()
    for g in range(PIX // GROUP - 2, PIX // GROUP):
        kept[g].wait()
    for one in (sum_a, sum_b, sum_c, sum_d, sum_e, etc, hidden_sum):
        one.finish()


def layer(dp_count, width, operands):
    lines = dp_count // 2

    def piece(rows, lanes, parts):
        chunk = -(-rows // parts)
        chunk = -(-chunk // 16) * 16
        if parts == lines:
            return (lines, chunk, lanes)
        return (2, lines, chunk, lanes)

    pieces = []
    for name, kind in KINDS:
        parts = dp_count if kind is PairFirst else lines
        pieces.append(piece(4 * width, D // 2, parts))

    def piece_scratch(shape):
        if len(shape) == 4:
            return [low(*shape[1:]), low(*shape[1:]), low(2, *shape[1:]), vmem(*shape[2:])]
        return [low(2, *shape), vmem(*shape[1:]), low(*shape[1:]), low(*shape[1:])]

    half = D // 2
    pixel_lanes = BANDS * PIX

    def vmem(*shape, dtype=F32):
        return pltpu.VMEM(shape, dtype)

    def low(*shape):
        return pltpu.VMEM(shape, BF16)

    scratch = [
        low(4, 256, width),
        vmem(ROWS, D),
        vmem(ROWS, D),
        vmem(ROWS, 1),
        vmem(ROWS, D),
        vmem(ROWS, 1),
        vmem(ROWS, D),
        low(ROWS, D),
        low(ROWS, D),
        low(ROWS, width),
        low(ROWS, width),
        low(ROWS, width),
        vmem(width // HEAD_DIM, ROWS, ROWS),
        low(ROWS, width),
        low(ROWS, width),
        low(3, ROWS, width),
        low(ROWS, D),
        vmem(ROWS, D),
        low(ROWS, D),
        low(ROWS, D),
        low(ROWS, D),
        low(2, 2, lines, PIX * SLOTS // 2 + SLOTS, 256),
        low(2, lines, 256, width),
        low(PIX * SLOTS, pixel_lanes),
        low(pixel_lanes, width),
        low(dp_count * GROUP * SLOTS, GROUP * NB),
        low(PIX // GROUP, dp_count * GROUP * SLOTS, width),
        low(PIX // GROUP * width, GROUP * NB),
        vmem(2, width * GROUP, HYP),
        vmem(NB, HYP),
        vmem(4, NB, HYP),
    ]
    scratch += [low(2, ROWS, half)] * 4 + [low(2, pixel_lanes // 2, 256)]
    scratch += [low(5, ROWS, half)] * 4 + [low(5, pixel_lanes // 2, 256)]
    scratch += [vmem(2, ROWS, half)] * 4 + [vmem(2, pixel_lanes // 2, 256)]
    scratch.append([low(*shape) for shape in pieces])
    scratch.append([piece_scratch(shape) for shape in pieces])
    scratch += [vmem(16, D), vmem(16, D), vmem(lines, 16, D)]
    dma = pltpu.SemaphoreType.DMA
    scratch += [dma((5, 16)), dma((5, 16)), dma((len(pieces) + 3, 4 * lines + 1)), dma((len(pieces) + 3, 4 * lines + 1)), dma((6,)), dma((6,))]
    scratch += [dma((dp_count,)), dma((dp_count,)), dma((2,))]
    far = pl.BlockSpec(memory_space=pl.ANY)
    big = (0, 2, 3, 9, 10, 11, 13, 14)
    scratch += [pltpu.VMEM(operands[k].shape, operands[k].dtype) for k in big]
    scratch += [vmem(SEQ, D), vmem(pixel_lanes, 256), [low(*shape) for shape in pieces]]
    scratch += [dma((len(big),)), dma((len(pieces) + 2,))]
    ref = pl.BlockSpec(memory_space=pltpu.VMEM)
    shapes = [
        jax.ShapeDtypeStruct((SEQ, D), F32),
        jax.ShapeDtypeStruct((pixel_lanes, 256), F32),
        jax.ShapeDtypeStruct((16, D), F32),
        jax.ShapeDtypeStruct((NB, HYP), F32),
        jax.ShapeDtypeStruct((width, PIX, HYP), F32),
        [jax.ShapeDtypeStruct(shape, BF16) for shape in pieces],
    ]
    output, grad_patches, smalls, hidden_grad, grad_gen, wholes = pl.pallas_call(
        functools.partial(layer_kernel, lines, KINDS),
        out_shape=shapes,
        in_specs=[far if k in big else ref for k in range(len(operands))],
        out_specs=[far, far, ref, ref, far, [far] * len(pieces)],
        scratch_shapes=scratch,
        compiler_params=pltpu.CompilerParams(
            collective_id=0, has_side_effects=True, vmem_limit_bytes=62 * 1024 * 1024
        ),
        name="layer",
    )(*operands)
    wholes = {name: out.reshape(-1, out.shape[-1]) for (name, kind), out in zip(KINDS, wholes)}
    return output, grad_patches, smalls, hidden_grad, grad_gen, wholes


def local(
    dp_count,
    patches,
    wavelengths,
    band_ids,
    band_mask,
    sensor,
    lengths,
    visible,
    meta,
    w_hyper,
    b_hyper,
    w_gen,
    cls_token,
    w_meta,
    gain_one,
    shift_one,
    w_qkv,
    w_out,
    gain_two,
    shift_two,
    w_up,
    b_up,
    w_down,
    b_down,
    cotangent,
):
    highest = lax.Precision.HIGHEST
    width = w_gen.shape[0]
    features = sinus_waves(wavelengths, HYP)
    positions = grid_codes(visible, lengths, D, VIS_MAX)[0]
    hyper_pre = jnp.dot(features, w_hyper, precision=highest) + b_hyper
    hidden, hyper_pull = jax.vjp(gelu_exact, hyper_pre)
    hidden_low = hidden.astype(BF16)
    ids, mask = band_ids[sensor[0]], band_mask[sensor[0]]
    select = (ids[:, None] == jnp.arange(NB)[None, :]).astype(F32) * mask[:, None].astype(F32)
    place = jnp.arange(ROWS)
    live = ((place < lengths[0]) | ((place >= 256) & (place < SEQ))).astype(F32)
    meta_row = jnp.dot(meta, w_meta, precision=highest)[0]
    rows_in = jnp.stack([gain_one, shift_one, gain_two, shift_two, b_down, cls_token, meta_row, meta_row])
    operands = (
        patches[0].T,
        hidden_low,
        w_gen.reshape(width, PIX * HYP),
        positions,
        rows_in,
        meta.reshape(-1, 1),
        live[None, :],
        live[:, None],
        jnp.pad(select.astype(BF16), ((0, 16 - BANDS), (0, 0))),
        w_qkv,
        w_out,
        w_up,
        b_up[None, :],
        w_down,
        cotangent[0],
    )
    output, grad_patches, smalls, grad_hidden, grad_w_gen, wholes = layer(dp_count, width, operands)

    def joined(name):
        halves = [wholes[f"{name}{j}"][: 4 * width] for j in range(2)]
        return jnp.concatenate(halves, axis=1).astype(F32)

    grad_w_down, grad_w_up, attn = joined("down"), joined("up"), joined("attn")
    grad_inner = hyper_pull(grad_hidden)[0]
    grad_w_hyper = jnp.dot(features.T, grad_inner, precision=highest)
    grad_b_hyper = jnp.sum(grad_inner, axis=0)
    return (
        output[None],
        grad_patches.T[None],
        grad_w_hyper,
        grad_b_hyper,
        grad_w_gen,
        smalls[4],
        smalls[8:16],
        smalls[0],
        smalls[1],
        attn[width : 4 * width].reshape(3, width, D),
        attn[:width],
        smalls[2],
        smalls[3],
        grad_w_up,
        smalls[6],
        grad_w_down,
        smalls[5],
    )


KINDS_MANY = (
    ("down0", PairFirst),
    ("down1", PairFirst),
    ("up0", PairFirst),
    ("up1", LineFirst),
    ("attn0", PairFirst),
    ("attn1", PairFirst),
    ("table0", PairFirst),
)


def layer_kernel_many(
    lines,
    kinds,
    patches,
    kern,
    positions,
    rows_in,
    meta_col,
    live_row,
    live_col,
    select,
    w_qkv,
    w_out,
    w_up,
    b_up,
    w_down,
    cotangent,
    output,
    grad_patches,
    smalls,
    wholes,
    embeds,
    tokens,
    xhat_one,
    rstd_one,
    xhat_two,
    rstd_two,
    after,
    normed,
    normed_two,
    queries,
    keys,
    values,
    probs,
    mixed,
    grad_mixed,
    grad_qkv,
    branch_grad,
    gate_grad,
    activation,
    grad_pre,
    grad_after,
    after_low,
    grad_tokens,
    embed_grad,
    spread,
    part_a,
    part_b,
    part_c,
    part_d,
    part_e,
    slots_a,
    slots_b,
    slots_c,
    slots_d,
    slots_e,
    out_a,
    out_b,
    out_c,
    out_d,
    out_e,
    grads,
    slots,
    small_part,
    small_pair,
    small_line,
    mp_sends,
    mp_recvs,
    dp_sends,
    dp_recvs,
    etc_sends,
    etc_recvs,
):
    core, pair, far = mp_peers()
    place = DpPlace(lines)
    greet([pair, far, place.pair] + [place.peer(k) for k in range(1, lines)])
    me = lax.axis_index("mp")
    width = w_out.shape[0]
    heads = width // HEAD_DIM
    full = D

    def mp_sum(part, slots, out, cuts, number):
        return MpSum(
            part,
            [slots.at[k] for k in range(5)],
            out,
            cuts,
            mp_sends.at[number],
            mp_recvs.at[number],
        )

    sum_a = mp_sum(part_a, slots_a, out_a, CUTS, 0)
    sum_b = mp_sum(part_b, slots_b, out_b, CUTS, 1)
    sum_c = mp_sum(part_c, slots_c, out_c, CUTS, 2)
    sum_d = mp_sum(part_d, slots_d, out_d, CUTS, 3)
    sum_e = mp_sum(part_e, slots_e, out_e, PIXEL_CUTS, 4)

    pieces = []
    for number, (name, kind) in enumerate(kinds):
        pieces.append(
            kind(
                place,
                grads[number],
                slots[number],
                wholes[number],
                dp_sends.at[number],
                dp_recvs.at[number],
            )
        )
    small = SmallSum(place, small_part, small_pair, small_line, smalls, dp_sends.at[len(kinds)], dp_recvs.at[len(kinds)])

    def put_piece(grad, first_row, block):
        rows = grad.shape[-2]
        for k in range(0, block.shape[0], rows):
            chunk = (first_row + k) // rows
            spot = (chunk,) if len(grad.shape) == 3 else (chunk // lines, chunk % lines)
            grad[spot] = block[k : k + rows].astype(BF16)

    gain_one, shift_one = rows_in[0:1], rows_in[1:2]
    gain_two, shift_two = rows_in[2:3], rows_in[3:4]
    b_down = rows_in[4:5]
    lane_head = lax.broadcasted_iota(jnp.int32, (1, width), 1) // HEAD_DIM
    head_masks = [(lane_head == h).astype(F32).astype(BF16) for h in range(heads)]

    etc = Sender(etc_sends, etc_recvs)
    kept = {}

    def embed():
        embeds[me] = dot_tn(patches[...], kern[...]).astype(BF16)
        mine = embeds.at[me]
        kept["pair"] = etc.go(0, mine, mine, pair)
        kept["far"] = etc.go(1, mine, mine, far)

    def epass():
        kept["far"].wait_recv()
        got = embeds.at[lax.rem(me + 2, 4)]
        kept["passed"] = etc.go(2, got, got, pair)

    def fillgate():
        branch_grad[0:256] = (live_col[0:256] * cotangent[2:258]).astype(BF16)
        branch_grad[256:272] = jnp.concatenate(
            [cotangent[0:2], jnp.zeros((14, full), F32)], axis=0
        ).astype(BF16)
        small_part[...] = jnp.zeros_like(small_part)
        small_part[5:6] = col_sum(branch_grad[...].astype(F32))
        gate_grad[...] = dot_nt(branch_grad[...], w_down[...])

    def tokens_norm():
        kept["pair"].wait_recv()
        kept["passed"].wait_recv()
        for lo, n in CUTS:
            hi = min(lo + n, 256)
            for i in range(4):
                cols = slice(i * width, (i + 1) * width)
                tokens[lo:hi, cols] = embeds[i, lo:hi].astype(F32)
            tokens[lo:hi] += positions[lo:hi]
            if lo + n > 256:
                tokens[256:272] = jnp.concatenate([rows_in[5:7], jnp.zeros((14, full), F32)], axis=0)
            rows = slice(lo, lo + n)
            x = tokens[rows]
            centred = x - row_mean(x)
            rstd = lax.rsqrt(row_mean(centred * centred) + 1e-05)
            rstd_one[rows] = rstd
            xhat = centred * rstd
            xhat_one[rows] = xhat
            normed[rows] = (xhat * gain_one + shift_one).astype(BF16)

    def attention():
        queries[...] = dot_nt(normed[...], w_qkv[0]).astype(BF16)
        keys[...] = dot_nt(normed[...], w_qkv[1]).astype(BF16)
        values[...] = dot_nt(normed[...], w_qkv[2]).astype(BF16)
        live_keys = live_row[...] > 0
        total = None
        for h in range(heads):
            raw = dot_nt(queries[...] * head_masks[h], keys[...]) * 0.125
            raw = jnp.where(live_keys, raw, -1000000000.0)
            expo = jnp.exp(raw - jnp.max(raw, axis=-1, keepdims=True))
            prob = expo / jnp.sum(expo, axis=-1, keepdims=True)
            probs[h] = prob
            term = dot(prob.astype(BF16), values[...] * head_masks[h])
            total = term if total is None else total + term
        mixed[...] = total.astype(BF16)

    def put_part(part, rows, block):
        half = block.shape[1] // 2
        part[0, rows] = block[:, :half].astype(BF16)
        part[1, rows] = block[:, half:].astype(BF16)

    def get_out(out, rows):
        return jnp.concatenate([out[0, rows], out[1, rows]], axis=1)

    def span(i):
        lo, n = CUTS[i]
        return slice(lo, lo + n)

    def attn_part(i):
        put_part(part_a, span(i), dot(mixed[span(i)], w_out[...]))

    def feedforward(i):
        rows = span(i)
        x = tokens[rows] + get_out(out_a, rows)
        after[rows] = x
        centred = x - row_mean(x)
        rstd = lax.rsqrt(row_mean(centred * centred) + 1e-05)
        rstd_two[rows] = rstd
        xhat = centred * rstd
        xhat_two[rows] = xhat
        normed_two[rows] = (xhat * gain_two + shift_two).astype(BF16)
        gate = dot(normed_two[rows], w_up[...]) + b_up[...]
        cdf = 0.5 + 0.5 * lax.erf(gate * (2.0**-0.5))
        activation[rows] = (gate * cdf).astype(BF16)
        pdf = jnp.exp(-0.5 * gate * gate) * ((2.0 * math.pi) ** -0.5)
        grad_pre[rows] = (gate_grad[rows] * (cdf + gate * pdf)).astype(BF16)
        put_part(part_c, rows, dot_nt(grad_pre[rows], w_up[...]))

    half = full // 2

    def grad_of_down(j):
        cols = slice(j * half, (j + 1) * half)
        put_piece(pieces[j].grad, 0, dot_tn(activation[...], branch_grad[:, cols]))

    def grad_of_up(j):
        cols = slice(j * half, (j + 1) * half)
        put_piece(pieces[2 + j].grad, 0, dot_tn(normed_two[...], grad_pre[:, cols]))
        if j == 1:
            small_part[6:7] = col_sum(grad_pre[...].astype(F32))

    def norm_two_back(i):
        rows = span(i)
        lo, n = CUTS[i]
        dy = get_out(out_c, rows)
        xhat = xhat_two[rows]
        small_part[2:3] += col_sum(dy * xhat)
        small_part[3:4] += col_sum(dy)
        e = dy * gain_two
        dx = rstd_two[rows] * (e - row_mean(e) - xhat * row_mean(e * xhat))
        if lo + n <= 256:
            grad_out = live_col[rows] * cotangent[lo + 2 : lo + n + 2]
        else:
            grad_out = jnp.concatenate(
                [live_col[lo:256] * cotangent[lo + 2 : 258], cotangent[0:2], jnp.zeros((14, full), F32)],
                axis=0,
            )
        grad_x = dx + grad_out
        grad_after[rows] = grad_x
        after_low[rows] = grad_x.astype(BF16)

    def mixed_back():
        grad_mixed[...] = dot_nt(after_low[...], w_out[...]).astype(BF16)
        kept["parts"] = [None, None, None]

    def head_back(h):
        mixed_h = grad_mixed[...] * head_masks[h]
        grad_probs = dot_nt(mixed_h, values[...])
        prob = probs[h]
        scores = prob * (grad_probs - jnp.sum(grad_probs * prob, axis=-1, keepdims=True))
        scores = scores.astype(BF16)
        terms = [
            dot(scores, keys[...] * head_masks[h]),
            dot_tn(scores, queries[...] * head_masks[h]),
            dot_tn(prob.astype(BF16), mixed_h),
        ]
        kept["parts"] = [t if p is None else p + t for p, t in zip(kept["parts"], terms)]
        if h == heads - 1:
            for t, scale in enumerate((0.125, 0.125, 1.0)):
                grad_qkv[t] = (kept["parts"][t] * scale).astype(BF16)

    def norm_part(i):
        rows = span(i)
        block = dot(grad_qkv[0, rows], w_qkv[0])
        block = block + dot(grad_qkv[1, rows], w_qkv[1])
        put_part(part_d, rows, block + dot(grad_qkv[2, rows], w_qkv[2]))

    def grad_of_attn(j):
        cols = slice(j * half, (j + 1) * half)
        grad = pieces[4 + j].grad
        put_piece(grad, 0, dot_tn(mixed[...], after_low[:, cols]))
        for t in range(3):
            put_piece(grad, (t + 1) * width, dot_tn(grad_qkv[t], normed[:, cols]))

    wide = NB * PIX

    def selection():
        band = lax.broadcasted_iota(jnp.int32, (BANDS * PIX, 16), 0) // PIX
        slot = lax.broadcasted_iota(jnp.int32, (BANDS * PIX, 16), 1)
        row_select = dot((band == slot).astype(F32).astype(BF16), select[...]).astype(BF16)
        table_band = lax.broadcasted_iota(jnp.int32, (NB, wide), 0)
        table_lane = lax.broadcasted_iota(jnp.int32, (NB, wide), 1) // PIX
        widen = (table_band == table_lane).astype(F32).astype(BF16)
        for b in range(BANDS):
            rows = slice(b * PIX, (b + 1) * PIX)
            spot = lax.broadcasted_iota(jnp.int32, (PIX, wide), 0)
            lane = lax.rem(lax.broadcasted_iota(jnp.int32, (PIX, wide), 1), PIX)
            block = dot(row_select[rows], widen)
            spread[rows] = jnp.where(spot == lane, block, 0.0).astype(BF16)

    def norm_one_back(i):
        rows = span(i)
        dy = get_out(out_d, rows)
        xhat = xhat_one[rows]
        small_part[0:1] += col_sum(dy * xhat)
        small_part[1:2] += col_sum(dy)
        e = dy * gain_one
        dx = rstd_one[rows] * (e - row_mean(e) - xhat * row_mean(e * xhat))
        grad_tokens[rows] = grad_after[rows] + dx

    def table_grad():
        for i in range(4):

            @pl.when(me == i)
            def _():
                embed_grad[...] = grad_tokens[0:256, i * width : (i + 1) * width].astype(BF16)

        grad_kern = dot(patches[...], embed_grad[...]).astype(BF16)
        table = dot_tn(grad_kern, spread[...])
        put_piece(pieces[6].grad, 0, table[:, : wide // 2])
        put_piece(pieces[6].grad, width, table[:, wide // 2 :])

    def small_ready():
        small_part[4:5] = grad_tokens[256:257]
        small_part[8:16] = meta_col[...] * grad_tokens[257:258]

    def pixel_part():
        pixels = dot_nt(kern[...], embed_grad[...]).astype(BF16)
        part_e[0] = pixels[: BANDS * PIX // 2]
        part_e[1] = pixels[BANDS * PIX // 2 :]

    def branch_part():
        for i in range(len(CUTS)):
            put_part(part_b, span(i), dot(activation[span(i)], w_down[...]))

    def final_output():
        for i, (lo, n) in enumerate(CUTS):
            rows = span(i)
            x = after[rows] + get_out(out_b, rows) + b_down
            if lo + n <= 256:
                output[lo + 2 : lo + n + 2] = live_col[rows] * x
            else:
                output[lo + 2 : 258] = live_col[lo:256] * x[: 256 - lo]
                output[0:2] = x[256 - lo : 258 - lo]

    def final_pixels():
        grad_patches[: BANDS * PIX // 2] = out_e[0]
        grad_patches[BANDS * PIX // 2 :] = out_e[1]

    down0, down1, up0, up1, attn0, attn1, table0 = pieces
    order = [
        embed,
        fillgate,
        selection,
        epass,
        tokens_norm,
        attention,
        (attn_part, 0),
        (sum_a.start, 0),
        (attn_part, 1),
        (sum_a.start, 1),
        (attn_part, 2),
        (sum_a.start, 2),
        (attn_part, 3),
        (sum_a.start, 3),
        (sum_a.relay, 0),
        (sum_a.relay, 1),
        (sum_a.relay, 2),
        (sum_a.relay, 3),
        (sum_a.forward, 0),
        (sum_a.forward, 1),
        (sum_a.total, 0),
        (feedforward, 0),
        (sum_a.total, 1),
        (sum_a.forward, 2),
        (sum_c.start, 0),
        (feedforward, 1),
        (sum_a.forward, 3),
        (sum_a.total, 2),
        (sum_c.relay, 0),
        (sum_c.start, 1),
        (feedforward, 2),
        (sum_a.total, 3),
        (sum_c.start, 2),
        (feedforward, 3),
        (sum_c.relay, 1),
        (sum_c.relay, 2),
        (sum_c.forward, 0),
        (sum_c.start, 3),
        (grad_of_down, 0),
        (grad_of_down, 1),
        down0.step,
        (sum_c.total, 0),
        down1.step,
        (sum_c.relay, 3),
        (grad_of_up, 0),
        up0.step,
        (sum_c.forward, 1),
        (grad_of_up, 1),
        up1.step,
        (sum_c.forward, 2),
        (norm_two_back, 0),
        (sum_c.total, 1),
        (norm_two_back, 1),
        (sum_c.total, 2),
        (sum_c.forward, 3),
        (norm_two_back, 2),
        branch_part,
        (sum_c.total, 3),
        (norm_two_back, 3),
        mixed_back,
        (head_back, 0),
        down0.step,
        down0.step,
        up1.step,
        (head_back, 1),
        (head_back, 2),
        (norm_part, 0),
        (sum_d.start, 0),
        (norm_part, 1),
        (sum_d.start, 1),
        (norm_part, 2),
        (sum_d.start, 2),
        (norm_part, 3),
        (sum_d.start, 3),
        (grad_of_attn, 0),
        (sum_d.relay, 0),
        (sum_d.relay, 1),
        (sum_d.relay, 2),
        down1.step,
        (sum_d.relay, 3),
        down0.step,
        down1.step,
        up1.step,
        up1.step,
        attn0.step,
        (grad_of_attn, 1),
        attn1.step,
        (sum_b.start, 0),
        (sum_b.start, 1),
        (sum_b.start, 2),
        (sum_b.start, 3),
        (sum_d.forward, 0),
        (sum_b.relay, 0),
        (sum_b.relay, 1),
        (sum_b.relay, 2),
        (sum_d.forward, 1),
        down0.step,
        down0.step,
        (sum_b.relay, 3),
        (sum_d.total, 0),
        (norm_one_back, 0),
        (sum_d.forward, 2),
        down1.step,
        (sum_d.total, 1),
        (norm_one_back, 1),
        (sum_d.forward, 3),
        up0.step,
        (sum_d.total, 2),
        up0.step,
        (norm_one_back, 2),
        up1.step,
        (sum_d.total, 3),
        (norm_one_back, 3),
        table_grad,
        down0.step,
        table0.step,
        down1.step,
        down1.step,
        up0.step,
        small_ready,
        small.start,
        pixel_part,
        (sum_e.start, 0),
        (sum_e.start, 1),
        (sum_b.forward, 0),
        (sum_b.forward, 1),
        (sum_b.forward, 2),
        (sum_b.forward, 3),
        attn0.step,
        attn0.step,
        (sum_e.relay, 0),
        (sum_e.relay, 1),
        (sum_b.total, 0),
        (sum_b.total, 1),
        (sum_b.total, 2),
        (sum_b.total, 3),
        final_output,
        down0.step,
        down1.step,
        attn0.step,
        up0.step,
        up0.step,
        (sum_e.forward, 0),
        attn1.step,
        down0.step,
        attn1.step,
        (sum_e.total, 0),
        (sum_e.forward, 1),
        (sum_e.total, 1),
        down1.step,
        final_pixels,
        up1.step,
        attn0.step,
        attn0.step,
        attn1.step,
        down0.step,
        up0.step,
        down1.step,
        up1.step,
        attn0.step,
        attn1.step,
        attn1.step,
        table0.step,
        table0.step,
        small.relay,
        down1.step,
        up0.step,
        up1.step,
        table0.step,
        attn0.step,
        attn1.step,
        down0.step,
        small.total,
        up0.step,
        table0.step,
        table0.step,
        down1.step,
        up1.step,
        up1.step,
        attn0.step,
        attn1.step,
        up0.step,
        table0.step,
        attn0.step,
        attn1.step,
        up0.step,
        table0.step,
        attn1.step,
        attn0.step,
        table0.step,
        attn1.step,
        table0.step,
        table0.step,
    ]
    for item in order:
        if isinstance(item, tuple):
            item[0](*item[1:])
        else:
            item()
    while any(piece.steps for piece in pieces):
        for piece in pieces:
            piece.step()
    for one in (sum_a, sum_b, sum_c, sum_d, sum_e, etc):
        one.finish()


def layer_many(dp_count, width, operands):
    lines = dp_count // 2

    def piece(rows, lanes, parts):
        chunk = -(-rows // parts)
        chunk = -(-chunk // 16) * 16
        if parts == lines:
            return (lines, chunk, lanes)
        return (2, lines, chunk, lanes)

    pieces = []
    for name, kind in KINDS_MANY:
        parts = dp_count if kind is PairFirst else lines
        if name == "table0":
            pieces.append(piece(2 * width, NB * PIX // 2, parts))
        else:
            pieces.append(piece(4 * width, D // 2, parts))

    def piece_scratch(shape):
        if len(shape) == 4:
            return [low(*shape[1:]), low(*shape[1:]), low(2, *shape[1:]), vmem(*shape[2:])]
        return [low(2, *shape), vmem(*shape[1:]), low(*shape[1:]), low(*shape[1:])]

    half = D // 2
    pixel_lanes = BANDS * PIX

    def vmem(*shape, dtype=F32):
        return pltpu.VMEM(shape, dtype)

    def low(*shape):
        return pltpu.VMEM(shape, BF16)

    scratch = [
        low(4, 256, width),
        vmem(ROWS, D),
        vmem(ROWS, D),
        vmem(ROWS, 1),
        vmem(ROWS, D),
        vmem(ROWS, 1),
        vmem(ROWS, D),
        low(ROWS, D),
        low(ROWS, D),
        low(ROWS, width),
        low(ROWS, width),
        low(ROWS, width),
        vmem(width // HEAD_DIM, ROWS, ROWS),
        low(ROWS, width),
        low(ROWS, width),
        low(3, ROWS, width),
        low(ROWS, D),
        vmem(ROWS, D),
        low(ROWS, D),
        low(ROWS, D),
        vmem(ROWS, D),
        low(ROWS, D),
        vmem(ROWS, D),
        low(256, width),
        low(pixel_lanes, NB * PIX),
    ]
    scratch += [low(2, ROWS, half)] * 4 + [low(2, pixel_lanes // 2, 256)]
    scratch += [low(5, ROWS, half)] * 4 + [low(5, pixel_lanes // 2, 256)]
    scratch += [vmem(2, ROWS, half)] * 4 + [vmem(2, pixel_lanes // 2, 256)]
    scratch.append([low(*shape) for shape in pieces])
    scratch.append([piece_scratch(shape) for shape in pieces])
    scratch += [vmem(16, D), vmem(16, D), vmem(lines, 16, D)]
    dma = pltpu.SemaphoreType.DMA
    scratch += [dma((5, 16)), dma((5, 16)), dma((len(pieces) + 1, 4 * lines + 1)), dma((len(pieces) + 1, 4 * lines + 1)), dma((3,)), dma((3,))]
    ref = pl.BlockSpec(memory_space=pltpu.VMEM)
    shapes = [
        jax.ShapeDtypeStruct((SEQ, D), F32),
        jax.ShapeDtypeStruct((pixel_lanes, 256), F32),
        jax.ShapeDtypeStruct((16, D), F32),
        [jax.ShapeDtypeStruct(shape, BF16) for shape in pieces],
    ]
    output, grad_patches, smalls, wholes = pl.pallas_call(
        functools.partial(layer_kernel_many, lines, KINDS_MANY),
        out_shape=shapes,
        in_specs=[ref] * len(operands),
        out_specs=[ref] * 3 + [[ref] * len(pieces)],
        scratch_shapes=scratch,
        compiler_params=pltpu.CompilerParams(
            collective_id=0, has_side_effects=True, vmem_limit_bytes=62 * 1024 * 1024
        ),
        name="layer",
    )(*operands)
    wholes = {name: out.reshape(-1, out.shape[-1]) for (name, kind), out in zip(KINDS_MANY, wholes)}
    return output, grad_patches, smalls, wholes


def small_sum_kernel_many(axis, count, part, out, slots, sends, recvs):
    me = lax.axis_index(axis)
    peers = [{axis: lax.rem(me + k, count)} for k in range(1, count)]
    greet(peers)
    copies = []
    for k, peer in enumerate(peers):
        copy = remote(part, slots.at[me], sends.at[k], recvs.at[k], peer)
        copy.start()
        copies.append(copy)
    slots[me] = part[...]
    for copy in copies:
        copy.wait()
    total = slots[0]
    for k in range(1, count):
        total = total + slots[k]
    out[...] = total


def small_sum_many(part, axis, count, number):
    vmem = pl.BlockSpec(memory_space=pltpu.VMEM)
    return pl.pallas_call(
        functools.partial(small_sum_kernel_many, axis, count),
        out_shape=jax.ShapeDtypeStruct(part.shape, F32),
        in_specs=[vmem],
        out_specs=vmem,
        scratch_shapes=[
            pltpu.VMEM((count,) + part.shape, F32),
            pltpu.SemaphoreType.DMA((count - 1,)),
            pltpu.SemaphoreType.DMA((count - 1,)),
        ],
        compiler_params=pltpu.CompilerParams(collective_id=number, has_side_effects=True),
        name="small_sum_" + axis,
    )(part)


def local_many(
    dp_count,
    patches,
    wavelengths,
    band_ids,
    band_mask,
    sensor,
    lengths,
    visible,
    meta,
    w_hyper,
    b_hyper,
    w_gen,
    cls_token,
    w_meta,
    gain_one,
    shift_one,
    w_qkv,
    w_out,
    gain_two,
    shift_two,
    w_up,
    b_up,
    w_down,
    b_down,
    cotangent,
):
    highest = lax.Precision.HIGHEST
    width = w_gen.shape[0]
    features = sinus_waves(wavelengths, HYP)
    positions = grid_codes(visible, lengths, D, VIS_MAX)[0]
    hyper_pre = jnp.dot(features, w_hyper, precision=highest) + b_hyper
    hidden, hyper_pull = jax.vjp(gelu_exact, hyper_pre)
    hidden_low = hidden.astype(BF16)
    ids, mask = band_ids[sensor[0]], band_mask[sensor[0]]
    select = (ids[:, None] == jnp.arange(NB)[None, :]).astype(F32) * mask[:, None].astype(F32)
    chosen = jnp.dot(select.astype(BF16), hidden_low, preferred_element_type=F32).astype(BF16)
    kern = jnp.einsum("bh,dph->bpd", chosen, w_gen, preferred_element_type=F32).astype(BF16)
    kern = kern.reshape(BANDS * PIX, width)
    place = jnp.arange(ROWS)
    live = ((place < lengths[0]) | ((place >= 256) & (place < SEQ))).astype(F32)
    meta_row = jnp.dot(meta, w_meta, precision=highest)[0]
    rows_in = jnp.stack([gain_one, shift_one, gain_two, shift_two, b_down, cls_token, meta_row, meta_row])
    operands = (
        patches[0].T,
        kern,
        positions,
        rows_in,
        meta.reshape(-1, 1),
        live[None, :],
        live[:, None],
        jnp.pad(select.astype(BF16), ((0, 16 - BANDS), (0, 0))),
        w_qkv,
        w_out,
        w_up,
        b_up[None, :],
        w_down,
        cotangent[0],
    )
    output, grad_patches, smalls, wholes = layer_many(dp_count, width, operands)

    def joined(name):
        halves = [wholes[f"{name}{j}"][: 4 * width] for j in range(2)]
        return jnp.concatenate(halves, axis=1).astype(F32)

    grad_w_down, grad_w_up, attn = joined("down"), joined("up"), joined("attn")
    table = wholes["table0"][: 2 * width].reshape(2, width, NB // 2, PIX)
    low_halves = hidden_low.reshape(2, NB // 2, HYP)
    grad_w_gen = jnp.einsum("anh,adnp->dph", low_halves, table, preferred_element_type=F32)
    hidden_part = jnp.einsum("adnp,dph->anh", table, w_gen, preferred_element_type=F32)
    grad_hidden = small_sum_many(hidden_part.reshape(NB, HYP), "mp", 4, 1)
    grad_inner = hyper_pull(grad_hidden)[0]
    grad_w_hyper = jnp.dot(features.T, grad_inner, precision=highest)
    grad_b_hyper = jnp.sum(grad_inner, axis=0)
    return (
        output[None],
        grad_patches.T[None],
        grad_w_hyper,
        grad_b_hyper,
        grad_w_gen,
        smalls[4],
        smalls[8:16],
        smalls[0],
        smalls[1],
        attn[width : 4 * width].reshape(3, width, D),
        attn[:width],
        smalls[2],
        smalls[3],
        grad_w_up,
        smalls[6],
        grad_w_down,
        smalls[5],
    )


def solution(mesh):
    return jax.shard_map(
        functools.partial(local if mesh.shape["dp"] <= 8 else local_many, mesh.shape["dp"]),
        mesh=mesh,
        in_specs=(
            P("dp", None, None),
            P(),
            P(),
            P(),
            P("dp"),
            P("dp"),
            P("dp", None),
            P("dp", None),
            P(),
            P(),
            P("mp", None, None),
            P(),
            P(),
            P(),
            P(),
            P(None, "mp", None),
            P("mp", None),
            P(),
            P(),
            P(None, "mp"),
            P("mp"),
            P("mp", None),
            P(),
            P("dp", None, None),
        ),
        out_specs=(
            P("dp", None, None),
            P("dp", None, None),
            P(),
            P(),
            P("mp", None, None),
            P(),
            P(),
            P(),
            P(),
            P(None, "mp", None),
            P("mp", None),
            P(),
            P(),
            P(None, "mp"),
            P("mp"),
            P("mp", None),
            P(),
        ),
        check_vma=False,
    )
```

```python
import functools
import math

import jax
import jax.numpy as jnp
from jax import lax
from jax.experimental import pallas as pl
from jax.experimental.pallas import tpu as pltpu
from jax.sharding import PartitionSpec as P

F32 = jnp.float32
BF16 = jnp.bfloat16
MESH = pl.DeviceIdType.MESH

D = 768
HEAD_DIM = 64
PIX = 64
HYP = 128
BANDS = 13
NB = 32
SENSORS = 4
VIS_MAX = 256
SEQ = 258


def sinus_waves(wavelengths, width):
    half_width = width // 2
    steps = jnp.arange(half_width, dtype=jnp.float32)
    freqs = jnp.exp(steps * (6.0 * math.log(2.0) / half_width))
    angles = wavelengths[:, None] * freqs[None, :]
    return jnp.concatenate([jnp.sin(angles), jnp.cos(angles)], axis=1)


def grid_sines(visible, lengths, width, most):
    short_side = math.isqrt(most)
    long_side = 2 * short_side
    sides = jnp.where(lengths == most, long_side, short_side).astype(jnp.int32)[:, None]
    grid_rows = (visible // sides).astype(jnp.float32)
    grid_cols = (visible % sides).astype(jnp.float32)
    quarter = width // 4
    omegas = jnp.exp(jnp.arange(quarter, dtype=jnp.float32) * (-math.log(10000.0) / quarter))
    row_angle = grid_rows[..., None] * omegas
    col_angle = grid_cols[..., None] * omegas
    return [jnp.sin(row_angle), jnp.cos(row_angle), jnp.sin(col_angle), jnp.cos(col_angle)]


def grid_codes(visible, lengths, width, most):
    return jnp.concatenate(grid_sines(visible, lengths, width, most), axis=-1)


def gelu_exact(values):
    return jax.nn.gelu(values, approximate=False)


def remote(src, dst, send_sem, recv_sem, device):
    return pltpu.make_async_remote_copy(
        src_ref=src,
        dst_ref=dst,
        send_sem=send_sem,
        recv_sem=recv_sem,
        device_id=device,
        device_id_type=MESH,
    )


def greet(devices):
    barrier = pltpu.get_barrier_semaphore()
    for device in devices:
        pl.semaphore_signal(barrier, inc=1, device_id=device, device_id_type=MESH)
    pl.semaphore_wait(barrier, len(devices))


def mp_peers():
    place = lax.axis_index("mp")
    core = lax.rem(place, 2)
    return core, {"mp": place + 1 - 2 * core}, {"mp": lax.rem(place + 2, 4)}


class Sender:
    def __init__(self, sends, recvs):
        self.sends, self.recvs, self.copies = sends, recvs, []

    def go(self, number, src, dst, device):
        copy = remote(src, dst, self.sends.at[number], self.recvs.at[number], device)
        copy.start()
        self.copies.append(copy)
        return copy

    def finish(self):
        for copy in self.copies:
            copy.wait_send()


class MpSum(Sender):
    def __init__(self, part, slots, out, cuts, sends, recvs):
        super().__init__(sends, recvs)
        self.part, self.out, self.cuts = part, out, cuts
        self.pair_in, self.chip_sum, self.far_in, self.other_near, self.other_far = slots
        self.core, self.pair, self.far = mp_peers()
        self.first, self.second, self.third = {}, {}, {}

    def number(self, step, i):
        return step * len(self.cuts) + i

    def start(self, i):
        rows = pl.ds(*self.cuts[i])
        self.first[i] = self.go(
            self.number(0, i), self.part.at[1 - self.core, rows], self.pair_in.at[rows], self.pair
        )

    def relay(self, i):
        rows = pl.ds(*self.cuts[i])
        self.first[i].wait_recv()
        self.chip_sum[rows] = (
            self.part[self.core, rows].astype(F32) + self.pair_in[rows].astype(F32)
        ).astype(BF16)
        mine = self.chip_sum.at[rows]
        self.second[i] = (
            self.go(self.number(1, i), mine, self.far_in.at[rows], self.far),
            self.go(self.number(2, i), mine, self.other_near.at[rows], self.pair),
        )

    def forward(self, i):
        rows = pl.ds(*self.cuts[i])
        self.second[i][0].wait_recv()
        self.third[i] = self.go(
            self.number(3, i), self.far_in.at[rows], self.other_far.at[rows], self.pair
        )
        self.out[self.core, rows] = self.chip_sum[rows].astype(F32) + self.far_in[rows].astype(F32)

    def total(self, i):
        rows = pl.ds(*self.cuts[i])
        self.second[i][1].wait_recv()
        self.third[i].wait_recv()
        self.out[1 - self.core, rows] = self.other_near[rows].astype(F32) + self.other_far[
            rows
        ].astype(F32)


class DpPlace:
    def __init__(self, lines):
        place = lax.axis_index("dp")
        self.lines = lines
        self.inner = lax.rem(place, 2)
        self.outer = place // 2
        self.pair = {"dp": self.outer * 2 + 1 - self.inner}

    def peer(self, k):
        return {"dp": lax.rem(self.outer + k, self.lines) * 2 + self.inner}


class Chain:
    def __init__(self, place, sends, recvs):
        self.place, self.sends, self.recvs = place, sends, recvs
        self.ends = []
        self.low = place.outer < (place.lines + 1) // 2
        self.depth = jnp.where(self.low, place.outer, place.lines - 1 - place.outer)

    def copy(self, number, src, dst, device):
        return remote(src, dst, self.sends.at[number], self.recvs.at[number], device)

    def start(self, copy, cond=None):
        if cond is None:
            copy.start()
        else:
            pl.when(cond)(copy.start)
        self.ends.append((copy, cond))

    def next_to(self, up):
        place = self.place
        outer = jnp.where(up, place.outer + 1, place.outer - 1)
        outer = jnp.clip(outer, 0, place.lines - 1)
        return {"dp": outer * 2 + place.inner}

    def step(self):
        if self.steps:
            self.steps.pop(0)()

    def drain(self):
        while self.steps:
            self.step()

    def finish(self):
        for copy, cond in self.ends:
            if cond is None:
                copy.wait_send()
            else:
                pl.when(cond)(copy.wait_send)

    def hop(self, flow, i, outward):
        lines = self.place.lines
        up = self.low if outward else jnp.logical_not(self.low)
        way = jnp.where(up, 0, 1)
        chunk = jnp.where(up, lines - 1 - i, i)
        slot = flow.at[way, chunk]
        return slot, chunk, self.copy(way * lines + chunk, slot, slot, self.next_to(up))

    def out(self, own, flow):
        for i in range(self.place.lines - 1):
            slot, chunk, copy = self.hop(flow, i, True)

            @pl.when(self.depth == 0)
            def _(slot=slot, chunk=chunk):
                slot[...] = own[chunk]

            self.start(copy, self.depth == 0)

    def on(self, own, flow, i, outward):
        slot, chunk, copy = self.hop(flow, i, outward)
        inner = i < self.place.lines - 1 - self.depth if outward else i < self.depth
        active = jnp.logical_and(self.depth > 0, inner)

        @pl.when(active)
        def _():
            copy.wait_recv()
            slot[...] = (slot[...].astype(F32) + own[chunk].astype(F32)).astype(BF16)

        self.start(copy, active)

    def sum_steps(self, own, flow):
        lines = self.place.lines
        steps = [functools.partial(self.out, own, flow)]
        for i in range(lines - 2):
            steps.append(functools.partial(self.on, own, flow, i, True))
            if i < (lines + 1) // 2 - 1:
                steps.append(functools.partial(self.on, own, flow, i, False))
        return steps

    def sum_end(self, own, flow, total):
        lines, z = self.place.lines, self.place.outer
        total[...] = own[z].astype(F32)
        for way, cond in ((0, z > 0), (1, z < lines - 1)):
            slot = flow.at[way, z]
            copy = self.copy(way * lines + z, slot, slot, self.next_to(z > 0))

            @pl.when(cond)
            def _(slot=slot, copy=copy):
                copy.wait_recv()
                total[...] += slot[...].astype(F32)

    def spread_start(self, whole, base):
        lines, z = self.place.lines, self.place.outer
        mine = whole.at[z]
        self.start(self.copy(base + z, mine, mine, self.next_to(True)), z < lines - 1)
        self.start(self.copy(base + z, mine, mine, self.next_to(False)), z > 0)

    def spread_step(self, whole, base, r, then=None):
        lines, z = self.place.lines, self.place.outer
        for up, chunk, cond, more in (
            (True, z - r, z - r >= 0, z < lines - 1),
            (False, z + r, z + r < lines, z > 0),
        ):
            chunk = jnp.clip(chunk, 0, lines - 1)
            slot = whole.at[chunk]
            copy = self.copy(base + chunk, slot, slot, self.next_to(up))
            pl.when(cond)(copy.wait_recv)
            self.start(copy, jnp.logical_and(cond, more))
            if then is not None:
                then(chunk, slot, cond)


class PairFirst(Chain):
    def __init__(self, place, grad, scratch, whole, sends, recvs):
        super().__init__(place, sends, recvs)
        self.grad, self.whole = grad, whole.at[place.inner]
        self.pair_in, self.half, self.flow, self.total = scratch
        lines = place.lines
        steps = [self.pair_start, self.pair_end] + self.sum_steps(self.half, self.flow)
        steps.append(self.line_end)
        for r in range(1, lines):
            steps.append(functools.partial(self.spread_step, self.whole, 2 * lines, r, self.to_pair))
        steps.append(self.end)
        self.steps = steps

    def pair_start(self):
        place = self.place
        copy = self.copy(4 * place.lines, self.grad.at[1 - place.inner], self.pair_in, place.pair)
        self.first = copy
        self.start(copy)

    def pair_end(self):
        self.first.wait_recv()
        for z in range(self.place.lines):
            self.half[z] = (
                self.grad[self.place.inner, z].astype(F32) + self.pair_in[z].astype(F32)
            ).astype(BF16)

    def to_pair(self, chunk, slot, cond=None):
        self.start(self.copy(3 * self.place.lines + chunk, slot, slot, self.place.pair), cond)

    def line_end(self):
        z = self.place.outer
        self.sum_end(self.half, self.flow, self.total)
        self.whole[z] = self.total[...].astype(BF16)
        self.spread_start(self.whole, 2 * self.place.lines)
        self.to_pair(z, self.whole.at[z])

    def end(self):
        for z in range(self.place.lines):
            slot = self.whole.at[z]
            self.copy(3 * self.place.lines + z, slot, slot, self.place.pair).wait_recv()
        self.finish()


class LineFirst(Chain):
    def __init__(self, place, grad, scratch, whole, sends, recvs):
        super().__init__(place, sends, recvs)
        self.grad, self.whole = grad, whole
        self.flow, self.total, self.mine, self.pair_in = scratch
        lines = place.lines
        steps = self.sum_steps(self.grad, self.flow)
        steps += [self.pair_start, self.pair_end]
        for r in range(1, lines):
            steps.append(functools.partial(self.spread_step, self.whole, 2 * lines, r))
        steps.append(self.finish)
        self.steps = steps

    def pair_start(self):
        self.sum_end(self.grad, self.flow, self.total)
        self.mine[...] = self.total[...].astype(BF16)
        copy = self.copy(4 * self.place.lines, self.mine, self.pair_in, self.place.pair)
        self.first = copy
        self.start(copy)

    def pair_end(self):
        self.first.wait_recv()
        self.whole[self.place.outer] = (
            self.mine[...].astype(F32) + self.pair_in[...].astype(F32)
        ).astype(BF16)
        self.spread_start(self.whole, 2 * self.place.lines)


class LineGather(Chain):
    def __init__(self, place, bank, sends, recvs, share=None):
        super().__init__(place, sends, recvs)
        self.bank, self.share = bank, share
        lines = place.lines
        self.mine = bank.at[place.inner]
        steps = [self.begin]
        for r in range(1, lines):
            steps.append(functools.partial(self.spread_step, self.mine, 0, r, self.hand_on))
        self.steps = steps + [self.from_pair, self.end]

    def hand_on(self, chunk, slot, cond=None):
        lines = self.place.lines
        self.start(self.copy(lines + chunk, slot, slot, self.place.pair), cond)
        self.to_core(self.place.inner * lines + chunk, slot, cond)

    def to_core(self, number, slot, cond=None):
        if self.share is not None:
            device, sends, recvs = self.share[:3]
            self.start(remote(slot, slot, sends.at[number], recvs.at[number], device), cond)

    def begin(self):
        z = self.place.outer
        self.spread_start(self.mine, 0)
        self.hand_on(z, self.mine.at[z])

    def from_pair(self):
        lines, other = self.place.lines, 1 - self.place.inner
        for z in range(lines):
            slot = self.bank.at[other, z]
            self.copy(lines + z, slot, slot, self.place.pair).wait_recv()
            self.to_core(other * lines + z, slot)

    def end(self):
        if self.share is not None:
            device, sends, recvs, there = self.share
            for i in range(2):
                for z in range(self.place.lines):
                    number, slot = i * self.place.lines + z, there.at[i, z]
                    remote(slot, slot, sends.at[number], recvs.at[number], device).wait_recv()
        self.finish()


class SmallSum(Sender):
    def __init__(self, place, part, pair_in, line_in, out, sends, recvs):
        super().__init__(sends, recvs)
        self.place, self.part, self.pair_in, self.line_in, self.out = place, part, pair_in, line_in, out

    def start(self):
        self.first = self.go(0, self.part, self.pair_in, self.place.pair)

    def relay(self):
        place, lines = self.place, self.place.lines
        self.first.wait_recv()
        self.line_in[place.outer] = self.part[...] + self.pair_in[...]
        mine = self.line_in.at[place.outer]
        self.second = [self.go(k, mine, mine, place.peer(k)) for k in range(1, lines)]

    def total(self):
        for copy in self.second:
            copy.wait_recv()
        total = self.line_in[0]
        for z in range(1, self.place.lines):
            total = total + self.line_in[z]
        self.out[...] = total
        self.finish()


class MpSmall(Sender):
    def __init__(self, part, slots, out, sends, recvs):
        super().__init__(sends, recvs)
        self.part, self.slots, self.out = part, slots, out
        core, pair, far = mp_peers()
        self.peers = [pair, far, {"mp": far["mp"] + 1 - 2 * core}]

    def begin(self):
        me = lax.axis_index("mp")
        self.slots[me] = self.part[...]
        for k, peer in enumerate(self.peers):
            self.go(k, self.part, self.slots.at[me], peer)

    def total(self):
        for copy in self.copies:
            copy.wait_recv()
        total = self.slots[0]
        for k in range(1, 4):
            total = total + self.slots[k]
        self.out[...] = total


def dot(left, right):
    return jnp.dot(left, right, preferred_element_type=F32)


def dot_nt(left, right):
    return lax.dot_general(left, right, (((1,), (1,)), ((), ())), preferred_element_type=F32)


def dot_tn(left, right):
    return lax.dot_general(left, right, (((0,), (0,)), ((), ())), preferred_element_type=F32)


def row_mean(values):
    return jnp.mean(values, axis=-1, keepdims=True)


def col_sum(values):
    return jnp.sum(values, axis=0, keepdims=True)


ROWS = 272
CUTS = [(0, 64), (64, 64), (128, 64), (192, 80)]
GROUP = 8
SLOTS = 16
PIXEL_CUTS = [(0, 208), (208, 208)]


KINDS = (
    ("down0", LineFirst),
    ("down1", PairFirst),
    ("up0", PairFirst),
    ("up1", LineFirst),
    ("attn0", PairFirst),
    ("attn1", PairFirst),
)


def layer_kernel(
    lines,
    kinds,
    far_patches,
    hidden,
    far_w_gen,
    sines,
    row_parts,
    w_meta,
    meta,
    lengths,
    sensor,
    band_ids,
    band_mask,
    far_w_qkv,
    far_w_out,
    far_w_up,
    far_w_down,
    far_cotangent,
    far_output,
    far_grad_patches,
    smalls,
    hidden_grad,
    grad_gen,
    far_wholes,
    embeds,
    tokens,
    xhat_one,
    rstd_one,
    xhat_two,
    rstd_two,
    after,
    normed,
    normed_two,
    queries,
    keys,
    values,
    probs,
    mixed,
    grad_mixed,
    grad_qkv,
    branch_grad,
    gate_grad,
    activation,
    grad_pre,
    after_low,
    bank,
    embed_bank,
    spots,
    kern,
    picks,
    kern_grads,
    table,
    gen_out,
    hidden_part,
    hidden_slots,
    part_a,
    part_b,
    part_c,
    part_d,
    part_e,
    slots_a,
    slots_b,
    slots_c,
    slots_d,
    slots_e,
    out_a,
    out_b,
    out_c,
    out_d,
    out_e,
    grads,
    slots,
    small_part,
    small_pair,
    small_line,
    mp_sends,
    mp_recvs,
    dp_sends,
    dp_recvs,
    etc_sends,
    etc_recvs,
    share_sends,
    share_recvs,
    out_sem,
    patches,
    raw_gen,
    w_table,
    positions,
    rows_in,
    meta_col,
    live_row,
    live_col,
    select,
    w_qkv,
    w_out,
    w_up,
    w_down,
    cotangent,
    output,
    grad_patches,
    wholes,
    in_sems,
    end_sems,
):
    core, pair, far = mp_peers()
    place = DpPlace(lines)
    loads = {}
    gen_block = raw_gen.shape[1]
    moves = [(far_w_gen.at[pl.ds(k * gen_block, gen_block)], raw_gen.at[k]) for k in range(2)]
    moves += [
        (far_patches, patches),
        (far_cotangent, cotangent),
        (far_w_down, w_down),
        (far_w_qkv, w_qkv),
        (far_w_out, w_out),
        (far_w_up, w_up),
    ]
    moves += [(sines[k], positions.at[k]) for k in range(4)]
    for number, (src, dst) in enumerate(moves):
        loads[number] = pltpu.make_async_copy(src, dst, in_sems.at[number])
        loads[number].start()

    def need(number):
        if number in loads:
            loads.pop(number).wait()

    for k, part in enumerate(row_parts[:6]):
        rows_in[k : k + 1] = part[...].reshape(1, D)
    meta_row = meta[0, 0] * w_meta[0:1]
    for k in range(1, w_meta.shape[0]):
        meta_row = meta_row + meta[0, k] * w_meta[k : k + 1]
    rows_in[6:7] = meta_row
    meta_at = lax.broadcasted_iota(jnp.int32, meta_col.shape, 0)
    meta_values = jnp.zeros(meta_col.shape, F32)
    for k in range(w_meta.shape[0]):
        meta_values = jnp.where(meta_at == k, meta[0, k], meta_values)
    meta_col[...] = meta_values
    for live in (live_row, live_col):
        at = lax.broadcasted_iota(jnp.int32, live.shape, 0 if live is live_col else 1)
        live[...] = ((at < lengths[0]) | ((at >= 256) & (at < SEQ))).astype(F32)
    slot_at = lax.broadcasted_iota(jnp.int32, select.shape, 0)
    band_at = lax.broadcasted_iota(jnp.int32, select.shape, 1)
    picked = jnp.zeros(select.shape, F32)
    for b in range(BANDS):
        on = (slot_at == b) & (band_at == band_ids[sensor[0], b])
        picked = jnp.where(on, band_mask[sensor[0], b].astype(F32), picked)
    select[...] = picked.astype(BF16)
    b_up = row_parts[6]

    stores = []

    def keep(src, dst):
        stores.append(pltpu.make_async_copy(src, dst, end_sems.at[len(stores)]))
        stores[-1].start()

    cross = {"mp": far["mp"] + 1 - 2 * core}
    greet([pair, far, cross, place.pair] + [place.peer(k) for k in range(1, lines)])
    me = lax.axis_index("mp")
    width = w_out.shape[0]
    heads = width // HEAD_DIM
    full = D

    def mp_sum(part, slots, out, cuts, number):
        return MpSum(
            part,
            [slots.at[k] for k in range(5)],
            out,
            cuts,
            mp_sends.at[number],
            mp_recvs.at[number],
        )

    sum_a = mp_sum(part_a, slots_a, out_a, CUTS, 0)
    sum_b = mp_sum(part_b, slots_b, out_b, CUTS, 1)
    sum_c = mp_sum(part_c, slots_c, out_c, CUTS, 2)
    sum_d = mp_sum(part_d, slots_d, out_d, CUTS, 3)
    sum_e = mp_sum(part_e, slots_e, out_e, PIXEL_CUTS, 4)

    pieces = []
    for number, (name, kind) in enumerate(kinds):
        pieces.append(
            kind(
                place,
                grads[number],
                slots[number],
                wholes[number],
                dp_sends.at[number],
                dp_recvs.at[number],
            )
        )
    count = len(kinds)
    early = LineGather(
        place,
        bank.at[core],
        dp_sends.at[count + 1],
        dp_recvs.at[count + 1],
        (pair, share_sends, share_recvs, bank.at[1 - core]),
    )
    late = LineGather(place, embed_bank, dp_sends.at[count + 2], dp_recvs.at[count + 2])
    hidden_sum = MpSmall(hidden_part, hidden_slots, hidden_grad, etc_sends.at[pl.ds(3, 3)], etc_recvs.at[pl.ds(3, 3)])
    small = SmallSum(place, small_part, small_pair, small_line, smalls, dp_sends.at[len(kinds)], dp_recvs.at[len(kinds)])

    def put_piece(grad, first_row, block):
        rows = grad.shape[-2]
        for k in range(0, block.shape[0], rows):
            chunk = (first_row + k) // rows
            spot = (chunk,) if len(grad.shape) == 3 else (chunk // lines, chunk % lines)
            grad[spot] = block[k : k + rows].astype(BF16)

    gain_one, shift_one = rows_in[0:1], rows_in[1:2]
    gain_two, shift_two = rows_in[2:3], rows_in[3:4]
    b_down = rows_in[4:5]
    lane_head = lax.broadcasted_iota(jnp.int32, (1, width), 1) // HEAD_DIM
    head_masks = [(lane_head == h).astype(F32).astype(BF16) for h in range(heads)]

    grad_after, grad_tokens = gate_grad, tokens
    etc = Sender(etc_sends, etc_recvs)
    kept = {}

    def iota(rows, lanes, dim):
        return lax.broadcasted_iota(jnp.int32, (rows, lanes), dim)

    def blocks(block, rows, lanes):
        tall = jnp.concatenate([block] * GROUP, axis=0)
        wide = jnp.concatenate([tall] * GROUP, axis=1)
        on = iota(*wide.shape, 0) // rows == iota(*wide.shape, 1) // lanes
        return jnp.where(on, wide.astype(F32), 0.0).astype(BF16)

    pixels = BANDS * PIX
    part_rows = PIX // GROUP // 2
    group_rows = GROUP * SLOTS

    def relay_gen():
        stage = gen_out.reshape(gen_block * PIX, HYP)
        for i in range(width // gen_block):
            need(i) if i < 2 else kept["gen"].pop(0).wait()
            stage[...] = raw_gen[i % 2].reshape(gen_block * PIX, HYP).astype(F32)
            if i + 2 < width // gen_block:
                copy = pltpu.make_async_copy(
                    far_w_gen.at[pl.ds((i + 2) * gen_block, gen_block)], raw_gen.at[i % 2], in_sems.at[i % 2]
                )
                copy.start()
                kept.setdefault("gen", []).append(copy)
            for p in range(PIX):
                w_table[i * gen_block : (i + 1) * gen_block, p * HYP : (p + 1) * HYP] = stage[
                    pl.ds(p, gen_block, stride=PIX), :
                ].astype(BF16)

    def w_group(g):
        return w_table[:, g * GROUP * HYP : (g + 1) * GROUP * HYP]

    def make_kern():
        relay_gen()
        row, col = iota(PIX * SLOTS, pixels, 0), iota(PIX * SLOTS, pixels, 1)
        want = lax.rem(row, SLOTS) * PIX + row // SLOTS
        spots[...] = (col == want).astype(F32).astype(BF16)
        chosen = dot(select[...], hidden[...]).astype(BF16)
        wide = blocks(chosen, SLOTS, HYP)
        for g in range(PIX // GROUP):
            kern_grads[g, 0:group_rows] = dot_nt(wide, w_group(g)).astype(BF16)
        rows = jnp.concatenate([kern_grads[g, 0:group_rows] for g in range(PIX // GROUP)], axis=0)
        kern[...] = dot_tn(spots[...], rows).astype(BF16)

    def fill_bank():
        need(2)
        half_rows = PIX * SLOTS // 2
        for c in range(2):

            @pl.when(core == c)
            def _():
                rows = dot(spots[c * half_rows : (c + 1) * half_rows], patches[...])
                bank[c, place.inner, place.outer, 0:half_rows] = rows.astype(BF16)
                bank[c, place.inner, place.outer, half_rows : half_rows + SLOTS, 0:128] = jnp.concatenate(
                    [select[...].astype(F32), jnp.zeros((SLOTS, 128 - NB), F32)], axis=1
                ).astype(BF16)
                bank[c, place.inner, place.outer, half_rows : half_rows + SLOTS, 128:256] = jnp.zeros(
                    (SLOTS, 128), BF16
                )

    def make_picks():
        half_rows = PIX * SLOTS // 2
        for c in range(2 * lines):
            mine = bank[0, c // lines, c % lines, half_rows : half_rows + SLOTS, 0:128]
            picks[c * group_rows : (c + 1) * group_rows] = blocks(mine[:, 0:NB], SLOTS, NB)

    def kern_grad(c):
        block = embed_bank[c // lines, c % lines]
        for h in range(2):
            rows = dot(bank[h, c // lines, c % lines, 0 : PIX * SLOTS // 2], block).astype(BF16)
            for k in range(part_rows):
                kern_grads[h * part_rows + k, c * group_rows : (c + 1) * group_rows] = rows[
                    k * group_rows : (k + 1) * group_rows
                ]

    def kern_grad_half(i):
        for c in range(i * lines, (i + 1) * lines):
            kern_grad(c)

    def table_part(g):
        got = dot_tn(kern_grads[g], picks[...]).astype(BF16)
        table[g * width : (g + 1) * width] = got
        grads_g = dot(got, kept["hidden"])
        if g >= 2:
            kept[g - 2].wait()
        for k in range(GROUP):
            gen_out[g % 2, pl.ds(k, width, stride=GROUP), :] = grads_g[:, k * HYP : (k + 1) * HYP]
        kept[g] = pltpu.make_async_copy(
            gen_out.at[g % 2].reshape(width, GROUP, HYP),
            grad_gen.at[:, pl.ds(g * GROUP, GROUP), :],
            out_sem.at[g % 2],
        )
        kept[g].start()

    def table_start():
        kept["hidden"] = blocks(hidden[...], NB, HYP)

    def hidden_grads():
        flat = jnp.concatenate([w_group(g) for g in range(PIX // GROUP)], axis=0)
        every = dot_tn(table[...], flat)
        total = every[0:NB, 0:HYP]
        for k in range(1, GROUP):
            total = total + every[k * NB : (k + 1) * NB, k * HYP : (k + 1) * HYP]
        hidden_part[...] = total

    def embed():
        need(2)
        embeds[me] = dot_tn(patches[...], kern[...]).astype(BF16)
        mine = embeds.at[me]
        kept["pair"] = etc.go(0, mine, mine, pair)
        kept["far"] = etc.go(1, mine, mine, far)

    def epass():
        kept["far"].wait_recv()
        got = embeds.at[lax.rem(me + 2, 4)]
        kept["passed"] = etc.go(2, got, got, pair)

    def fillgate():
        need(3)
        need(4)
        branch_grad[0:256] = (live_col[0:256] * cotangent[2:258]).astype(BF16)
        branch_grad[256:272] = jnp.concatenate(
            [cotangent[0:2], jnp.zeros((14, full), F32)], axis=0
        ).astype(BF16)
        small_part[...] = jnp.zeros_like(small_part)
        small_part[5:6] = col_sum(branch_grad[...].astype(F32))
        gate_grad[...] = dot_nt(branch_grad[...], w_down[...])

    def tokens_norm():
        for k in range(4):
            need(8 + k)
        kept["pair"].wait_recv()
        kept["passed"].wait_recv()
        for lo, n in CUTS:
            hi = min(lo + n, 256)
            for i in range(4):
                cols = slice(i * width, (i + 1) * width)
                tokens[lo:hi, cols] = embeds[i, lo:hi].astype(F32) + positions[i, lo:hi]
            if lo + n > 256:
                tokens[256:272] = jnp.concatenate([rows_in[5:7], jnp.zeros((14, full), F32)], axis=0)
            rows = slice(lo, lo + n)
            x = tokens[rows]
            centred = x - row_mean(x)
            rstd = lax.rsqrt(row_mean(centred * centred) + 1e-05)
            rstd_one[rows] = rstd
            xhat = centred * rstd
            xhat_one[rows] = xhat
            normed[rows] = (xhat * gain_one + shift_one).astype(BF16)

    def attention():
        need(5)
        queries[...] = dot_nt(normed[...], w_qkv[0]).astype(BF16)
        keys[...] = dot_nt(normed[...], w_qkv[1]).astype(BF16)
        values[...] = dot_nt(normed[...], w_qkv[2]).astype(BF16)
        live_keys = live_row[...] > 0
        total = None
        for h in range(heads):
            raw = dot_nt(queries[...] * head_masks[h], keys[...]) * 0.125
            raw = jnp.where(live_keys, raw, -1000000000.0)
            expo = jnp.exp(raw - jnp.max(raw, axis=-1, keepdims=True))
            prob = expo / jnp.sum(expo, axis=-1, keepdims=True)
            probs[h] = prob
            term = dot(prob.astype(BF16), values[...] * head_masks[h])
            total = term if total is None else total + term
        mixed[...] = total.astype(BF16)

    def put_part(part, rows, block):
        half = block.shape[1] // 2
        part[0, rows] = block[:, :half].astype(BF16)
        part[1, rows] = block[:, half:].astype(BF16)

    def get_out(out, rows):
        return jnp.concatenate([out[0, rows], out[1, rows]], axis=1)

    def span(i):
        lo, n = CUTS[i]
        return slice(lo, lo + n)

    def attn_part(i):
        need(6)
        put_part(part_a, span(i), dot(mixed[span(i)], w_out[...]))

    def feedforward(i):
        need(7)
        rows = span(i)
        x = tokens[rows] + get_out(out_a, rows)
        after[rows] = x
        centred = x - row_mean(x)
        rstd = lax.rsqrt(row_mean(centred * centred) + 1e-05)
        rstd_two[rows] = rstd
        xhat = centred * rstd
        xhat_two[rows] = xhat
        normed_two[rows] = (xhat * gain_two + shift_two).astype(BF16)
        gate = dot(normed_two[rows], w_up[...]) + b_up[...].reshape(1, width * 4)
        cdf = 0.5 + 0.5 * lax.erf(gate * (2.0**-0.5))
        activation[rows] = (gate * cdf).astype(BF16)
        pdf = jnp.exp(-0.5 * gate * gate) * ((2.0 * math.pi) ** -0.5)
        grad_pre[rows] = (gate_grad[rows] * (cdf + gate * pdf)).astype(BF16)
        put_part(part_c, rows, dot_nt(grad_pre[rows], w_up[...]))

    half = full // 2

    def grad_of_down(j):
        cols = slice(j * half, (j + 1) * half)
        put_piece(pieces[j].grad, 0, dot_tn(activation[...], branch_grad[:, cols]))

    def grad_of_up(j):
        cols = slice(j * half, (j + 1) * half)
        put_piece(pieces[2 + j].grad, 0, dot_tn(normed_two[...], grad_pre[:, cols]))
        if j == 1:
            small_part[6:7] = col_sum(grad_pre[...].astype(F32))

    def norm_two_back(i):
        rows = span(i)
        lo, n = CUTS[i]
        dy = get_out(out_c, rows)
        xhat = xhat_two[rows]
        small_part[2:3] += col_sum(dy * xhat)
        small_part[3:4] += col_sum(dy)
        e = dy * gain_two
        dx = rstd_two[rows] * (e - row_mean(e) - xhat * row_mean(e * xhat))
        if lo + n <= 256:
            grad_out = live_col[rows] * cotangent[lo + 2 : lo + n + 2]
        else:
            grad_out = jnp.concatenate(
                [live_col[lo:256] * cotangent[lo + 2 : 258], cotangent[0:2], jnp.zeros((14, full), F32)],
                axis=0,
            )
        grad_x = dx + grad_out
        grad_after[rows] = grad_x
        after_low[rows] = grad_x.astype(BF16)

    def mixed_back():
        grad_mixed[...] = dot_nt(after_low[...], w_out[...]).astype(BF16)
        kept["parts"] = [None, None, None]

    def head_back(h):
        mixed_h = grad_mixed[...] * head_masks[h]
        grad_probs = dot_nt(mixed_h, values[...])
        prob = probs[h]
        scores = prob * (grad_probs - jnp.sum(grad_probs * prob, axis=-1, keepdims=True))
        scores = scores.astype(BF16)
        terms = [
            dot(scores, keys[...] * head_masks[h]),
            dot_tn(scores, queries[...] * head_masks[h]),
            dot_tn(prob.astype(BF16), mixed_h),
        ]
        kept["parts"] = [t if p is None else p + t for p, t in zip(kept["parts"], terms)]
        if h == heads - 1:
            for t, scale in enumerate((0.125, 0.125, 1.0)):
                grad_qkv[t] = (kept["parts"][t] * scale).astype(BF16)

    def norm_part(i):
        rows = span(i)
        block = dot(grad_qkv[0, rows], w_qkv[0])
        block = block + dot(grad_qkv[1, rows], w_qkv[1])
        put_part(part_d, rows, block + dot(grad_qkv[2, rows], w_qkv[2]))

    def grad_of_attn(j):
        cols = slice(j * half, (j + 1) * half)
        grad = pieces[4 + j].grad
        put_piece(grad, 0, dot_tn(mixed[...], after_low[:, cols]))
        for t in range(3):
            put_piece(grad, (t + 1) * width, dot_tn(grad_qkv[t], normed[:, cols]))

    def norm_one_back(i):
        rows = span(i)
        dy = get_out(out_d, rows)
        xhat = xhat_one[rows]
        small_part[0:1] += col_sum(dy * xhat)
        small_part[1:2] += col_sum(dy)
        e = dy * gain_one
        dx = rstd_one[rows] * (e - row_mean(e) - xhat * row_mean(e * xhat))
        grad_tokens[rows] = grad_after[rows] + dx

    def embed_grads():
        for i in range(4):

            @pl.when(me == i)
            def _():
                embed_bank[place.inner, place.outer] = grad_tokens[0:256, i * width : (i + 1) * width].astype(BF16)

    def small_ready():
        small_part[4:5] = grad_tokens[256:257]
        small_part[8:16] = meta_col[...] * grad_tokens[257:258]

    def pixel_part():
        pixels = dot_nt(kern[...], embed_bank[place.inner, place.outer]).astype(BF16)
        part_e[0] = pixels[: BANDS * PIX // 2]
        part_e[1] = pixels[BANDS * PIX // 2 :]

    def branch_part():
        need(4)
        for i in range(len(CUTS)):
            put_part(part_b, span(i), dot(activation[span(i)], w_down[...]))

    def final_output():
        for i, (lo, n) in enumerate(CUTS):
            rows = span(i)
            x = after[rows] + get_out(out_b, rows) + b_down
            if lo + n <= 256:
                output[lo + 2 : lo + n + 2] = live_col[rows] * x
            else:
                output[lo + 2 : 258] = live_col[lo:256] * x[: 256 - lo]
                output[0:2] = x[256 - lo : 258 - lo]
        keep(output, far_output)

    def final_pixels():
        grad_patches[: BANDS * PIX // 2] = out_e[0]
        grad_patches[BANDS * PIX // 2 :] = out_e[1]
        keep(grad_patches, far_grad_patches)

    down0, down1, up0, up1, attn0, attn1 = pieces
    order = [
        make_kern,
        embed,
        fill_bank,
        early.step,
        epass,
        tokens_norm,
        attention,
        (attn_part, 0),
        (sum_a.start, 0),
        (attn_part, 3),
        (sum_a.start, 3),
        (attn_part, 2),
        early.step,
        (attn_part, 1),
        (sum_a.relay, 0),
        (sum_a.start, 1),
        fillgate,
        (sum_a.relay, 3),
        (sum_a.start, 2),
        (sum_a.relay, 1),
        (sum_a.relay, 2),
        (sum_a.forward, 0),
        (sum_a.total, 0),
        (sum_a.forward, 3),
        (feedforward, 0),
        (sum_c.start, 0),
        (sum_a.forward, 1),
        (sum_a.total, 3),
        (feedforward, 3),
        (sum_c.start, 3),
        (sum_a.forward, 2),
        (sum_c.relay, 0),
        (sum_a.total, 1),
        (feedforward, 1),
        (sum_c.start, 1),
        (sum_c.relay, 3),
        (sum_a.total, 2),
        (feedforward, 2),
        (grad_of_up, 1),
        up1.step,
        (sum_c.start, 2),
        (sum_c.relay, 1),
        (grad_of_up, 0),
        (sum_c.forward, 0),
        up0.step,
        (grad_of_down, 1),
        (sum_c.relay, 2),
        branch_part,
        (sum_c.forward, 3),
        (sum_c.forward, 1),
        down1.step,
        up1.step,
        (sum_c.forward, 2),
        (sum_c.total, 3),
        (sum_c.total, 0),
        (grad_of_down, 0),
        (sum_c.total, 1),
        (norm_two_back, 0),
        (norm_two_back, 1),
        (sum_c.total, 2),
        (norm_two_back, 2),
        (norm_two_back, 3),
        mixed_back,
        early.step,
        (head_back, 0),
        (head_back, 1),
        (head_back, 2),
        (norm_part, 2),
        (sum_b.start, 3),
        up0.step,
        up0.step,
        (norm_part, 0),
        (norm_part, 3),
        (sum_d.start, 2),
        up1.step,
        (sum_d.start, 0),
        (sum_b.relay, 3),
        (sum_b.start, 1),
        (sum_d.relay, 2),
        (sum_d.start, 3),
        (norm_part, 1),
        (sum_d.start, 1),
        (grad_of_attn, 0),
        down0.step,
        up0.step,
        up1.step,
        (sum_d.relay, 3),
        (sum_d.forward, 2),
        (sum_d.relay, 0),
        (sum_d.total, 2),
        up0.step,
        up0.step,
        (sum_d.relay, 1),
        (grad_of_attn, 1),
        attn0.step,
        (sum_b.relay, 1),
        down0.step,
        (sum_d.forward, 3),
        attn1.step,
        (sum_d.forward, 0),
        (sum_d.forward, 1),
        (sum_d.total, 3),
        (sum_d.total, 0),
        up1.step,
        (norm_one_back, 0),
        (norm_one_back, 3),
        early.step,
        (sum_d.total, 1),
        (norm_one_back, 2),
        (sum_b.start, 0),
        (sum_b.forward, 1),
        (norm_one_back, 1),
        embed_grads,
        down1.step,
        (sum_b.forward, 3),
        late.step,
        pixel_part,
        down1.step,
        small_ready,
        up0.step,
        (sum_b.start, 2),
        (sum_b.total, 1),
        (sum_e.start, 1),
        down0.step,
        down0.step,
        attn0.step,
        attn0.step,
        small.start,
        down1.step,
        late.step,
        down1.step,
        table_start,
        down1.step,
        up0.step,
        late.step,
        (sum_e.relay, 1),
        (sum_b.relay, 2),
        attn0.step,
        down1.step,
        (sum_e.start, 0),
        attn1.step,
        (sum_b.total, 3),
        up1.step,
        (sum_b.relay, 0),
        late.step,
        attn0.step,
        attn0.step,
        down0.step,
        attn1.step,
        down1.step,
        attn1.step,
        attn0.step,
        up0.step,
        (sum_e.relay, 0),
        early.step,
        attn1.step,
        small.relay,
        early.drain,
        attn0.step,
        late.step,
        late.drain,
        (sum_b.forward, 0),
        (sum_b.forward, 2),
        make_picks,
        (kern_grad_half, 0),
        (kern_grad_half, 1),
        (sum_b.total, 0),
        attn1.step,
        up1.step,
        (sum_e.forward, 1),
        (table_part, 0),
        attn1.step,
        (table_part, 1),
        (table_part, 2),
        down0.step,
        up1.step,
        (table_part, 3),
        down1.step,
        (table_part, 4),
        attn1.step,
        (sum_e.forward, 0),
        up0.step,
        down1.step,
        (table_part, 5),
        (sum_b.total, 2),
        final_output,
        up0.step,
        (table_part, 6),
        attn0.step,
        attn1.step,
        (table_part, 7),
        hidden_grads,
        (sum_e.total, 0),
        (sum_e.total, 1),
        down0.step,
        small.total,
        attn1.step,
        up1.step,
        attn0.step,
        up1.step,
        final_pixels,
        down1.step,
        hidden_sum.begin,
        down0.step,
        attn1.step,
        hidden_sum.total,
        attn0.step,
        down0.step,
        down0.step,
    ]
    def send_out(number):
        whole = wholes[number]
        if number < 4:
            keep(whole, far_wholes[number])
        else:
            flat = whole if len(whole.shape) == 3 else whole.reshape(2 * lines, *whole.shape[2:])
            first = width // whole.shape[-2]
            keep(flat.at[pl.ds(0, first)], far_wholes[number])
            keep(flat.at[pl.ds(first, flat.shape[0] - first)], far_wholes[number + 2])

    for number, piece in enumerate(pieces):
        piece.steps.append(functools.partial(send_out, number))
    for item in order:
        if isinstance(item, tuple):
            item[0](*item[1:])
        else:
            item()
    for piece in pieces:
        piece.drain()
    for copy in stores:
        copy.wait()
    for g in range(PIX // GROUP - 2, PIX // GROUP):
        kept[g].wait()
    for one in (sum_a, sum_b, sum_c, sum_d, sum_e, etc, hidden_sum):
        one.finish()


def layer(dp_count, width, operands):
    lines = dp_count // 2

    def piece(rows, lanes, parts):
        chunk = -(-rows // parts)
        chunk = -(-chunk // 16) * 16
        if parts == lines:
            return (lines, chunk, lanes)
        return (2, lines, chunk, lanes)

    pieces = []
    for name, kind in KINDS:
        parts = dp_count if kind is PairFirst else lines
        pieces.append(piece(4 * width, D // 2, parts))

    splits = []
    for count in (1, 3):
        for shape in pieces[4:]:
            splits.append((count * width // shape[-2], *shape[-2:]))

    def piece_scratch(shape):
        if len(shape) == 4:
            return [low(*shape[1:]), low(*shape[1:]), low(2, *shape[1:]), vmem(*shape[2:])]
        return [low(2, *shape), vmem(*shape[1:]), low(*shape[1:]), low(*shape[1:])]

    half = D // 2
    pixel_lanes = BANDS * PIX

    def vmem(*shape, dtype=F32):
        return pltpu.VMEM(shape, dtype)

    def low(*shape):
        return pltpu.VMEM(shape, BF16)

    scratch = [
        low(4, 256, width),
        vmem(ROWS, D),
        vmem(ROWS, D),
        vmem(ROWS, 1),
        vmem(ROWS, D),
        vmem(ROWS, 1),
        vmem(ROWS, D),
        low(ROWS, D),
        low(ROWS, D),
        low(ROWS, width),
        low(ROWS, width),
        low(ROWS, width),
        vmem(width // HEAD_DIM, ROWS, ROWS),
        low(ROWS, width),
        low(ROWS, width),
        low(3, ROWS, width),
        low(ROWS, D),
        vmem(ROWS, D),
        low(ROWS, D),
        low(ROWS, D),
        low(ROWS, D),
        low(2, 2, lines, PIX * SLOTS // 2 + SLOTS, 256),
        low(2, lines, 256, width),
        low(PIX * SLOTS, pixel_lanes),
        low(pixel_lanes, width),
        low(dp_count * GROUP * SLOTS, GROUP * NB),
        low(PIX // GROUP, dp_count * GROUP * SLOTS, width),
        low(PIX // GROUP * width, GROUP * NB),
        vmem(2, width * GROUP, HYP),
        vmem(NB, HYP),
        vmem(4, NB, HYP),
    ]
    scratch += [low(2, ROWS, half)] * 4 + [low(2, pixel_lanes // 2, 256)]
    scratch += [low(5, ROWS, half)] * 4 + [low(5, pixel_lanes // 2, 256)]
    scratch += [vmem(2, ROWS, half)] * 4 + [vmem(2, pixel_lanes // 2, 256)]
    scratch.append([low(*shape) for shape in pieces])
    scratch.append([piece_scratch(shape) for shape in pieces])
    scratch += [vmem(16, D), vmem(16, D), vmem(lines, 16, D)]
    dma = pltpu.SemaphoreType.DMA
    scratch += [dma((5, 16)), dma((5, 16)), dma((len(pieces) + 3, 4 * lines + 1)), dma((len(pieces) + 3, 4 * lines + 1)), dma((6,)), dma((6,))]
    scratch += [dma((dp_count,)), dma((dp_count,)), dma((2,))]
    far = pl.BlockSpec(memory_space=pl.ANY)
    ref = pl.BlockSpec(memory_space=pltpu.VMEM)
    smem = pl.BlockSpec(memory_space=pltpu.SMEM)
    specs = [far, ref, far, [far] * 4, [ref] * 7, ref, smem, smem, smem, smem, smem] + [far] * 5
    scratch += [low(*operands[0].shape), low(2, width // 4, PIX, HYP), low(width, PIX * HYP)]
    scratch += [vmem(4, 256, D // 4), vmem(8, D), vmem(8, 1), vmem(1, ROWS), vmem(ROWS, 1), low(SLOTS, NB)]
    scratch += [pltpu.VMEM(x.shape, x.dtype) for x in operands[11:]]
    scratch += [vmem(SEQ, D), vmem(pixel_lanes, 256), [low(*shape) for shape in pieces]]
    scratch += [dma((12,)), dma((len(pieces) + 4,))]
    shapes = [
        jax.ShapeDtypeStruct((SEQ, D), F32),
        jax.ShapeDtypeStruct((pixel_lanes, 256), F32),
        jax.ShapeDtypeStruct((16, D), F32),
        jax.ShapeDtypeStruct((NB, HYP), F32),
        jax.ShapeDtypeStruct((width, PIX, HYP), F32),
        [jax.ShapeDtypeStruct(shape, BF16) for shape in pieces[:4] + splits],
    ]
    output, grad_patches, smalls, hidden_grad, grad_gen, wholes = pl.pallas_call(
        functools.partial(layer_kernel, lines, KINDS),
        out_shape=shapes,
        in_specs=specs,
        out_specs=[far, far, ref, ref, far, [far] * (len(pieces) + 2)],
        scratch_shapes=scratch,
        compiler_params=pltpu.CompilerParams(
            collective_id=0, has_side_effects=True, vmem_limit_bytes=67_043_328
        ),
        name="layer",
    )(*operands)
    wholes = [out.reshape(-1, out.shape[-1]) for out in wholes]
    return output, grad_patches, smalls, hidden_grad, grad_gen, wholes


def local(
    dp_count,
    patches,
    wavelengths,
    band_ids,
    band_mask,
    sensor,
    lengths,
    visible,
    meta,
    w_hyper,
    b_hyper,
    w_gen,
    cls_token,
    w_meta,
    gain_one,
    shift_one,
    w_qkv,
    w_out,
    gain_two,
    shift_two,
    w_up,
    b_up,
    w_down,
    b_down,
    cotangent,
):
    highest = lax.Precision.HIGHEST
    width = w_gen.shape[0]
    features = sinus_waves(wavelengths, HYP)
    sines = [part[0] for part in grid_sines(visible, lengths, D, VIS_MAX)]
    hyper_pre = jnp.dot(features, w_hyper, precision=highest) + b_hyper
    hidden, hyper_pull = jax.vjp(gelu_exact, hyper_pre)
    hidden_low = hidden.astype(BF16)
    operands = (
        patches[0].T,
        hidden_low,
        w_gen,
        sines,
        [gain_one, shift_one, gain_two, shift_two, b_down, cls_token, b_up],
        w_meta,
        meta,
        lengths,
        sensor,
        band_ids,
        band_mask,
        w_qkv,
        w_out,
        w_up,
        w_down,
        cotangent[0],
    )
    output, grad_patches, smalls, grad_hidden, grad_w_gen, wholes = layer(dp_count, width, operands)

    grad_w_down, grad_w_up, grad_w_out, grad_w_qkv = [
        jnp.concatenate(wholes[k : k + 2], axis=1).astype(F32) for k in (0, 2, 4, 6)
    ]
    grad_inner = hyper_pull(grad_hidden)[0]
    grad_w_hyper = jnp.dot(features.T, grad_inner, precision=highest)
    grad_b_hyper = jnp.sum(grad_inner, axis=0)
    return (
        output[None],
        grad_patches.T[None],
        grad_w_hyper,
        grad_b_hyper,
        grad_w_gen,
        smalls[4],
        smalls[8:16],
        smalls[0],
        smalls[1],
        grad_w_qkv.reshape(3, width, D),
        grad_w_out,
        smalls[2],
        smalls[3],
        grad_w_up,
        smalls[6],
        grad_w_down,
        smalls[5],
    )


KINDS_MANY = (
    ("down0", PairFirst),
    ("down1", PairFirst),
    ("up0", PairFirst),
    ("up1", LineFirst),
    ("attn0", PairFirst),
    ("attn1", PairFirst),
    ("table0", PairFirst),
)


def layer_kernel_many(
    lines,
    kinds,
    patches,
    kern,
    positions,
    rows_in,
    meta_col,
    live_row,
    live_col,
    select,
    w_qkv,
    w_out,
    w_up,
    b_up,
    w_down,
    cotangent,
    output,
    grad_patches,
    smalls,
    wholes,
    embeds,
    tokens,
    xhat_one,
    rstd_one,
    xhat_two,
    rstd_two,
    after,
    normed,
    normed_two,
    queries,
    keys,
    values,
    probs,
    mixed,
    grad_mixed,
    grad_qkv,
    branch_grad,
    gate_grad,
    activation,
    grad_pre,
    grad_after,
    after_low,
    grad_tokens,
    embed_grad,
    spread,
    part_a,
    part_b,
    part_c,
    part_d,
    part_e,
    slots_a,
    slots_b,
    slots_c,
    slots_d,
    slots_e,
    out_a,
    out_b,
    out_c,
    out_d,
    out_e,
    grads,
    slots,
    small_part,
    small_pair,
    small_line,
    mp_sends,
    mp_recvs,
    dp_sends,
    dp_recvs,
    etc_sends,
    etc_recvs,
):
    core, pair, far = mp_peers()
    place = DpPlace(lines)
    greet([pair, far, place.pair] + [place.peer(k) for k in range(1, lines)])
    me = lax.axis_index("mp")
    width = w_out.shape[0]
    heads = width // HEAD_DIM
    full = D

    def mp_sum(part, slots, out, cuts, number):
        return MpSum(
            part,
            [slots.at[k] for k in range(5)],
            out,
            cuts,
            mp_sends.at[number],
            mp_recvs.at[number],
        )

    sum_a = mp_sum(part_a, slots_a, out_a, CUTS, 0)
    sum_b = mp_sum(part_b, slots_b, out_b, CUTS, 1)
    sum_c = mp_sum(part_c, slots_c, out_c, CUTS, 2)
    sum_d = mp_sum(part_d, slots_d, out_d, CUTS, 3)
    sum_e = mp_sum(part_e, slots_e, out_e, PIXEL_CUTS, 4)

    pieces = []
    for number, (name, kind) in enumerate(kinds):
        pieces.append(
            kind(
                place,
                grads[number],
                slots[number],
                wholes[number],
                dp_sends.at[number],
                dp_recvs.at[number],
            )
        )
    small = SmallSum(place, small_part, small_pair, small_line, smalls, dp_sends.at[len(kinds)], dp_recvs.at[len(kinds)])

    def put_piece(grad, first_row, block):
        rows = grad.shape[-2]
        for k in range(0, block.shape[0], rows):
            chunk = (first_row + k) // rows
            spot = (chunk,) if len(grad.shape) == 3 else (chunk // lines, chunk % lines)
            grad[spot] = block[k : k + rows].astype(BF16)

    gain_one, shift_one = rows_in[0:1], rows_in[1:2]
    gain_two, shift_two = rows_in[2:3], rows_in[3:4]
    b_down = rows_in[4:5]
    lane_head = lax.broadcasted_iota(jnp.int32, (1, width), 1) // HEAD_DIM
    head_masks = [(lane_head == h).astype(F32).astype(BF16) for h in range(heads)]

    etc = Sender(etc_sends, etc_recvs)
    kept = {}

    def embed():
        embeds[me] = dot_tn(patches[...], kern[...]).astype(BF16)
        mine = embeds.at[me]
        kept["pair"] = etc.go(0, mine, mine, pair)
        kept["far"] = etc.go(1, mine, mine, far)

    def epass():
        kept["far"].wait_recv()
        got = embeds.at[lax.rem(me + 2, 4)]
        kept["passed"] = etc.go(2, got, got, pair)

    def fillgate():
        branch_grad[0:256] = (live_col[0:256] * cotangent[2:258]).astype(BF16)
        branch_grad[256:272] = jnp.concatenate(
            [cotangent[0:2], jnp.zeros((14, full), F32)], axis=0
        ).astype(BF16)
        small_part[...] = jnp.zeros_like(small_part)
        small_part[5:6] = col_sum(branch_grad[...].astype(F32))
        gate_grad[...] = dot_nt(branch_grad[...], w_down[...])

    def tokens_norm():
        kept["pair"].wait_recv()
        kept["passed"].wait_recv()
        for lo, n in CUTS:
            hi = min(lo + n, 256)
            for i in range(4):
                cols = slice(i * width, (i + 1) * width)
                tokens[lo:hi, cols] = embeds[i, lo:hi].astype(F32)
            tokens[lo:hi] += positions[lo:hi]
            if lo + n > 256:
                tokens[256:272] = jnp.concatenate([rows_in[5:7], jnp.zeros((14, full), F32)], axis=0)
            rows = slice(lo, lo + n)
            x = tokens[rows]
            centred = x - row_mean(x)
            rstd = lax.rsqrt(row_mean(centred * centred) + 1e-05)
            rstd_one[rows] = rstd
            xhat = centred * rstd
            xhat_one[rows] = xhat
            normed[rows] = (xhat * gain_one + shift_one).astype(BF16)

    def attention():
        queries[...] = dot_nt(normed[...], w_qkv[0]).astype(BF16)
        keys[...] = dot_nt(normed[...], w_qkv[1]).astype(BF16)
        values[...] = dot_nt(normed[...], w_qkv[2]).astype(BF16)
        live_keys = live_row[...] > 0
        total = None
        for h in range(heads):
            raw = dot_nt(queries[...] * head_masks[h], keys[...]) * 0.125
            raw = jnp.where(live_keys, raw, -1000000000.0)
            expo = jnp.exp(raw - jnp.max(raw, axis=-1, keepdims=True))
            prob = expo / jnp.sum(expo, axis=-1, keepdims=True)
            probs[h] = prob
            term = dot(prob.astype(BF16), values[...] * head_masks[h])
            total = term if total is None else total + term
        mixed[...] = total.astype(BF16)

    def put_part(part, rows, block):
        half = block.shape[1] // 2
        part[0, rows] = block[:, :half].astype(BF16)
        part[1, rows] = block[:, half:].astype(BF16)

    def get_out(out, rows):
        return jnp.concatenate([out[0, rows], out[1, rows]], axis=1)

    def span(i):
        lo, n = CUTS[i]
        return slice(lo, lo + n)

    def attn_part(i):
        put_part(part_a, span(i), dot(mixed[span(i)], w_out[...]))

    def feedforward(i):
        rows = span(i)
        x = tokens[rows] + get_out(out_a, rows)
        after[rows] = x
        centred = x - row_mean(x)
        rstd = lax.rsqrt(row_mean(centred * centred) + 1e-05)
        rstd_two[rows] = rstd
        xhat = centred * rstd
        xhat_two[rows] = xhat
        normed_two[rows] = (xhat * gain_two + shift_two).astype(BF16)
        gate = dot(normed_two[rows], w_up[...]) + b_up[...]
        cdf = 0.5 + 0.5 * lax.erf(gate * (2.0**-0.5))
        activation[rows] = (gate * cdf).astype(BF16)
        pdf = jnp.exp(-0.5 * gate * gate) * ((2.0 * math.pi) ** -0.5)
        grad_pre[rows] = (gate_grad[rows] * (cdf + gate * pdf)).astype(BF16)
        put_part(part_c, rows, dot_nt(grad_pre[rows], w_up[...]))

    half = full // 2

    def grad_of_down(j):
        cols = slice(j * half, (j + 1) * half)
        put_piece(pieces[j].grad, 0, dot_tn(activation[...], branch_grad[:, cols]))

    def grad_of_up(j):
        cols = slice(j * half, (j + 1) * half)
        put_piece(pieces[2 + j].grad, 0, dot_tn(normed_two[...], grad_pre[:, cols]))
        if j == 1:
            small_part[6:7] = col_sum(grad_pre[...].astype(F32))

    def norm_two_back(i):
        rows = span(i)
        lo, n = CUTS[i]
        dy = get_out(out_c, rows)
        xhat = xhat_two[rows]
        small_part[2:3] += col_sum(dy * xhat)
        small_part[3:4] += col_sum(dy)
        e = dy * gain_two
        dx = rstd_two[rows] * (e - row_mean(e) - xhat * row_mean(e * xhat))
        if lo + n <= 256:
            grad_out = live_col[rows] * cotangent[lo + 2 : lo + n + 2]
        else:
            grad_out = jnp.concatenate(
                [live_col[lo:256] * cotangent[lo + 2 : 258], cotangent[0:2], jnp.zeros((14, full), F32)],
                axis=0,
            )
        grad_x = dx + grad_out
        grad_after[rows] = grad_x
        after_low[rows] = grad_x.astype(BF16)

    def mixed_back():
        grad_mixed[...] = dot_nt(after_low[...], w_out[...]).astype(BF16)
        kept["parts"] = [None, None, None]

    def head_back(h):
        mixed_h = grad_mixed[...] * head_masks[h]
        grad_probs = dot_nt(mixed_h, values[...])
        prob = probs[h]
        scores = prob * (grad_probs - jnp.sum(grad_probs * prob, axis=-1, keepdims=True))
        scores = scores.astype(BF16)
        terms = [
            dot(scores, keys[...] * head_masks[h]),
            dot_tn(scores, queries[...] * head_masks[h]),
            dot_tn(prob.astype(BF16), mixed_h),
        ]
        kept["parts"] = [t if p is None else p + t for p, t in zip(kept["parts"], terms)]
        if h == heads - 1:
            for t, scale in enumerate((0.125, 0.125, 1.0)):
                grad_qkv[t] = (kept["parts"][t] * scale).astype(BF16)

    def norm_part(i):
        rows = span(i)
        block = dot(grad_qkv[0, rows], w_qkv[0])
        block = block + dot(grad_qkv[1, rows], w_qkv[1])
        put_part(part_d, rows, block + dot(grad_qkv[2, rows], w_qkv[2]))

    def grad_of_attn(j):
        cols = slice(j * half, (j + 1) * half)
        grad = pieces[4 + j].grad
        put_piece(grad, 0, dot_tn(mixed[...], after_low[:, cols]))
        for t in range(3):
            put_piece(grad, (t + 1) * width, dot_tn(grad_qkv[t], normed[:, cols]))

    wide = NB * PIX

    def selection():
        band = lax.broadcasted_iota(jnp.int32, (BANDS * PIX, 16), 0) // PIX
        slot = lax.broadcasted_iota(jnp.int32, (BANDS * PIX, 16), 1)
        row_select = dot((band == slot).astype(F32).astype(BF16), select[...]).astype(BF16)
        table_band = lax.broadcasted_iota(jnp.int32, (NB, wide), 0)
        table_lane = lax.broadcasted_iota(jnp.int32, (NB, wide), 1) // PIX
        widen = (table_band == table_lane).astype(F32).astype(BF16)
        for b in range(BANDS):
            rows = slice(b * PIX, (b + 1) * PIX)
            spot = lax.broadcasted_iota(jnp.int32, (PIX, wide), 0)
            lane = lax.rem(lax.broadcasted_iota(jnp.int32, (PIX, wide), 1), PIX)
            block = dot(row_select[rows], widen)
            spread[rows] = jnp.where(spot == lane, block, 0.0).astype(BF16)

    def norm_one_back(i):
        rows = span(i)
        dy = get_out(out_d, rows)
        xhat = xhat_one[rows]
        small_part[0:1] += col_sum(dy * xhat)
        small_part[1:2] += col_sum(dy)
        e = dy * gain_one
        dx = rstd_one[rows] * (e - row_mean(e) - xhat * row_mean(e * xhat))
        grad_tokens[rows] = grad_after[rows] + dx

    def table_grad():
        for i in range(4):

            @pl.when(me == i)
            def _():
                embed_grad[...] = grad_tokens[0:256, i * width : (i + 1) * width].astype(BF16)

        grad_kern = dot(patches[...], embed_grad[...]).astype(BF16)
        table = dot_tn(grad_kern, spread[...])
        put_piece(pieces[6].grad, 0, table[:, : wide // 2])
        put_piece(pieces[6].grad, width, table[:, wide // 2 :])

    def small_ready():
        small_part[4:5] = grad_tokens[256:257]
        small_part[8:16] = meta_col[...] * grad_tokens[257:258]

    def pixel_part():
        pixels = dot_nt(kern[...], embed_grad[...]).astype(BF16)
        part_e[0] = pixels[: BANDS * PIX // 2]
        part_e[1] = pixels[BANDS * PIX // 2 :]

    def branch_part():
        for i in range(len(CUTS)):
            put_part(part_b, span(i), dot(activation[span(i)], w_down[...]))

    def final_output():
        for i, (lo, n) in enumerate(CUTS):
            rows = span(i)
            x = after[rows] + get_out(out_b, rows) + b_down
            if lo + n <= 256:
                output[lo + 2 : lo + n + 2] = live_col[rows] * x
            else:
                output[lo + 2 : 258] = live_col[lo:256] * x[: 256 - lo]
                output[0:2] = x[256 - lo : 258 - lo]

    def final_pixels():
        grad_patches[: BANDS * PIX // 2] = out_e[0]
        grad_patches[BANDS * PIX // 2 :] = out_e[1]

    down0, down1, up0, up1, attn0, attn1, table0 = pieces
    order = [
        embed,
        fillgate,
        selection,
        epass,
        tokens_norm,
        attention,
        (attn_part, 0),
        (sum_a.start, 0),
        (attn_part, 1),
        (sum_a.start, 1),
        (attn_part, 2),
        (sum_a.start, 2),
        (attn_part, 3),
        (sum_a.start, 3),
        (sum_a.relay, 0),
        (sum_a.relay, 1),
        (sum_a.relay, 2),
        (sum_a.relay, 3),
        (sum_a.forward, 0),
        (sum_a.forward, 1),
        (sum_a.total, 0),
        (feedforward, 0),
        (sum_a.total, 1),
        (sum_a.forward, 2),
        (sum_c.start, 0),
        (feedforward, 1),
        (sum_a.forward, 3),
        (sum_a.total, 2),
        (sum_c.relay, 0),
        (sum_c.start, 1),
        (feedforward, 2),
        (sum_a.total, 3),
        (sum_c.start, 2),
        (feedforward, 3),
        (sum_c.relay, 1),
        (sum_c.relay, 2),
        (sum_c.forward, 0),
        (sum_c.start, 3),
        (grad_of_down, 0),
        (grad_of_down, 1),
        down0.step,
        (sum_c.total, 0),
        down1.step,
        (sum_c.relay, 3),
        (grad_of_up, 0),
        up0.step,
        (sum_c.forward, 1),
        (grad_of_up, 1),
        up1.step,
        (sum_c.forward, 2),
        (norm_two_back, 0),
        (sum_c.total, 1),
        (norm_two_back, 1),
        (sum_c.total, 2),
        (sum_c.forward, 3),
        (norm_two_back, 2),
        branch_part,
        (sum_c.total, 3),
        (norm_two_back, 3),
        mixed_back,
        (head_back, 0),
        down0.step,
        down0.step,
        up1.step,
        (head_back, 1),
        (head_back, 2),
        (norm_part, 0),
        (sum_d.start, 0),
        (norm_part, 1),
        (sum_d.start, 1),
        (norm_part, 2),
        (sum_d.start, 2),
        (norm_part, 3),
        (sum_d.start, 3),
        (grad_of_attn, 0),
        (sum_d.relay, 0),
        (sum_d.relay, 1),
        (sum_d.relay, 2),
        down1.step,
        (sum_d.relay, 3),
        down0.step,
        down1.step,
        up1.step,
        up1.step,
        attn0.step,
        (grad_of_attn, 1),
        attn1.step,
        (sum_b.start, 0),
        (sum_b.start, 1),
        (sum_b.start, 2),
        (sum_b.start, 3),
        (sum_d.forward, 0),
        (sum_b.relay, 0),
        (sum_b.relay, 1),
        (sum_b.relay, 2),
        (sum_d.forward, 1),
        down0.step,
        down0.step,
        (sum_b.relay, 3),
        (sum_d.total, 0),
        (norm_one_back, 0),
        (sum_d.forward, 2),
        down1.step,
        (sum_d.total, 1),
        (norm_one_back, 1),
        (sum_d.forward, 3),
        up0.step,
        (sum_d.total, 2),
        up0.step,
        (norm_one_back, 2),
        up1.step,
        (sum_d.total, 3),
        (norm_one_back, 3),
        table_grad,
        down0.step,
        table0.step,
        down1.step,
        down1.step,
        up0.step,
        small_ready,
        small.start,
        pixel_part,
        (sum_e.start, 0),
        (sum_e.start, 1),
        (sum_b.forward, 0),
        (sum_b.forward, 1),
        (sum_b.forward, 2),
        (sum_b.forward, 3),
        attn0.step,
        attn0.step,
        (sum_e.relay, 0),
        (sum_e.relay, 1),
        (sum_b.total, 0),
        (sum_b.total, 1),
        (sum_b.total, 2),
        (sum_b.total, 3),
        final_output,
        down0.step,
        down1.step,
        attn0.step,
        up0.step,
        up0.step,
        (sum_e.forward, 0),
        attn1.step,
        down0.step,
        attn1.step,
        (sum_e.total, 0),
        (sum_e.forward, 1),
        (sum_e.total, 1),
        down1.step,
        final_pixels,
        up1.step,
        attn0.step,
        attn0.step,
        attn1.step,
        down0.step,
        up0.step,
        down1.step,
        up1.step,
        attn0.step,
        attn1.step,
        attn1.step,
        table0.step,
        table0.step,
        small.relay,
        down1.step,
        up0.step,
        up1.step,
        table0.step,
        attn0.step,
        attn1.step,
        down0.step,
        small.total,
        up0.step,
        table0.step,
        table0.step,
        down1.step,
        up1.step,
        up1.step,
        attn0.step,
        attn1.step,
        up0.step,
        table0.step,
        attn0.step,
        attn1.step,
        up0.step,
        table0.step,
        attn1.step,
        attn0.step,
        table0.step,
        attn1.step,
        table0.step,
        table0.step,
    ]
    for item in order:
        if isinstance(item, tuple):
            item[0](*item[1:])
        else:
            item()
    while any(piece.steps for piece in pieces):
        for piece in pieces:
            piece.step()
    for one in (sum_a, sum_b, sum_c, sum_d, sum_e, etc):
        one.finish()


def layer_many(dp_count, width, operands):
    lines = dp_count // 2

    def piece(rows, lanes, parts):
        chunk = -(-rows // parts)
        chunk = -(-chunk // 16) * 16
        if parts == lines:
            return (lines, chunk, lanes)
        return (2, lines, chunk, lanes)

    pieces = []
    for name, kind in KINDS_MANY:
        parts = dp_count if kind is PairFirst else lines
        if name == "table0":
            pieces.append(piece(2 * width, NB * PIX // 2, parts))
        else:
            pieces.append(piece(4 * width, D // 2, parts))

    def piece_scratch(shape):
        if len(shape) == 4:
            return [low(*shape[1:]), low(*shape[1:]), low(2, *shape[1:]), vmem(*shape[2:])]
        return [low(2, *shape), vmem(*shape[1:]), low(*shape[1:]), low(*shape[1:])]

    half = D // 2
    pixel_lanes = BANDS * PIX

    def vmem(*shape, dtype=F32):
        return pltpu.VMEM(shape, dtype)

    def low(*shape):
        return pltpu.VMEM(shape, BF16)

    scratch = [
        low(4, 256, width),
        vmem(ROWS, D),
        vmem(ROWS, D),
        vmem(ROWS, 1),
        vmem(ROWS, D),
        vmem(ROWS, 1),
        vmem(ROWS, D),
        low(ROWS, D),
        low(ROWS, D),
        low(ROWS, width),
        low(ROWS, width),
        low(ROWS, width),
        vmem(width // HEAD_DIM, ROWS, ROWS),
        low(ROWS, width),
        low(ROWS, width),
        low(3, ROWS, width),
        low(ROWS, D),
        vmem(ROWS, D),
        low(ROWS, D),
        low(ROWS, D),
        vmem(ROWS, D),
        low(ROWS, D),
        vmem(ROWS, D),
        low(256, width),
        low(pixel_lanes, NB * PIX),
    ]
    scratch += [low(2, ROWS, half)] * 4 + [low(2, pixel_lanes // 2, 256)]
    scratch += [low(5, ROWS, half)] * 4 + [low(5, pixel_lanes // 2, 256)]
    scratch += [vmem(2, ROWS, half)] * 4 + [vmem(2, pixel_lanes // 2, 256)]
    scratch.append([low(*shape) for shape in pieces])
    scratch.append([piece_scratch(shape) for shape in pieces])
    scratch += [vmem(16, D), vmem(16, D), vmem(lines, 16, D)]
    dma = pltpu.SemaphoreType.DMA
    scratch += [dma((5, 16)), dma((5, 16)), dma((len(pieces) + 1, 4 * lines + 1)), dma((len(pieces) + 1, 4 * lines + 1)), dma((3,)), dma((3,))]
    ref = pl.BlockSpec(memory_space=pltpu.VMEM)
    shapes = [
        jax.ShapeDtypeStruct((SEQ, D), F32),
        jax.ShapeDtypeStruct((pixel_lanes, 256), F32),
        jax.ShapeDtypeStruct((16, D), F32),
        [jax.ShapeDtypeStruct(shape, BF16) for shape in pieces],
    ]
    output, grad_patches, smalls, wholes = pl.pallas_call(
        functools.partial(layer_kernel_many, lines, KINDS_MANY),
        out_shape=shapes,
        in_specs=[ref] * len(operands),
        out_specs=[ref] * 3 + [[ref] * len(pieces)],
        scratch_shapes=scratch,
        compiler_params=pltpu.CompilerParams(
            collective_id=0, has_side_effects=True, vmem_limit_bytes=62 * 1024 * 1024
        ),
        name="layer",
    )(*operands)
    wholes = {name: out.reshape(-1, out.shape[-1]) for (name, kind), out in zip(KINDS_MANY, wholes)}
    return output, grad_patches, smalls, wholes


def small_sum_kernel_many(axis, count, part, out, slots, sends, recvs):
    me = lax.axis_index(axis)
    peers = [{axis: lax.rem(me + k, count)} for k in range(1, count)]
    greet(peers)
    copies = []
    for k, peer in enumerate(peers):
        copy = remote(part, slots.at[me], sends.at[k], recvs.at[k], peer)
        copy.start()
        copies.append(copy)
    slots[me] = part[...]
    for copy in copies:
        copy.wait()
    total = slots[0]
    for k in range(1, count):
        total = total + slots[k]
    out[...] = total


def small_sum_many(part, axis, count, number):
    vmem = pl.BlockSpec(memory_space=pltpu.VMEM)
    return pl.pallas_call(
        functools.partial(small_sum_kernel_many, axis, count),
        out_shape=jax.ShapeDtypeStruct(part.shape, F32),
        in_specs=[vmem],
        out_specs=vmem,
        scratch_shapes=[
            pltpu.VMEM((count,) + part.shape, F32),
            pltpu.SemaphoreType.DMA((count - 1,)),
            pltpu.SemaphoreType.DMA((count - 1,)),
        ],
        compiler_params=pltpu.CompilerParams(collective_id=number, has_side_effects=True),
        name="small_sum_" + axis,
    )(part)


def local_many(
    dp_count,
    patches,
    wavelengths,
    band_ids,
    band_mask,
    sensor,
    lengths,
    visible,
    meta,
    w_hyper,
    b_hyper,
    w_gen,
    cls_token,
    w_meta,
    gain_one,
    shift_one,
    w_qkv,
    w_out,
    gain_two,
    shift_two,
    w_up,
    b_up,
    w_down,
    b_down,
    cotangent,
):
    highest = lax.Precision.HIGHEST
    width = w_gen.shape[0]
    features = sinus_waves(wavelengths, HYP)
    positions = grid_codes(visible, lengths, D, VIS_MAX)[0]
    hyper_pre = jnp.dot(features, w_hyper, precision=highest) + b_hyper
    hidden, hyper_pull = jax.vjp(gelu_exact, hyper_pre)
    hidden_low = hidden.astype(BF16)
    ids, mask = band_ids[sensor[0]], band_mask[sensor[0]]
    select = (ids[:, None] == jnp.arange(NB)[None, :]).astype(F32) * mask[:, None].astype(F32)
    chosen = jnp.dot(select.astype(BF16), hidden_low, preferred_element_type=F32).astype(BF16)
    kern = jnp.einsum("bh,dph->bpd", chosen, w_gen, preferred_element_type=F32).astype(BF16)
    kern = kern.reshape(BANDS * PIX, width)
    place = jnp.arange(ROWS)
    live = ((place < lengths[0]) | ((place >= 256) & (place < SEQ))).astype(F32)
    meta_row = jnp.dot(meta, w_meta, precision=highest)[0]
    rows_in = jnp.stack([gain_one, shift_one, gain_two, shift_two, b_down, cls_token, meta_row, meta_row])
    operands = (
        patches[0].T,
        kern,
        positions,
        rows_in,
        meta.reshape(-1, 1),
        live[None, :],
        live[:, None],
        jnp.pad(select.astype(BF16), ((0, 16 - BANDS), (0, 0))),
        w_qkv,
        w_out,
        w_up,
        b_up[None, :],
        w_down,
        cotangent[0],
    )
    output, grad_patches, smalls, wholes = layer_many(dp_count, width, operands)

    def joined(name):
        halves = [wholes[f"{name}{j}"][: 4 * width] for j in range(2)]
        return jnp.concatenate(halves, axis=1).astype(F32)

    grad_w_down, grad_w_up, attn = joined("down"), joined("up"), joined("attn")
    table = wholes["table0"][: 2 * width].reshape(2, width, NB // 2, PIX)
    low_halves = hidden_low.reshape(2, NB // 2, HYP)
    grad_w_gen = jnp.einsum("anh,adnp->dph", low_halves, table, preferred_element_type=F32)
    hidden_part = jnp.einsum("adnp,dph->anh", table, w_gen, preferred_element_type=F32)
    grad_hidden = small_sum_many(hidden_part.reshape(NB, HYP), "mp", 4, 1)
    grad_inner = hyper_pull(grad_hidden)[0]
    grad_w_hyper = jnp.dot(features.T, grad_inner, precision=highest)
    grad_b_hyper = jnp.sum(grad_inner, axis=0)
    return (
        output[None],
        grad_patches.T[None],
        grad_w_hyper,
        grad_b_hyper,
        grad_w_gen,
        smalls[4],
        smalls[8:16],
        smalls[0],
        smalls[1],
        attn[width : 4 * width].reshape(3, width, D),
        attn[:width],
        smalls[2],
        smalls[3],
        grad_w_up,
        smalls[6],
        grad_w_down,
        smalls[5],
    )


def solution(mesh):
    return jax.shard_map(
        functools.partial(local if mesh.shape["dp"] == 8 else local_many, mesh.shape["dp"]),
        mesh=mesh,
        in_specs=(
            P("dp", None, None),
            P(),
            P(),
            P(),
            P("dp"),
            P("dp"),
            P("dp", None),
            P("dp", None),
            P(),
            P(),
            P("mp", None, None),
            P(),
            P(),
            P(),
            P(),
            P(None, "mp", None),
            P("mp", None),
            P(),
            P(),
            P(None, "mp"),
            P("mp"),
            P("mp", None),
            P(),
            P("dp", None, None),
        ),
        out_specs=(
            P("dp", None, None),
            P("dp", None, None),
            P(),
            P(),
            P("mp", None, None),
            P(),
            P(),
            P(),
            P(),
            P(None, "mp", None),
            P("mp", None),
            P(),
            P(),
            P(None, "mp"),
            P("mp"),
            P("mp", None),
            P(),
        ),
        check_vma=False,
    )
```

```python
import functools
import math

import jax
import jax.numpy as jnp
from jax import lax
from jax.experimental import pallas as pl
from jax.experimental.pallas import tpu as pltpu
from jax.sharding import PartitionSpec as P

F32 = jnp.float32
BF16 = jnp.bfloat16
MESH = pl.DeviceIdType.MESH

D = 768
HEAD_DIM = 64
PIX = 64
HYP = 128
BANDS = 13
NB = 32
SENSORS = 4
VIS_MAX = 256
SEQ = 258


def sinus_waves(wavelengths, width):
    half_width = width // 2
    steps = jnp.arange(half_width, dtype=jnp.float32)
    freqs = jnp.exp(steps * (6.0 * math.log(2.0) / half_width))
    angles = wavelengths[:, None] * freqs[None, :]
    return jnp.concatenate([jnp.sin(angles), jnp.cos(angles)], axis=1)


def grid_omegas(width):
    quarter = width // 4
    return jnp.exp(jnp.arange(quarter, dtype=jnp.float32) * (-math.log(10000.0) / quarter))


def grid_waves(width, most):
    numbers = jnp.arange(2 * math.isqrt(most), dtype=jnp.float32)
    angles = numbers[:, None] * grid_omegas(width)
    return jnp.stack([jnp.sin(angles), jnp.cos(angles)])


def grid_codes(visible, lengths, width, most):
    short_side = math.isqrt(most)
    sides = jnp.where(lengths == most, 2 * short_side, short_side).astype(jnp.int32)[:, None]
    omegas = grid_omegas(width)
    row_angle = (visible // sides).astype(jnp.float32)[..., None] * omegas
    col_angle = (visible % sides).astype(jnp.float32)[..., None] * omegas
    return jnp.concatenate(
        [jnp.sin(row_angle), jnp.cos(row_angle), jnp.sin(col_angle), jnp.cos(col_angle)], axis=-1
    )


def gelu_exact(values):
    return jax.nn.gelu(values, approximate=False)


def remote(src, dst, send_sem, recv_sem, device):
    return pltpu.make_async_remote_copy(
        src_ref=src,
        dst_ref=dst,
        send_sem=send_sem,
        recv_sem=recv_sem,
        device_id=device,
        device_id_type=MESH,
    )


def greet(devices):
    barrier = pltpu.get_barrier_semaphore()
    for device in devices:
        pl.semaphore_signal(barrier, inc=1, device_id=device, device_id_type=MESH)
    pl.semaphore_wait(barrier, len(devices))


def mp_peers():
    place = lax.axis_index("mp")
    core = lax.rem(place, 2)
    return core, {"mp": place + 1 - 2 * core}, {"mp": lax.rem(place + 2, 4)}


class Sender:
    def __init__(self, sends, recvs):
        self.sends, self.recvs, self.copies = sends, recvs, []

    def go(self, number, src, dst, device):
        copy = remote(src, dst, self.sends.at[number], self.recvs.at[number], device)
        copy.start()
        self.copies.append(copy)
        return copy

    def finish(self):
        for copy in self.copies:
            copy.wait_send()


class MpSum(Sender):
    def __init__(self, part, slots, out, cuts, sends, recvs):
        super().__init__(sends, recvs)
        self.part, self.out, self.cuts = part, out, cuts
        self.pair_in, self.chip_sum, self.far_in, self.other_near, self.other_far = slots
        self.core, self.pair, self.far = mp_peers()
        self.first, self.second, self.third = {}, {}, {}

    def number(self, step, i):
        return step * len(self.cuts) + i

    def start(self, i):
        rows = pl.ds(*self.cuts[i])
        self.first[i] = self.go(
            self.number(0, i), self.part.at[1 - self.core, rows], self.pair_in.at[rows], self.pair
        )

    def relay(self, i):
        rows = pl.ds(*self.cuts[i])
        self.first[i].wait_recv()
        self.chip_sum[rows] = (
            self.part[self.core, rows].astype(F32) + self.pair_in[rows].astype(F32)
        ).astype(BF16)
        mine = self.chip_sum.at[rows]
        self.second[i] = (
            self.go(self.number(1, i), mine, self.far_in.at[rows], self.far),
            self.go(self.number(2, i), mine, self.other_near.at[rows], self.pair),
        )

    def forward(self, i):
        rows = pl.ds(*self.cuts[i])
        self.second[i][0].wait_recv()
        self.third[i] = self.go(
            self.number(3, i), self.far_in.at[rows], self.other_far.at[rows], self.pair
        )
        self.out[self.core, rows] = self.chip_sum[rows].astype(F32) + self.far_in[rows].astype(F32)

    def total(self, i):
        rows = pl.ds(*self.cuts[i])
        self.second[i][1].wait_recv()
        self.third[i].wait_recv()
        self.out[1 - self.core, rows] = self.other_near[rows].astype(F32) + self.other_far[
            rows
        ].astype(F32)


class DpPlace:
    def __init__(self, lines):
        place = lax.axis_index("dp")
        self.lines = lines
        self.inner = lax.rem(place, 2)
        self.outer = place // 2
        self.pair = {"dp": self.outer * 2 + 1 - self.inner}

    def peer(self, k):
        return {"dp": lax.rem(self.outer + k, self.lines) * 2 + self.inner}


class Chain:
    def __init__(self, place, sends, recvs):
        self.place, self.sends, self.recvs = place, sends, recvs
        self.ends = []
        self.low = place.outer < (place.lines + 1) // 2
        self.depth = jnp.where(self.low, place.outer, place.lines - 1 - place.outer)

    def copy(self, number, src, dst, device):
        return remote(src, dst, self.sends.at[number], self.recvs.at[number], device)

    def start(self, copy, cond=None):
        if cond is None:
            copy.start()
        else:
            pl.when(cond)(copy.start)
        self.ends.append((copy, cond))

    def next_to(self, up):
        place = self.place
        outer = jnp.where(up, place.outer + 1, place.outer - 1)
        outer = jnp.clip(outer, 0, place.lines - 1)
        return {"dp": outer * 2 + place.inner}

    def step(self):
        if self.steps:
            self.steps.pop(0)()

    def drain(self):
        while self.steps:
            self.step()

    def finish(self):
        for copy, cond in self.ends:
            if cond is None:
                copy.wait_send()
            else:
                pl.when(cond)(copy.wait_send)

    def hop(self, flow, i, outward):
        lines = self.place.lines
        up = self.low if outward else jnp.logical_not(self.low)
        way = jnp.where(up, 0, 1)
        chunk = jnp.where(up, lines - 1 - i, i)
        slot = flow.at[way, chunk]
        return slot, chunk, self.copy(way * lines + chunk, slot, slot, self.next_to(up))

    def out(self, own, flow):
        for i in range(self.place.lines - 1):
            slot, chunk, copy = self.hop(flow, i, True)

            @pl.when(self.depth == 0)
            def _(slot=slot, chunk=chunk):
                slot[...] = own[chunk]

            self.start(copy, self.depth == 0)

    def on(self, own, flow, i, outward):
        slot, chunk, copy = self.hop(flow, i, outward)
        inner = i < self.place.lines - 1 - self.depth if outward else i < self.depth
        active = jnp.logical_and(self.depth > 0, inner)

        @pl.when(active)
        def _():
            copy.wait_recv()
            slot[...] = (slot[...].astype(F32) + own[chunk].astype(F32)).astype(BF16)

        self.start(copy, active)

    def sum_steps(self, own, flow):
        lines = self.place.lines
        steps = [functools.partial(self.out, own, flow)]
        for i in range(lines - 2):
            steps.append(functools.partial(self.on, own, flow, i, True))
            if i < (lines + 1) // 2 - 1:
                steps.append(functools.partial(self.on, own, flow, i, False))
        return steps

    def sum_end(self, own, flow, total):
        lines, z = self.place.lines, self.place.outer
        total[...] = own[z].astype(F32)
        for way, cond in ((0, z > 0), (1, z < lines - 1)):
            slot = flow.at[way, z]
            copy = self.copy(way * lines + z, slot, slot, self.next_to(z > 0))

            @pl.when(cond)
            def _(slot=slot, copy=copy):
                copy.wait_recv()
                total[...] += slot[...].astype(F32)

    def spread_start(self, whole, base):
        lines, z = self.place.lines, self.place.outer
        mine = whole.at[z]
        self.start(self.copy(base + z, mine, mine, self.next_to(True)), z < lines - 1)
        self.start(self.copy(base + z, mine, mine, self.next_to(False)), z > 0)

    def spread_step(self, whole, base, r, then=None):
        lines, z = self.place.lines, self.place.outer
        for up, chunk, cond, more in (
            (True, z - r, z - r >= 0, z < lines - 1),
            (False, z + r, z + r < lines, z > 0),
        ):
            chunk = jnp.clip(chunk, 0, lines - 1)
            slot = whole.at[chunk]
            copy = self.copy(base + chunk, slot, slot, self.next_to(up))
            pl.when(cond)(copy.wait_recv)
            self.start(copy, jnp.logical_and(cond, more))
            if then is not None:
                then(chunk, slot, cond)


class PairFirst(Chain):
    def __init__(self, place, grad, scratch, whole, sends, recvs):
        super().__init__(place, sends, recvs)
        self.grad, self.whole = grad, whole.at[place.inner]
        self.pair_in, self.half, self.flow, self.total = scratch
        lines = place.lines
        steps = [self.pair_start, self.pair_end] + self.sum_steps(self.half, self.flow)
        steps.append(self.line_end)
        for r in range(1, lines):
            steps.append(functools.partial(self.spread_step, self.whole, 2 * lines, r, self.to_pair))
        steps.append(self.end)
        self.steps = steps

    def pair_start(self):
        place = self.place
        copy = self.copy(4 * place.lines, self.grad.at[1 - place.inner], self.pair_in, place.pair)
        self.first = copy
        self.start(copy)

    def pair_end(self):
        self.first.wait_recv()
        for z in range(self.place.lines):
            self.half[z] = (
                self.grad[self.place.inner, z].astype(F32) + self.pair_in[z].astype(F32)
            ).astype(BF16)

    def to_pair(self, chunk, slot, cond=None):
        self.start(self.copy(3 * self.place.lines + chunk, slot, slot, self.place.pair), cond)

    def line_end(self):
        z = self.place.outer
        self.sum_end(self.half, self.flow, self.total)
        self.whole[z] = self.total[...].astype(BF16)
        self.spread_start(self.whole, 2 * self.place.lines)
        self.to_pair(z, self.whole.at[z])

    def end(self):
        for z in range(self.place.lines):
            slot = self.whole.at[z]
            self.copy(3 * self.place.lines + z, slot, slot, self.place.pair).wait_recv()
        self.finish()


class LineFirst(Chain):
    def __init__(self, place, grad, scratch, whole, sends, recvs):
        super().__init__(place, sends, recvs)
        self.grad, self.whole = grad, whole
        self.flow, self.total, self.mine, self.pair_in = scratch
        lines = place.lines
        steps = self.sum_steps(self.grad, self.flow)
        steps += [self.pair_start, self.pair_end]
        for r in range(1, lines):
            steps.append(functools.partial(self.spread_step, self.whole, 2 * lines, r))
        steps.append(self.finish)
        self.steps = steps

    def pair_start(self):
        self.sum_end(self.grad, self.flow, self.total)
        self.mine[...] = self.total[...].astype(BF16)
        copy = self.copy(4 * self.place.lines, self.mine, self.pair_in, self.place.pair)
        self.first = copy
        self.start(copy)

    def pair_end(self):
        self.first.wait_recv()
        self.whole[self.place.outer] = (
            self.mine[...].astype(F32) + self.pair_in[...].astype(F32)
        ).astype(BF16)
        self.spread_start(self.whole, 2 * self.place.lines)


class LineGather(Chain):
    def __init__(self, place, bank, sends, recvs, share=None):
        super().__init__(place, sends, recvs)
        self.bank, self.share = bank, share
        lines = place.lines
        self.mine = bank.at[place.inner]
        steps = [self.begin]
        for r in range(1, lines):
            steps.append(functools.partial(self.spread_step, self.mine, 0, r, self.hand_on))
        self.steps = steps + [self.from_pair, self.end]

    def hand_on(self, chunk, slot, cond=None):
        lines = self.place.lines
        self.start(self.copy(lines + chunk, slot, slot, self.place.pair), cond)
        self.to_core(self.place.inner * lines + chunk, slot, cond)

    def to_core(self, number, slot, cond=None):
        if self.share is not None:
            device, sends, recvs = self.share[:3]
            self.start(remote(slot, slot, sends.at[number], recvs.at[number], device), cond)

    def begin(self):
        z = self.place.outer
        self.spread_start(self.mine, 0)
        self.hand_on(z, self.mine.at[z])

    def from_pair(self):
        lines, other = self.place.lines, 1 - self.place.inner
        for z in range(lines):
            slot = self.bank.at[other, z]
            self.copy(lines + z, slot, slot, self.place.pair).wait_recv()
            self.to_core(other * lines + z, slot)

    def end(self):
        if self.share is not None:
            device, sends, recvs, there = self.share
            for i in range(2):
                for z in range(self.place.lines):
                    number, slot = i * self.place.lines + z, there.at[i, z]
                    remote(slot, slot, sends.at[number], recvs.at[number], device).wait_recv()
        self.finish()


class SmallSum(Sender):
    def __init__(self, place, part, pair_in, line_in, out, sends, recvs):
        super().__init__(sends, recvs)
        self.place, self.part, self.pair_in, self.line_in, self.out = place, part, pair_in, line_in, out

    def start(self):
        self.first = self.go(0, self.part, self.pair_in, self.place.pair)

    def relay(self):
        place, lines = self.place, self.place.lines
        self.first.wait_recv()
        self.line_in[place.outer] = self.part[...] + self.pair_in[...]
        mine = self.line_in.at[place.outer]
        self.second = [self.go(k, mine, mine, place.peer(k)) for k in range(1, lines)]

    def total(self):
        for copy in self.second:
            copy.wait_recv()
        total = self.line_in[0]
        for z in range(1, self.place.lines):
            total = total + self.line_in[z]
        self.out[...] = total
        self.finish()


class MpSmall(Sender):
    def __init__(self, part, slots, out, sends, recvs):
        super().__init__(sends, recvs)
        self.part, self.slots, self.out = part, slots, out
        core, pair, far = mp_peers()
        self.peers = [pair, far, {"mp": far["mp"] + 1 - 2 * core}]

    def begin(self):
        me = lax.axis_index("mp")
        self.slots[me] = self.part[...]
        for k, peer in enumerate(self.peers):
            self.go(k, self.part, self.slots.at[me], peer)

    def total(self):
        for copy in self.copies:
            copy.wait_recv()
        total = self.slots[0]
        for k in range(1, 4):
            total = total + self.slots[k]
        self.out[...] = total


def dot(left, right):
    return jnp.dot(left, right, preferred_element_type=F32)


def dot_nt(left, right):
    return lax.dot_general(left, right, (((1,), (1,)), ((), ())), preferred_element_type=F32)


def dot_tn(left, right):
    return lax.dot_general(left, right, (((0,), (0,)), ((), ())), preferred_element_type=F32)


def row_mean(values):
    return jnp.mean(values, axis=-1, keepdims=True)


def col_sum(values):
    return jnp.sum(values, axis=0, keepdims=True)


ROWS = 272
CUTS = [(0, 64), (64, 64), (128, 64), (192, 80)]
GROUP = 8
SLOTS = 16
PIXEL_CUTS = [(0, 208), (208, 208)]


KINDS = (
    ("down0", LineFirst),
    ("down1", PairFirst),
    ("up0", PairFirst),
    ("up1", LineFirst),
    ("attn0", PairFirst),
    ("attn1", PairFirst),
)


def layer_kernel(
    lines,
    kinds,
    far_patches,
    hidden,
    far_w_gen,
    waves,
    visible,
    row_parts,
    w_meta,
    meta,
    lengths,
    sensor,
    band_ids,
    band_mask,
    far_w_qkv,
    far_w_out,
    far_w_up,
    far_w_down,
    far_cotangent,
    far_output,
    far_grad_patches,
    smalls,
    hidden_grad,
    grad_gen,
    far_wholes,
    embeds,
    tokens,
    xhat_one,
    rstd_one,
    xhat_two,
    rstd_two,
    after,
    normed,
    normed_two,
    queries,
    keys,
    values,
    probs,
    mixed,
    grad_mixed,
    grad_qkv,
    branch_grad,
    gate_grad,
    activation,
    grad_pre,
    after_low,
    bank,
    embed_bank,
    spots,
    kern,
    picks,
    kern_grads,
    table,
    gen_out,
    hidden_part,
    hidden_slots,
    part_a,
    part_b,
    part_c,
    part_d,
    part_e,
    slots_a,
    slots_b,
    slots_c,
    slots_d,
    slots_e,
    out_a,
    out_b,
    out_c,
    out_d,
    out_e,
    grads,
    slots,
    small_part,
    small_pair,
    small_line,
    mp_sends,
    mp_recvs,
    dp_sends,
    dp_recvs,
    etc_sends,
    etc_recvs,
    share_sends,
    share_recvs,
    out_sem,
    patches,
    raw_gen,
    w_table,
    positions,
    rows_in,
    meta_col,
    live_row,
    live_col,
    select,
    w_qkv,
    w_out,
    w_up,
    w_down,
    cotangent,
    output,
    grad_patches,
    wholes,
    in_sems,
    end_sems,
):
    core, pair, far = mp_peers()
    place = DpPlace(lines)
    loads = {}
    gen_block = raw_gen.shape[1]
    moves = [(far_w_gen.at[pl.ds(k * gen_block, gen_block)], raw_gen.at[k]) for k in range(2)]
    moves += [
        (far_patches, patches),
        (far_cotangent, cotangent),
        (far_w_down, w_down),
        (far_w_qkv, w_qkv),
        (far_w_out, w_out),
        (far_w_up, w_up),
    ]
    for number, (src, dst) in enumerate(moves):
        loads[number] = pltpu.make_async_copy(src, dst, in_sems.at[number])
        loads[number].start()

    def need(number):
        if number in loads:
            loads.pop(number).wait()

    for k, part in enumerate(row_parts[:6]):
        rows_in[k : k + 1] = part[...].reshape(1, D)
    meta_row = meta[0, 0] * w_meta[0:1]
    for k in range(1, w_meta.shape[0]):
        meta_row = meta_row + meta[0, k] * w_meta[k : k + 1]
    rows_in[6:7] = meta_row
    meta_at = lax.broadcasted_iota(jnp.int32, meta_col.shape, 0)
    meta_values = jnp.zeros(meta_col.shape, F32)
    for k in range(w_meta.shape[0]):
        meta_values = jnp.where(meta_at == k, meta[0, k], meta_values)
    meta_col[...] = meta_values
    for live in (live_row, live_col):
        at = lax.broadcasted_iota(jnp.int32, live.shape, 0 if live is live_col else 1)
        live[...] = ((at < lengths[0]) | ((at >= 256) & (at < SEQ))).astype(F32)
    slot_at = lax.broadcasted_iota(jnp.int32, select.shape, 0)
    band_at = lax.broadcasted_iota(jnp.int32, select.shape, 1)
    picked = jnp.zeros(select.shape, F32)
    for b in range(BANDS):
        on = (slot_at == b) & (band_at == band_ids[sensor[0], b])
        picked = jnp.where(on, band_mask[sensor[0], b].astype(F32), picked)
    select[...] = picked.astype(BF16)
    b_up = row_parts[6]

    stores = []

    def keep(src, dst):
        stores.append(pltpu.make_async_copy(src, dst, end_sems.at[len(stores)]))
        stores[-1].start()

    cross = {"mp": far["mp"] + 1 - 2 * core}
    greet([pair, far, cross, place.pair] + [place.peer(k) for k in range(1, lines)])
    me = lax.axis_index("mp")
    width = w_out.shape[0]
    heads = width // HEAD_DIM
    full = D

    def mp_sum(part, slots, out, cuts, number):
        return MpSum(
            part,
            [slots.at[k] for k in range(5)],
            out,
            cuts,
            mp_sends.at[number],
            mp_recvs.at[number],
        )

    sum_a = mp_sum(part_a, slots_a, out_a, CUTS, 0)
    sum_b = mp_sum(part_b, slots_b, out_b, CUTS, 1)
    sum_c = mp_sum(part_c, slots_c, out_c, CUTS, 2)
    sum_d = mp_sum(part_d, slots_d, out_d, CUTS, 3)
    sum_e = mp_sum(part_e, slots_e, out_e, PIXEL_CUTS, 4)

    pieces = []
    for number, (name, kind) in enumerate(kinds):
        pieces.append(
            kind(
                place,
                grads[number],
                slots[number],
                wholes[number],
                dp_sends.at[number],
                dp_recvs.at[number],
            )
        )
    count = len(kinds)
    early = LineGather(
        place,
        bank.at[core],
        dp_sends.at[count + 1],
        dp_recvs.at[count + 1],
        (pair, share_sends, share_recvs, bank.at[1 - core]),
    )
    late = LineGather(place, embed_bank, dp_sends.at[count + 2], dp_recvs.at[count + 2])
    hidden_sum = MpSmall(hidden_part, hidden_slots, hidden_grad, etc_sends.at[pl.ds(3, 3)], etc_recvs.at[pl.ds(3, 3)])
    small = SmallSum(place, small_part, small_pair, small_line, smalls, dp_sends.at[len(kinds)], dp_recvs.at[len(kinds)])

    def put_piece(grad, first_row, block):
        rows = grad.shape[-2]
        for k in range(0, block.shape[0], rows):
            chunk = (first_row + k) // rows
            spot = (chunk,) if len(grad.shape) == 3 else (chunk // lines, chunk % lines)
            grad[spot] = block[k : k + rows].astype(BF16)

    gain_one, shift_one = rows_in[0:1], rows_in[1:2]
    gain_two, shift_two = rows_in[2:3], rows_in[3:4]
    b_down = rows_in[4:5]
    lane_head = lax.broadcasted_iota(jnp.int32, (1, width), 1) // HEAD_DIM
    head_masks = [(lane_head == h).astype(F32).astype(BF16) for h in range(heads)]

    grad_after, grad_tokens = gate_grad, tokens
    etc = Sender(etc_sends, etc_recvs)
    kept = {}

    def iota(rows, lanes, dim):
        return lax.broadcasted_iota(jnp.int32, (rows, lanes), dim)

    def blocks(block, rows, lanes):
        tall = jnp.concatenate([block] * GROUP, axis=0)
        wide = jnp.concatenate([tall] * GROUP, axis=1)
        on = iota(*wide.shape, 0) // rows == iota(*wide.shape, 1) // lanes
        return jnp.where(on, wide.astype(F32), 0.0).astype(BF16)

    pixels = BANDS * PIX
    part_rows = PIX // GROUP // 2
    group_rows = GROUP * SLOTS

    def relay_gen():
        stage = gen_out.reshape(gen_block * PIX, HYP)
        for i in range(width // gen_block):
            need(i) if i < 2 else kept["gen"].pop(0).wait()
            stage[...] = raw_gen[i % 2].reshape(gen_block * PIX, HYP).astype(F32)
            if i + 2 < width // gen_block:
                copy = pltpu.make_async_copy(
                    far_w_gen.at[pl.ds((i + 2) * gen_block, gen_block)], raw_gen.at[i % 2], in_sems.at[i % 2]
                )
                copy.start()
                kept.setdefault("gen", []).append(copy)
            for p in range(PIX):
                w_table[i * gen_block : (i + 1) * gen_block, p * HYP : (p + 1) * HYP] = stage[
                    pl.ds(p, gen_block, stride=PIX), :
                ].astype(BF16)

    def make_positions():
        side = math.isqrt(VIS_MAX)
        big = lengths[0] == VIS_MAX
        at = iota(2 * side, VIS_MAX, 0)
        for k in range(2):
            small, large = (visible[...] // side, visible[...] // (2 * side)) if k == 0 else (
                lax.rem(visible[...], side),
                lax.rem(visible[...], 2 * side),
            )
            pick = (at == jnp.where(big, large, small)).astype(F32)
            for w in range(2):
                positions[2 * k + w] = lax.dot_general(
                    pick,
                    waves[w],
                    (((0,), (0,)), ((), ())),
                    precision=lax.Precision.HIGHEST,
                    preferred_element_type=F32,
                )

    def w_group(g):
        return w_table[:, g * GROUP * HYP : (g + 1) * GROUP * HYP]

    def make_kern():
        row, col = iota(PIX * SLOTS, pixels, 0), iota(PIX * SLOTS, pixels, 1)
        want = lax.rem(row, SLOTS) * PIX + row // SLOTS
        spots[...] = (col == want).astype(F32).astype(BF16)
        relay_gen()
        chosen = dot(select[...], hidden[...]).astype(BF16)
        wide = blocks(chosen, SLOTS, HYP)
        for g in range(PIX // GROUP):
            kern_grads[g, 0:group_rows] = dot_nt(wide, w_group(g)).astype(BF16)
        rows = jnp.concatenate([kern_grads[g, 0:group_rows] for g in range(PIX // GROUP)], axis=0)
        kern[...] = dot_tn(spots[...], rows).astype(BF16)

    def fill_bank():
        need(2)
        half_rows = PIX * SLOTS // 2
        for c in range(2):

            @pl.when(core == c)
            def _():
                rows = dot(spots[c * half_rows : (c + 1) * half_rows], patches[...])
                bank[c, place.inner, place.outer, 0:half_rows] = rows.astype(BF16)
                bank[c, place.inner, place.outer, half_rows : half_rows + SLOTS, 0:128] = jnp.concatenate(
                    [select[...].astype(F32), jnp.zeros((SLOTS, 128 - NB), F32)], axis=1
                ).astype(BF16)
                bank[c, place.inner, place.outer, half_rows : half_rows + SLOTS, 128:256] = jnp.zeros(
                    (SLOTS, 128), BF16
                )

    def make_picks():
        half_rows = PIX * SLOTS // 2
        for c in range(2 * lines):
            mine = bank[0, c // lines, c % lines, half_rows : half_rows + SLOTS, 0:128]
            picks[c * group_rows : (c + 1) * group_rows] = blocks(mine[:, 0:NB], SLOTS, NB)

    def kern_grad(c):
        block = embed_bank[c // lines, c % lines]
        for h in range(2):
            rows = dot(bank[h, c // lines, c % lines, 0 : PIX * SLOTS // 2], block).astype(BF16)
            for k in range(part_rows):
                kern_grads[h * part_rows + k, c * group_rows : (c + 1) * group_rows] = rows[
                    k * group_rows : (k + 1) * group_rows
                ]

    def kern_grad_half(i):
        for c in range(i * lines, (i + 1) * lines):
            kern_grad(c)

    def table_part(g):
        got = dot_tn(kern_grads[g], picks[...]).astype(BF16)
        table[g * width : (g + 1) * width] = got
        grads_g = dot(got, kept["hidden"])
        if g >= 2:
            kept[g - 2].wait()
        for k in range(GROUP):
            gen_out[g % 2, pl.ds(k, width, stride=GROUP), :] = grads_g[:, k * HYP : (k + 1) * HYP]
        kept[g] = pltpu.make_async_copy(
            gen_out.at[g % 2].reshape(width, GROUP, HYP),
            grad_gen.at[:, pl.ds(g * GROUP, GROUP), :],
            out_sem.at[g % 2],
        )
        kept[g].start()

    def table_start():
        kept["hidden"] = blocks(hidden[...], NB, HYP)

    def hidden_grads():
        flat = jnp.concatenate([w_group(g) for g in range(PIX // GROUP)], axis=0)
        every = dot_tn(table[...], flat)
        total = every[0:NB, 0:HYP]
        for k in range(1, GROUP):
            total = total + every[k * NB : (k + 1) * NB, k * HYP : (k + 1) * HYP]
        hidden_part[...] = total

    def embed():
        need(2)
        embeds[me] = dot_tn(patches[...], kern[...]).astype(BF16)
        mine = embeds.at[me]
        kept["pair"] = etc.go(0, mine, mine, pair)
        kept["far"] = etc.go(1, mine, mine, far)

    def epass():
        kept["far"].wait_recv()
        got = embeds.at[lax.rem(me + 2, 4)]
        kept["passed"] = etc.go(2, got, got, pair)

    def fillgate():
        need(3)
        need(4)
        branch_grad[0:256] = (live_col[0:256] * cotangent[2:258]).astype(BF16)
        branch_grad[256:272] = jnp.concatenate(
            [cotangent[0:2], jnp.zeros((14, full), F32)], axis=0
        ).astype(BF16)
        small_part[...] = jnp.zeros_like(small_part)
        small_part[5:6] = col_sum(branch_grad[...].astype(F32))
        gate_grad[...] = dot_nt(branch_grad[...], w_down[...])

    def tokens_norm():
        kept["pair"].wait_recv()
        kept["passed"].wait_recv()
        for lo, n in CUTS:
            hi = min(lo + n, 256)
            for i in range(4):
                cols = slice(i * width, (i + 1) * width)
                tokens[lo:hi, cols] = embeds[i, lo:hi].astype(F32) + positions[i, lo:hi]
            if lo + n > 256:
                tokens[256:272] = jnp.concatenate([rows_in[5:7], jnp.zeros((14, full), F32)], axis=0)
            rows = slice(lo, lo + n)
            x = tokens[rows]
            centred = x - row_mean(x)
            rstd = lax.rsqrt(row_mean(centred * centred) + 1e-05)
            rstd_one[rows] = rstd
            xhat = centred * rstd
            xhat_one[rows] = xhat
            normed[rows] = (xhat * gain_one + shift_one).astype(BF16)

    def attention():
        need(5)
        queries[...] = dot_nt(normed[...], w_qkv[0]).astype(BF16)
        keys[...] = dot_nt(normed[...], w_qkv[1]).astype(BF16)
        values[...] = dot_nt(normed[...], w_qkv[2]).astype(BF16)
        live_keys = live_row[...] > 0
        total = None
        for h in range(heads):
            raw = dot_nt(queries[...] * head_masks[h], keys[...]) * 0.125
            raw = jnp.where(live_keys, raw, -1000000000.0)
            expo = jnp.exp(raw - jnp.max(raw, axis=-1, keepdims=True))
            prob = expo / jnp.sum(expo, axis=-1, keepdims=True)
            probs[h] = prob
            term = dot(prob.astype(BF16), values[...] * head_masks[h])
            total = term if total is None else total + term
        mixed[...] = total.astype(BF16)

    def put_part(part, rows, block):
        half = block.shape[1] // 2
        part[0, rows] = block[:, :half].astype(BF16)
        part[1, rows] = block[:, half:].astype(BF16)

    def get_out(out, rows):
        return jnp.concatenate([out[0, rows], out[1, rows]], axis=1)

    def span(i):
        lo, n = CUTS[i]
        return slice(lo, lo + n)

    def attn_part(i):
        need(6)
        put_part(part_a, span(i), dot(mixed[span(i)], w_out[...]))

    def feedforward(i):
        need(7)
        rows = span(i)
        x = tokens[rows] + get_out(out_a, rows)
        after[rows] = x
        centred = x - row_mean(x)
        rstd = lax.rsqrt(row_mean(centred * centred) + 1e-05)
        rstd_two[rows] = rstd
        xhat = centred * rstd
        xhat_two[rows] = xhat
        normed_two[rows] = (xhat * gain_two + shift_two).astype(BF16)
        gate = dot(normed_two[rows], w_up[...]) + b_up[...].reshape(1, width * 4)
        cdf = 0.5 + 0.5 * lax.erf(gate * (2.0**-0.5))
        activation[rows] = (gate * cdf).astype(BF16)
        pdf = jnp.exp(-0.5 * gate * gate) * ((2.0 * math.pi) ** -0.5)
        grad_pre[rows] = (gate_grad[rows] * (cdf + gate * pdf)).astype(BF16)
        put_part(part_c, rows, dot_nt(grad_pre[rows], w_up[...]))

    half = full // 2

    def grad_of_down(j):
        cols = slice(j * half, (j + 1) * half)
        put_piece(pieces[j].grad, 0, dot_tn(activation[...], branch_grad[:, cols]))

    def grad_of_up(j):
        cols = slice(j * half, (j + 1) * half)
        put_piece(pieces[2 + j].grad, 0, dot_tn(normed_two[...], grad_pre[:, cols]))
        if j == 1:
            small_part[6:7] = col_sum(grad_pre[...].astype(F32))

    def norm_two_back(i):
        rows = span(i)
        lo, n = CUTS[i]
        dy = get_out(out_c, rows)
        xhat = xhat_two[rows]
        small_part[2:3] += col_sum(dy * xhat)
        small_part[3:4] += col_sum(dy)
        e = dy * gain_two
        dx = rstd_two[rows] * (e - row_mean(e) - xhat * row_mean(e * xhat))
        if lo + n <= 256:
            grad_out = live_col[rows] * cotangent[lo + 2 : lo + n + 2]
        else:
            grad_out = jnp.concatenate(
                [live_col[lo:256] * cotangent[lo + 2 : 258], cotangent[0:2], jnp.zeros((14, full), F32)],
                axis=0,
            )
        grad_x = dx + grad_out
        grad_after[rows] = grad_x
        after_low[rows] = grad_x.astype(BF16)

    def mixed_back():
        grad_mixed[...] = dot_nt(after_low[...], w_out[...]).astype(BF16)
        kept["parts"] = [None, None, None]

    def head_back(h):
        mixed_h = grad_mixed[...] * head_masks[h]
        grad_probs = dot_nt(mixed_h, values[...])
        prob = probs[h]
        scores = prob * (grad_probs - jnp.sum(grad_probs * prob, axis=-1, keepdims=True))
        scores = scores.astype(BF16)
        terms = [
            dot(scores, keys[...] * head_masks[h]),
            dot_tn(scores, queries[...] * head_masks[h]),
            dot_tn(prob.astype(BF16), mixed_h),
        ]
        kept["parts"] = [t if p is None else p + t for p, t in zip(kept["parts"], terms)]
        if h == heads - 1:
            for t, scale in enumerate((0.125, 0.125, 1.0)):
                grad_qkv[t] = (kept["parts"][t] * scale).astype(BF16)

    def norm_part(i):
        rows = span(i)
        block = dot(grad_qkv[0, rows], w_qkv[0])
        block = block + dot(grad_qkv[1, rows], w_qkv[1])
        put_part(part_d, rows, block + dot(grad_qkv[2, rows], w_qkv[2]))

    def grad_of_attn(j):
        cols = slice(j * half, (j + 1) * half)
        grad = pieces[4 + j].grad
        put_piece(grad, 0, dot_tn(mixed[...], after_low[:, cols]))
        for t in range(3):
            put_piece(grad, (t + 1) * width, dot_tn(grad_qkv[t], normed[:, cols]))

    def norm_one_back(i):
        rows = span(i)
        dy = get_out(out_d, rows)
        xhat = xhat_one[rows]
        small_part[0:1] += col_sum(dy * xhat)
        small_part[1:2] += col_sum(dy)
        e = dy * gain_one
        dx = rstd_one[rows] * (e - row_mean(e) - xhat * row_mean(e * xhat))
        grad_tokens[rows] = grad_after[rows] + dx

    def embed_grads():
        for i in range(4):

            @pl.when(me == i)
            def _():
                embed_bank[place.inner, place.outer] = grad_tokens[0:256, i * width : (i + 1) * width].astype(BF16)

    def small_ready():
        small_part[4:5] = grad_tokens[256:257]
        small_part[8:16] = meta_col[...] * grad_tokens[257:258]

    def pixel_part():
        pixels = dot_nt(kern[...], embed_bank[place.inner, place.outer]).astype(BF16)
        part_e[0] = pixels[: BANDS * PIX // 2]
        part_e[1] = pixels[BANDS * PIX // 2 :]

    def branch_part():
        need(4)
        for i in range(len(CUTS)):
            put_part(part_b, span(i), dot(activation[span(i)], w_down[...]))

    def final_output():
        for i, (lo, n) in enumerate(CUTS):
            rows = span(i)
            x = after[rows] + get_out(out_b, rows) + b_down
            if lo + n <= 256:
                output[lo + 2 : lo + n + 2] = live_col[rows] * x
            else:
                output[lo + 2 : 258] = live_col[lo:256] * x[: 256 - lo]
                output[0:2] = x[256 - lo : 258 - lo]
        keep(output, far_output)

    def final_pixels():
        grad_patches[: BANDS * PIX // 2] = out_e[0]
        grad_patches[BANDS * PIX // 2 :] = out_e[1]
        keep(grad_patches, far_grad_patches)

    down0, down1, up0, up1, attn0, attn1 = pieces
    order = [
        make_kern,
        embed,
        fill_bank,
        early.step,
        make_positions,
        epass,
        tokens_norm,
        attention,
        (attn_part, 0),
        (sum_a.start, 0),
        (attn_part, 3),
        (sum_a.start, 3),
        (attn_part, 2),
        early.step,
        (attn_part, 1),
        (sum_a.relay, 0),
        (sum_a.start, 1),
        fillgate,
        (sum_a.relay, 3),
        (sum_a.start, 2),
        (sum_a.relay, 1),
        (sum_a.relay, 2),
        (sum_a.forward, 0),
        (sum_a.total, 0),
        (sum_a.forward, 3),
        (feedforward, 0),
        (sum_c.start, 0),
        (sum_a.forward, 1),
        (sum_a.total, 3),
        (feedforward, 3),
        (sum_c.start, 3),
        (sum_a.forward, 2),
        (sum_c.relay, 0),
        (sum_a.total, 1),
        (feedforward, 1),
        (sum_c.start, 1),
        (sum_c.relay, 3),
        (sum_a.total, 2),
        (feedforward, 2),
        (grad_of_up, 1),
        up1.step,
        (sum_c.start, 2),
        (sum_c.relay, 1),
        (grad_of_up, 0),
        (sum_c.forward, 0),
        up0.step,
        (grad_of_down, 1),
        (sum_c.relay, 2),
        branch_part,
        (sum_c.forward, 3),
        (sum_c.forward, 1),
        down1.step,
        up1.step,
        (sum_c.forward, 2),
        (sum_c.total, 3),
        (sum_c.total, 0),
        (grad_of_down, 0),
        (sum_c.total, 1),
        (norm_two_back, 0),
        (norm_two_back, 1),
        (sum_c.total, 2),
        (norm_two_back, 2),
        (norm_two_back, 3),
        mixed_back,
        early.step,
        (head_back, 0),
        (head_back, 1),
        (head_back, 2),
        (norm_part, 2),
        (sum_b.start, 3),
        up0.step,
        up0.step,
        (norm_part, 0),
        (norm_part, 3),
        (sum_d.start, 2),
        up1.step,
        (sum_d.start, 0),
        (sum_b.relay, 3),
        (sum_b.start, 1),
        (sum_d.relay, 2),
        (sum_d.start, 3),
        (norm_part, 1),
        (sum_d.start, 1),
        (grad_of_attn, 0),
        down0.step,
        up0.step,
        up1.step,
        (sum_d.relay, 3),
        (sum_d.forward, 2),
        (sum_d.relay, 0),
        (sum_d.total, 2),
        up0.step,
        up0.step,
        (sum_d.relay, 1),
        (grad_of_attn, 1),
        attn0.step,
        (sum_b.relay, 1),
        down0.step,
        (sum_d.forward, 3),
        attn1.step,
        (sum_d.forward, 0),
        (sum_d.forward, 1),
        (sum_d.total, 3),
        (sum_d.total, 0),
        up1.step,
        (norm_one_back, 0),
        (norm_one_back, 3),
        early.step,
        (sum_d.total, 1),
        (norm_one_back, 2),
        (sum_b.start, 0),
        (sum_b.forward, 1),
        (norm_one_back, 1),
        embed_grads,
        down1.step,
        (sum_b.forward, 3),
        late.step,
        pixel_part,
        down1.step,
        small_ready,
        up0.step,
        (sum_b.start, 2),
        (sum_b.total, 1),
        (sum_e.start, 1),
        down0.step,
        down0.step,
        attn0.step,
        attn0.step,
        small.start,
        down1.step,
        late.step,
        down1.step,
        table_start,
        down1.step,
        up0.step,
        late.step,
        (sum_e.relay, 1),
        (sum_b.relay, 2),
        attn0.step,
        down1.step,
        (sum_e.start, 0),
        attn1.step,
        (sum_b.total, 3),
        up1.step,
        (sum_b.relay, 0),
        late.step,
        attn0.step,
        attn0.step,
        down0.step,
        attn1.step,
        down1.step,
        attn1.step,
        attn0.step,
        up0.step,
        (sum_e.relay, 0),
        early.step,
        attn1.step,
        small.relay,
        early.drain,
        attn0.step,
        late.step,
        late.drain,
        (sum_b.forward, 0),
        (sum_b.forward, 2),
        make_picks,
        (kern_grad_half, 0),
        (kern_grad_half, 1),
        (sum_b.total, 0),
        attn1.step,
        up1.step,
        (sum_e.forward, 1),
        (table_part, 0),
        attn1.step,
        (table_part, 1),
        (table_part, 2),
        down0.step,
        up1.step,
        (table_part, 3),
        down1.step,
        (table_part, 4),
        attn1.step,
        (sum_e.forward, 0),
        up0.step,
        down1.step,
        (table_part, 5),
        (sum_b.total, 2),
        final_output,
        up0.step,
        (table_part, 6),
        attn0.step,
        attn1.step,
        (table_part, 7),
        hidden_grads,
        (sum_e.total, 0),
        (sum_e.total, 1),
        down0.step,
        small.total,
        attn1.step,
        up1.step,
        attn0.step,
        up1.step,
        final_pixels,
        down1.step,
        hidden_sum.begin,
        down0.step,
        attn1.step,
        hidden_sum.total,
        attn0.step,
        down0.step,
        down0.step,
    ]
    def send_out(number):
        whole = wholes[number]
        if number < 4:
            keep(whole, far_wholes[number])
        else:
            flat = whole if len(whole.shape) == 3 else whole.reshape(2 * lines, *whole.shape[2:])
            first = width // whole.shape[-2]
            keep(flat.at[pl.ds(0, first)], far_wholes[number])
            keep(flat.at[pl.ds(first, flat.shape[0] - first)], far_wholes[number + 2])

    for number, piece in enumerate(pieces):
        piece.steps.append(functools.partial(send_out, number))
    for item in order:
        if isinstance(item, tuple):
            item[0](*item[1:])
        else:
            item()
    for piece in pieces:
        piece.drain()
    for copy in stores:
        copy.wait()
    for g in range(PIX // GROUP - 2, PIX // GROUP):
        kept[g].wait()
    for one in (sum_a, sum_b, sum_c, sum_d, sum_e, etc, hidden_sum):
        one.finish()


def layer(dp_count, width, operands):
    lines = dp_count // 2

    def piece(rows, lanes, parts):
        chunk = -(-rows // parts)
        chunk = -(-chunk // 16) * 16
        if parts == lines:
            return (lines, chunk, lanes)
        return (2, lines, chunk, lanes)

    pieces = []
    for name, kind in KINDS:
        parts = dp_count if kind is PairFirst else lines
        pieces.append(piece(4 * width, D // 2, parts))

    splits = []
    for count in (1, 3):
        for shape in pieces[4:]:
            splits.append((count * width // shape[-2], *shape[-2:]))

    def piece_scratch(shape):
        if len(shape) == 4:
            return [low(*shape[1:]), low(*shape[1:]), low(2, *shape[1:]), vmem(*shape[2:])]
        return [low(2, *shape), vmem(*shape[1:]), low(*shape[1:]), low(*shape[1:])]

    half = D // 2
    pixel_lanes = BANDS * PIX

    def vmem(*shape, dtype=F32):
        return pltpu.VMEM(shape, dtype)

    def low(*shape):
        return pltpu.VMEM(shape, BF16)

    scratch = [
        low(4, 256, width),
        vmem(ROWS, D),
        vmem(ROWS, D),
        vmem(ROWS, 1),
        vmem(ROWS, D),
        vmem(ROWS, 1),
        vmem(ROWS, D),
        low(ROWS, D),
        low(ROWS, D),
        low(ROWS, width),
        low(ROWS, width),
        low(ROWS, width),
        vmem(width // HEAD_DIM, ROWS, ROWS),
        low(ROWS, width),
        low(ROWS, width),
        low(3, ROWS, width),
        low(ROWS, D),
        vmem(ROWS, D),
        low(ROWS, D),
        low(ROWS, D),
        low(ROWS, D),
        low(2, 2, lines, PIX * SLOTS // 2 + SLOTS, 256),
        low(2, lines, 256, width),
        low(PIX * SLOTS, pixel_lanes),
        low(pixel_lanes, width),
        low(dp_count * GROUP * SLOTS, GROUP * NB),
        low(PIX // GROUP, dp_count * GROUP * SLOTS, width),
        low(PIX // GROUP * width, GROUP * NB),
        vmem(2, width * GROUP, HYP),
        vmem(NB, HYP),
        vmem(4, NB, HYP),
    ]
    scratch += [low(2, ROWS, half)] * 4 + [low(2, pixel_lanes // 2, 256)]
    scratch += [low(5, ROWS, half)] * 4 + [low(5, pixel_lanes // 2, 256)]
    scratch += [vmem(2, ROWS, half)] * 4 + [vmem(2, pixel_lanes // 2, 256)]
    scratch.append([low(*shape) for shape in pieces])
    scratch.append([piece_scratch(shape) for shape in pieces])
    scratch += [vmem(16, D), vmem(16, D), vmem(lines, 16, D)]
    dma = pltpu.SemaphoreType.DMA
    scratch += [dma((5, 16)), dma((5, 16)), dma((len(pieces) + 3, 4 * lines + 1)), dma((len(pieces) + 3, 4 * lines + 1)), dma((6,)), dma((6,))]
    scratch += [dma((dp_count,)), dma((dp_count,)), dma((2,))]
    far = pl.BlockSpec(memory_space=pl.ANY)
    ref = pl.BlockSpec(memory_space=pltpu.VMEM)
    smem = pl.BlockSpec(memory_space=pltpu.SMEM)
    specs = [far, ref, far, ref, ref, [ref] * 7, ref, smem, smem, smem, smem, smem] + [far] * 5
    scratch += [low(*operands[0].shape), low(2, width // 4, PIX, HYP), low(width, PIX * HYP)]
    scratch += [vmem(4, 256, D // 4), vmem(8, D), vmem(8, 1), vmem(1, ROWS), vmem(ROWS, 1), low(SLOTS, NB)]
    scratch += [pltpu.VMEM(x.shape, x.dtype) for x in operands[12:]]
    scratch += [vmem(SEQ, D), vmem(pixel_lanes, 256), [low(*shape) for shape in pieces]]
    scratch += [dma((12,)), dma((len(pieces) + 4,))]
    shapes = [
        jax.ShapeDtypeStruct((SEQ, D), F32),
        jax.ShapeDtypeStruct((pixel_lanes, 256), F32),
        jax.ShapeDtypeStruct((16, D), F32),
        jax.ShapeDtypeStruct((NB, HYP), F32),
        jax.ShapeDtypeStruct((width, PIX, HYP), F32),
        [jax.ShapeDtypeStruct(shape, BF16) for shape in pieces[:4] + splits],
    ]
    output, grad_patches, smalls, hidden_grad, grad_gen, wholes = pl.pallas_call(
        functools.partial(layer_kernel, lines, KINDS),
        out_shape=shapes,
        in_specs=specs,
        out_specs=[far, far, ref, ref, far, [far] * (len(pieces) + 2)],
        scratch_shapes=scratch,
        compiler_params=pltpu.CompilerParams(
            collective_id=0, has_side_effects=True, vmem_limit_bytes=67_043_328
        ),
        name="layer",
    )(*operands)
    wholes = [out.reshape(-1, out.shape[-1]) for out in wholes]
    return output, grad_patches, smalls, hidden_grad, grad_gen, wholes


def local(
    dp_count,
    patches,
    wavelengths,
    band_ids,
    band_mask,
    sensor,
    lengths,
    visible,
    meta,
    w_hyper,
    b_hyper,
    w_gen,
    cls_token,
    w_meta,
    gain_one,
    shift_one,
    w_qkv,
    w_out,
    gain_two,
    shift_two,
    w_up,
    b_up,
    w_down,
    b_down,
    cotangent,
):
    highest = lax.Precision.HIGHEST
    width = w_gen.shape[0]
    features = sinus_waves(wavelengths, HYP)
    hyper_pre = jnp.dot(features, w_hyper, precision=highest) + b_hyper
    hidden, hyper_pull = jax.vjp(gelu_exact, hyper_pre)
    hidden_low = hidden.astype(BF16)
    operands = (
        patches[0].T,
        hidden_low,
        w_gen,
        grid_waves(D, VIS_MAX),
        visible,
        [gain_one, shift_one, gain_two, shift_two, b_down, cls_token, b_up],
        w_meta,
        meta,
        lengths,
        sensor,
        band_ids,
        band_mask,
        w_qkv,
        w_out,
        w_up,
        w_down,
        cotangent[0],
    )
    output, grad_patches, smalls, grad_hidden, grad_w_gen, wholes = layer(dp_count, width, operands)

    grad_w_down, grad_w_up, grad_w_out, grad_w_qkv = [
        jnp.concatenate(wholes[k : k + 2], axis=1).astype(F32) for k in (0, 2, 4, 6)
    ]
    grad_inner = hyper_pull(grad_hidden)[0]
    grad_w_hyper = jnp.dot(features.T, grad_inner, precision=highest)
    grad_b_hyper = jnp.sum(grad_inner, axis=0)
    return (
        output[None],
        grad_patches.T[None],
        grad_w_hyper,
        grad_b_hyper,
        grad_w_gen,
        smalls[4],
        smalls[8:16],
        smalls[0],
        smalls[1],
        grad_w_qkv.reshape(3, width, D),
        grad_w_out,
        smalls[2],
        smalls[3],
        grad_w_up,
        smalls[6],
        grad_w_down,
        smalls[5],
    )


KINDS_MANY = (
    ("down0", PairFirst),
    ("down1", PairFirst),
    ("up0", PairFirst),
    ("up1", LineFirst),
    ("attn0", PairFirst),
    ("attn1", PairFirst),
    ("table0", PairFirst),
)


def layer_kernel_many(
    lines,
    kinds,
    patches,
    kern,
    positions,
    rows_in,
    meta_col,
    live_row,
    live_col,
    select,
    w_qkv,
    w_out,
    w_up,
    b_up,
    w_down,
    cotangent,
    output,
    grad_patches,
    smalls,
    wholes,
    embeds,
    tokens,
    xhat_one,
    rstd_one,
    xhat_two,
    rstd_two,
    after,
    normed,
    normed_two,
    queries,
    keys,
    values,
    probs,
    mixed,
    grad_mixed,
    grad_qkv,
    branch_grad,
    gate_grad,
    activation,
    grad_pre,
    grad_after,
    after_low,
    grad_tokens,
    embed_grad,
    spread,
    part_a,
    part_b,
    part_c,
    part_d,
    part_e,
    slots_a,
    slots_b,
    slots_c,
    slots_d,
    slots_e,
    out_a,
    out_b,
    out_c,
    out_d,
    out_e,
    grads,
    slots,
    small_part,
    small_pair,
    small_line,
    mp_sends,
    mp_recvs,
    dp_sends,
    dp_recvs,
    etc_sends,
    etc_recvs,
):
    core, pair, far = mp_peers()
    place = DpPlace(lines)
    greet([pair, far, place.pair] + [place.peer(k) for k in range(1, lines)])
    me = lax.axis_index("mp")
    width = w_out.shape[0]
    heads = width // HEAD_DIM
    full = D

    def mp_sum(part, slots, out, cuts, number):
        return MpSum(
            part,
            [slots.at[k] for k in range(5)],
            out,
            cuts,
            mp_sends.at[number],
            mp_recvs.at[number],
        )

    sum_a = mp_sum(part_a, slots_a, out_a, CUTS, 0)
    sum_b = mp_sum(part_b, slots_b, out_b, CUTS, 1)
    sum_c = mp_sum(part_c, slots_c, out_c, CUTS, 2)
    sum_d = mp_sum(part_d, slots_d, out_d, CUTS, 3)
    sum_e = mp_sum(part_e, slots_e, out_e, PIXEL_CUTS, 4)

    pieces = []
    for number, (name, kind) in enumerate(kinds):
        pieces.append(
            kind(
                place,
                grads[number],
                slots[number],
                wholes[number],
                dp_sends.at[number],
                dp_recvs.at[number],
            )
        )
    small = SmallSum(place, small_part, small_pair, small_line, smalls, dp_sends.at[len(kinds)], dp_recvs.at[len(kinds)])

    def put_piece(grad, first_row, block):
        rows = grad.shape[-2]
        for k in range(0, block.shape[0], rows):
            chunk = (first_row + k) // rows
            spot = (chunk,) if len(grad.shape) == 3 else (chunk // lines, chunk % lines)
            grad[spot] = block[k : k + rows].astype(BF16)

    gain_one, shift_one = rows_in[0:1], rows_in[1:2]
    gain_two, shift_two = rows_in[2:3], rows_in[3:4]
    b_down = rows_in[4:5]
    lane_head = lax.broadcasted_iota(jnp.int32, (1, width), 1) // HEAD_DIM
    head_masks = [(lane_head == h).astype(F32).astype(BF16) for h in range(heads)]

    etc = Sender(etc_sends, etc_recvs)
    kept = {}

    def embed():
        embeds[me] = dot_tn(patches[...], kern[...]).astype(BF16)
        mine = embeds.at[me]
        kept["pair"] = etc.go(0, mine, mine, pair)
        kept["far"] = etc.go(1, mine, mine, far)

    def epass():
        kept["far"].wait_recv()
        got = embeds.at[lax.rem(me + 2, 4)]
        kept["passed"] = etc.go(2, got, got, pair)

    def fillgate():
        branch_grad[0:256] = (live_col[0:256] * cotangent[2:258]).astype(BF16)
        branch_grad[256:272] = jnp.concatenate(
            [cotangent[0:2], jnp.zeros((14, full), F32)], axis=0
        ).astype(BF16)
        small_part[...] = jnp.zeros_like(small_part)
        small_part[5:6] = col_sum(branch_grad[...].astype(F32))
        gate_grad[...] = dot_nt(branch_grad[...], w_down[...])

    def tokens_norm():
        kept["pair"].wait_recv()
        kept["passed"].wait_recv()
        for lo, n in CUTS:
            hi = min(lo + n, 256)
            for i in range(4):
                cols = slice(i * width, (i + 1) * width)
                tokens[lo:hi, cols] = embeds[i, lo:hi].astype(F32)
            tokens[lo:hi] += positions[lo:hi]
            if lo + n > 256:
                tokens[256:272] = jnp.concatenate([rows_in[5:7], jnp.zeros((14, full), F32)], axis=0)
            rows = slice(lo, lo + n)
            x = tokens[rows]
            centred = x - row_mean(x)
            rstd = lax.rsqrt(row_mean(centred * centred) + 1e-05)
            rstd_one[rows] = rstd
            xhat = centred * rstd
            xhat_one[rows] = xhat
            normed[rows] = (xhat * gain_one + shift_one).astype(BF16)

    def attention():
        queries[...] = dot_nt(normed[...], w_qkv[0]).astype(BF16)
        keys[...] = dot_nt(normed[...], w_qkv[1]).astype(BF16)
        values[...] = dot_nt(normed[...], w_qkv[2]).astype(BF16)
        live_keys = live_row[...] > 0
        total = None
        for h in range(heads):
            raw = dot_nt(queries[...] * head_masks[h], keys[...]) * 0.125
            raw = jnp.where(live_keys, raw, -1000000000.0)
            expo = jnp.exp(raw - jnp.max(raw, axis=-1, keepdims=True))
            prob = expo / jnp.sum(expo, axis=-1, keepdims=True)
            probs[h] = prob
            term = dot(prob.astype(BF16), values[...] * head_masks[h])
            total = term if total is None else total + term
        mixed[...] = total.astype(BF16)

    def put_part(part, rows, block):
        half = block.shape[1] // 2
        part[0, rows] = block[:, :half].astype(BF16)
        part[1, rows] = block[:, half:].astype(BF16)

    def get_out(out, rows):
        return jnp.concatenate([out[0, rows], out[1, rows]], axis=1)

    def span(i):
        lo, n = CUTS[i]
        return slice(lo, lo + n)

    def attn_part(i):
        put_part(part_a, span(i), dot(mixed[span(i)], w_out[...]))

    def feedforward(i):
        rows = span(i)
        x = tokens[rows] + get_out(out_a, rows)
        after[rows] = x
        centred = x - row_mean(x)
        rstd = lax.rsqrt(row_mean(centred * centred) + 1e-05)
        rstd_two[rows] = rstd
        xhat = centred * rstd
        xhat_two[rows] = xhat
        normed_two[rows] = (xhat * gain_two + shift_two).astype(BF16)
        gate = dot(normed_two[rows], w_up[...]) + b_up[...]
        cdf = 0.5 + 0.5 * lax.erf(gate * (2.0**-0.5))
        activation[rows] = (gate * cdf).astype(BF16)
        pdf = jnp.exp(-0.5 * gate * gate) * ((2.0 * math.pi) ** -0.5)
        grad_pre[rows] = (gate_grad[rows] * (cdf + gate * pdf)).astype(BF16)
        put_part(part_c, rows, dot_nt(grad_pre[rows], w_up[...]))

    half = full // 2

    def grad_of_down(j):
        cols = slice(j * half, (j + 1) * half)
        put_piece(pieces[j].grad, 0, dot_tn(activation[...], branch_grad[:, cols]))

    def grad_of_up(j):
        cols = slice(j * half, (j + 1) * half)
        put_piece(pieces[2 + j].grad, 0, dot_tn(normed_two[...], grad_pre[:, cols]))
        if j == 1:
            small_part[6:7] = col_sum(grad_pre[...].astype(F32))

    def norm_two_back(i):
        rows = span(i)
        lo, n = CUTS[i]
        dy = get_out(out_c, rows)
        xhat = xhat_two[rows]
        small_part[2:3] += col_sum(dy * xhat)
        small_part[3:4] += col_sum(dy)
        e = dy * gain_two
        dx = rstd_two[rows] * (e - row_mean(e) - xhat * row_mean(e * xhat))
        if lo + n <= 256:
            grad_out = live_col[rows] * cotangent[lo + 2 : lo + n + 2]
        else:
            grad_out = jnp.concatenate(
                [live_col[lo:256] * cotangent[lo + 2 : 258], cotangent[0:2], jnp.zeros((14, full), F32)],
                axis=0,
            )
        grad_x = dx + grad_out
        grad_after[rows] = grad_x
        after_low[rows] = grad_x.astype(BF16)

    def mixed_back():
        grad_mixed[...] = dot_nt(after_low[...], w_out[...]).astype(BF16)
        kept["parts"] = [None, None, None]

    def head_back(h):
        mixed_h = grad_mixed[...] * head_masks[h]
        grad_probs = dot_nt(mixed_h, values[...])
        prob = probs[h]
        scores = prob * (grad_probs - jnp.sum(grad_probs * prob, axis=-1, keepdims=True))
        scores = scores.astype(BF16)
        terms = [
            dot(scores, keys[...] * head_masks[h]),
            dot_tn(scores, queries[...] * head_masks[h]),
            dot_tn(prob.astype(BF16), mixed_h),
        ]
        kept["parts"] = [t if p is None else p + t for p, t in zip(kept["parts"], terms)]
        if h == heads - 1:
            for t, scale in enumerate((0.125, 0.125, 1.0)):
                grad_qkv[t] = (kept["parts"][t] * scale).astype(BF16)

    def norm_part(i):
        rows = span(i)
        block = dot(grad_qkv[0, rows], w_qkv[0])
        block = block + dot(grad_qkv[1, rows], w_qkv[1])
        put_part(part_d, rows, block + dot(grad_qkv[2, rows], w_qkv[2]))

    def grad_of_attn(j):
        cols = slice(j * half, (j + 1) * half)
        grad = pieces[4 + j].grad
        put_piece(grad, 0, dot_tn(mixed[...], after_low[:, cols]))
        for t in range(3):
            put_piece(grad, (t + 1) * width, dot_tn(grad_qkv[t], normed[:, cols]))

    wide = NB * PIX

    def selection():
        band = lax.broadcasted_iota(jnp.int32, (BANDS * PIX, 16), 0) // PIX
        slot = lax.broadcasted_iota(jnp.int32, (BANDS * PIX, 16), 1)
        row_select = dot((band == slot).astype(F32).astype(BF16), select[...]).astype(BF16)
        table_band = lax.broadcasted_iota(jnp.int32, (NB, wide), 0)
        table_lane = lax.broadcasted_iota(jnp.int32, (NB, wide), 1) // PIX
        widen = (table_band == table_lane).astype(F32).astype(BF16)
        for b in range(BANDS):
            rows = slice(b * PIX, (b + 1) * PIX)
            spot = lax.broadcasted_iota(jnp.int32, (PIX, wide), 0)
            lane = lax.rem(lax.broadcasted_iota(jnp.int32, (PIX, wide), 1), PIX)
            block = dot(row_select[rows], widen)
            spread[rows] = jnp.where(spot == lane, block, 0.0).astype(BF16)

    def norm_one_back(i):
        rows = span(i)
        dy = get_out(out_d, rows)
        xhat = xhat_one[rows]
        small_part[0:1] += col_sum(dy * xhat)
        small_part[1:2] += col_sum(dy)
        e = dy * gain_one
        dx = rstd_one[rows] * (e - row_mean(e) - xhat * row_mean(e * xhat))
        grad_tokens[rows] = grad_after[rows] + dx

    def table_grad():
        for i in range(4):

            @pl.when(me == i)
            def _():
                embed_grad[...] = grad_tokens[0:256, i * width : (i + 1) * width].astype(BF16)

        grad_kern = dot(patches[...], embed_grad[...]).astype(BF16)
        table = dot_tn(grad_kern, spread[...])
        put_piece(pieces[6].grad, 0, table[:, : wide // 2])
        put_piece(pieces[6].grad, width, table[:, wide // 2 :])

    def small_ready():
        small_part[4:5] = grad_tokens[256:257]
        small_part[8:16] = meta_col[...] * grad_tokens[257:258]

    def pixel_part():
        pixels = dot_nt(kern[...], embed_grad[...]).astype(BF16)
        part_e[0] = pixels[: BANDS * PIX // 2]
        part_e[1] = pixels[BANDS * PIX // 2 :]

    def branch_part():
        for i in range(len(CUTS)):
            put_part(part_b, span(i), dot(activation[span(i)], w_down[...]))

    def final_output():
        for i, (lo, n) in enumerate(CUTS):
            rows = span(i)
            x = after[rows] + get_out(out_b, rows) + b_down
            if lo + n <= 256:
                output[lo + 2 : lo + n + 2] = live_col[rows] * x
            else:
                output[lo + 2 : 258] = live_col[lo:256] * x[: 256 - lo]
                output[0:2] = x[256 - lo : 258 - lo]

    def final_pixels():
        grad_patches[: BANDS * PIX // 2] = out_e[0]
        grad_patches[BANDS * PIX // 2 :] = out_e[1]

    down0, down1, up0, up1, attn0, attn1, table0 = pieces
    order = [
        embed,
        fillgate,
        selection,
        epass,
        tokens_norm,
        attention,
        (attn_part, 0),
        (sum_a.start, 0),
        (attn_part, 1),
        (sum_a.start, 1),
        (attn_part, 2),
        (sum_a.start, 2),
        (attn_part, 3),
        (sum_a.start, 3),
        (sum_a.relay, 0),
        (sum_a.relay, 1),
        (sum_a.relay, 2),
        (sum_a.relay, 3),
        (sum_a.forward, 0),
        (sum_a.forward, 1),
        (sum_a.total, 0),
        (feedforward, 0),
        (sum_a.total, 1),
        (sum_a.forward, 2),
        (sum_c.start, 0),
        (feedforward, 1),
        (sum_a.forward, 3),
        (sum_a.total, 2),
        (sum_c.relay, 0),
        (sum_c.start, 1),
        (feedforward, 2),
        (sum_a.total, 3),
        (sum_c.start, 2),
        (feedforward, 3),
        (sum_c.relay, 1),
        (sum_c.relay, 2),
        (sum_c.forward, 0),
        (sum_c.start, 3),
        (grad_of_down, 0),
        (grad_of_down, 1),
        down0.step,
        (sum_c.total, 0),
        down1.step,
        (sum_c.relay, 3),
        (grad_of_up, 0),
        up0.step,
        (sum_c.forward, 1),
        (grad_of_up, 1),
        up1.step,
        (sum_c.forward, 2),
        (norm_two_back, 0),
        (sum_c.total, 1),
        (norm_two_back, 1),
        (sum_c.total, 2),
        (sum_c.forward, 3),
        (norm_two_back, 2),
        branch_part,
        (sum_c.total, 3),
        (norm_two_back, 3),
        mixed_back,
        (head_back, 0),
        down0.step,
        down0.step,
        up1.step,
        (head_back, 1),
        (head_back, 2),
        (norm_part, 0),
        (sum_d.start, 0),
        (norm_part, 1),
        (sum_d.start, 1),
        (norm_part, 2),
        (sum_d.start, 2),
        (norm_part, 3),
        (sum_d.start, 3),
        (grad_of_attn, 0),
        (sum_d.relay, 0),
        (sum_d.relay, 1),
        (sum_d.relay, 2),
        down1.step,
        (sum_d.relay, 3),
        down0.step,
        down1.step,
        up1.step,
        up1.step,
        attn0.step,
        (grad_of_attn, 1),
        attn1.step,
        (sum_b.start, 0),
        (sum_b.start, 1),
        (sum_b.start, 2),
        (sum_b.start, 3),
        (sum_d.forward, 0),
        (sum_b.relay, 0),
        (sum_b.relay, 1),
        (sum_b.relay, 2),
        (sum_d.forward, 1),
        down0.step,
        down0.step,
        (sum_b.relay, 3),
        (sum_d.total, 0),
        (norm_one_back, 0),
        (sum_d.forward, 2),
        down1.step,
        (sum_d.total, 1),
        (norm_one_back, 1),
        (sum_d.forward, 3),
        up0.step,
        (sum_d.total, 2),
        up0.step,
        (norm_one_back, 2),
        up1.step,
        (sum_d.total, 3),
        (norm_one_back, 3),
        table_grad,
        down0.step,
        table0.step,
        down1.step,
        down1.step,
        up0.step,
        small_ready,
        small.start,
        pixel_part,
        (sum_e.start, 0),
        (sum_e.start, 1),
        (sum_b.forward, 0),
        (sum_b.forward, 1),
        (sum_b.forward, 2),
        (sum_b.forward, 3),
        attn0.step,
        attn0.step,
        (sum_e.relay, 0),
        (sum_e.relay, 1),
        (sum_b.total, 0),
        (sum_b.total, 1),
        (sum_b.total, 2),
        (sum_b.total, 3),
        final_output,
        down0.step,
        down1.step,
        attn0.step,
        up0.step,
        up0.step,
        (sum_e.forward, 0),
        attn1.step,
        down0.step,
        attn1.step,
        (sum_e.total, 0),
        (sum_e.forward, 1),
        (sum_e.total, 1),
        down1.step,
        final_pixels,
        up1.step,
        attn0.step,
        attn0.step,
        attn1.step,
        down0.step,
        up0.step,
        down1.step,
        up1.step,
        attn0.step,
        attn1.step,
        attn1.step,
        table0.step,
        table0.step,
        small.relay,
        down1.step,
        up0.step,
        up1.step,
        table0.step,
        attn0.step,
        attn1.step,
        down0.step,
        small.total,
        up0.step,
        table0.step,
        table0.step,
        down1.step,
        up1.step,
        up1.step,
        attn0.step,
        attn1.step,
        up0.step,
        table0.step,
        attn0.step,
        attn1.step,
        up0.step,
        table0.step,
        attn1.step,
        attn0.step,
        table0.step,
        attn1.step,
        table0.step,
        table0.step,
    ]
    for item in order:
        if isinstance(item, tuple):
            item[0](*item[1:])
        else:
            item()
    while any(piece.steps for piece in pieces):
        for piece in pieces:
            piece.step()
    for one in (sum_a, sum_b, sum_c, sum_d, sum_e, etc):
        one.finish()


def layer_many(dp_count, width, operands):
    lines = dp_count // 2

    def piece(rows, lanes, parts):
        chunk = -(-rows // parts)
        chunk = -(-chunk // 16) * 16
        if parts == lines:
            return (lines, chunk, lanes)
        return (2, lines, chunk, lanes)

    pieces = []
    for name, kind in KINDS_MANY:
        parts = dp_count if kind is PairFirst else lines
        if name == "table0":
            pieces.append(piece(2 * width, NB * PIX // 2, parts))
        else:
            pieces.append(piece(4 * width, D // 2, parts))

    def piece_scratch(shape):
        if len(shape) == 4:
            return [low(*shape[1:]), low(*shape[1:]), low(2, *shape[1:]), vmem(*shape[2:])]
        return [low(2, *shape), vmem(*shape[1:]), low(*shape[1:]), low(*shape[1:])]

    half = D // 2
    pixel_lanes = BANDS * PIX

    def vmem(*shape, dtype=F32):
        return pltpu.VMEM(shape, dtype)

    def low(*shape):
        return pltpu.VMEM(shape, BF16)

    scratch = [
        low(4, 256, width),
        vmem(ROWS, D),
        vmem(ROWS, D),
        vmem(ROWS, 1),
        vmem(ROWS, D),
        vmem(ROWS, 1),
        vmem(ROWS, D),
        low(ROWS, D),
        low(ROWS, D),
        low(ROWS, width),
        low(ROWS, width),
        low(ROWS, width),
        vmem(width // HEAD_DIM, ROWS, ROWS),
        low(ROWS, width),
        low(ROWS, width),
        low(3, ROWS, width),
        low(ROWS, D),
        vmem(ROWS, D),
        low(ROWS, D),
        low(ROWS, D),
        vmem(ROWS, D),
        low(ROWS, D),
        vmem(ROWS, D),
        low(256, width),
        low(pixel_lanes, NB * PIX),
    ]
    scratch += [low(2, ROWS, half)] * 4 + [low(2, pixel_lanes // 2, 256)]
    scratch += [low(5, ROWS, half)] * 4 + [low(5, pixel_lanes // 2, 256)]
    scratch += [vmem(2, ROWS, half)] * 4 + [vmem(2, pixel_lanes // 2, 256)]
    scratch.append([low(*shape) for shape in pieces])
    scratch.append([piece_scratch(shape) for shape in pieces])
    scratch += [vmem(16, D), vmem(16, D), vmem(lines, 16, D)]
    dma = pltpu.SemaphoreType.DMA
    scratch += [dma((5, 16)), dma((5, 16)), dma((len(pieces) + 1, 4 * lines + 1)), dma((len(pieces) + 1, 4 * lines + 1)), dma((3,)), dma((3,))]
    ref = pl.BlockSpec(memory_space=pltpu.VMEM)
    shapes = [
        jax.ShapeDtypeStruct((SEQ, D), F32),
        jax.ShapeDtypeStruct((pixel_lanes, 256), F32),
        jax.ShapeDtypeStruct((16, D), F32),
        [jax.ShapeDtypeStruct(shape, BF16) for shape in pieces],
    ]
    output, grad_patches, smalls, wholes = pl.pallas_call(
        functools.partial(layer_kernel_many, lines, KINDS_MANY),
        out_shape=shapes,
        in_specs=[ref] * len(operands),
        out_specs=[ref] * 3 + [[ref] * len(pieces)],
        scratch_shapes=scratch,
        compiler_params=pltpu.CompilerParams(
            collective_id=0, has_side_effects=True, vmem_limit_bytes=62 * 1024 * 1024
        ),
        name="layer",
    )(*operands)
    wholes = {name: out.reshape(-1, out.shape[-1]) for (name, kind), out in zip(KINDS_MANY, wholes)}
    return output, grad_patches, smalls, wholes


def small_sum_kernel_many(axis, count, part, out, slots, sends, recvs):
    me = lax.axis_index(axis)
    peers = [{axis: lax.rem(me + k, count)} for k in range(1, count)]
    greet(peers)
    copies = []
    for k, peer in enumerate(peers):
        copy = remote(part, slots.at[me], sends.at[k], recvs.at[k], peer)
        copy.start()
        copies.append(copy)
    slots[me] = part[...]
    for copy in copies:
        copy.wait()
    total = slots[0]
    for k in range(1, count):
        total = total + slots[k]
    out[...] = total


def small_sum_many(part, axis, count, number):
    vmem = pl.BlockSpec(memory_space=pltpu.VMEM)
    return pl.pallas_call(
        functools.partial(small_sum_kernel_many, axis, count),
        out_shape=jax.ShapeDtypeStruct(part.shape, F32),
        in_specs=[vmem],
        out_specs=vmem,
        scratch_shapes=[
            pltpu.VMEM((count,) + part.shape, F32),
            pltpu.SemaphoreType.DMA((count - 1,)),
            pltpu.SemaphoreType.DMA((count - 1,)),
        ],
        compiler_params=pltpu.CompilerParams(collective_id=number, has_side_effects=True),
        name="small_sum_" + axis,
    )(part)


def local_many(
    dp_count,
    patches,
    wavelengths,
    band_ids,
    band_mask,
    sensor,
    lengths,
    visible,
    meta,
    w_hyper,
    b_hyper,
    w_gen,
    cls_token,
    w_meta,
    gain_one,
    shift_one,
    w_qkv,
    w_out,
    gain_two,
    shift_two,
    w_up,
    b_up,
    w_down,
    b_down,
    cotangent,
):
    highest = lax.Precision.HIGHEST
    width = w_gen.shape[0]
    features = sinus_waves(wavelengths, HYP)
    positions = grid_codes(visible, lengths, D, VIS_MAX)[0]
    hyper_pre = jnp.dot(features, w_hyper, precision=highest) + b_hyper
    hidden, hyper_pull = jax.vjp(gelu_exact, hyper_pre)
    hidden_low = hidden.astype(BF16)
    ids, mask = band_ids[sensor[0]], band_mask[sensor[0]]
    select = (ids[:, None] == jnp.arange(NB)[None, :]).astype(F32) * mask[:, None].astype(F32)
    chosen = jnp.dot(select.astype(BF16), hidden_low, preferred_element_type=F32).astype(BF16)
    kern = jnp.einsum("bh,dph->bpd", chosen, w_gen, preferred_element_type=F32).astype(BF16)
    kern = kern.reshape(BANDS * PIX, width)
    place = jnp.arange(ROWS)
    live = ((place < lengths[0]) | ((place >= 256) & (place < SEQ))).astype(F32)
    meta_row = jnp.dot(meta, w_meta, precision=highest)[0]
    rows_in = jnp.stack([gain_one, shift_one, gain_two, shift_two, b_down, cls_token, meta_row, meta_row])
    operands = (
        patches[0].T,
        kern,
        positions,
        rows_in,
        meta.reshape(-1, 1),
        live[None, :],
        live[:, None],
        jnp.pad(select.astype(BF16), ((0, 16 - BANDS), (0, 0))),
        w_qkv,
        w_out,
        w_up,
        b_up[None, :],
        w_down,
        cotangent[0],
    )
    output, grad_patches, smalls, wholes = layer_many(dp_count, width, operands)

    def joined(name):
        halves = [wholes[f"{name}{j}"][: 4 * width] for j in range(2)]
        return jnp.concatenate(halves, axis=1).astype(F32)

    grad_w_down, grad_w_up, attn = joined("down"), joined("up"), joined("attn")
    table = wholes["table0"][: 2 * width].reshape(2, width, NB // 2, PIX)
    low_halves = hidden_low.reshape(2, NB // 2, HYP)
    grad_w_gen = jnp.einsum("anh,adnp->dph", low_halves, table, preferred_element_type=F32)
    hidden_part = jnp.einsum("adnp,dph->anh", table, w_gen, preferred_element_type=F32)
    grad_hidden = small_sum_many(hidden_part.reshape(NB, HYP), "mp", 4, 1)
    grad_inner = hyper_pull(grad_hidden)[0]
    grad_w_hyper = jnp.dot(features.T, grad_inner, precision=highest)
    grad_b_hyper = jnp.sum(grad_inner, axis=0)
    return (
        output[None],
        grad_patches.T[None],
        grad_w_hyper,
        grad_b_hyper,
        grad_w_gen,
        smalls[4],
        smalls[8:16],
        smalls[0],
        smalls[1],
        attn[width : 4 * width].reshape(3, width, D),
        attn[:width],
        smalls[2],
        smalls[3],
        grad_w_up,
        smalls[6],
        grad_w_down,
        smalls[5],
    )


def solution(mesh):
    return jax.shard_map(
        functools.partial(local if mesh.shape["dp"] == 8 else local_many, mesh.shape["dp"]),
        mesh=mesh,
        in_specs=(
            P("dp", None, None),
            P(),
            P(),
            P(),
            P("dp"),
            P("dp"),
            P("dp", None),
            P("dp", None),
            P(),
            P(),
            P("mp", None, None),
            P(),
            P(),
            P(),
            P(),
            P(None, "mp", None),
            P("mp", None),
            P(),
            P(),
            P(None, "mp"),
            P("mp"),
            P("mp", None),
            P(),
            P("dp", None, None),
        ),
        out_specs=(
            P("dp", None, None),
            P("dp", None, None),
            P(),
            P(),
            P("mp", None, None),
            P(),
            P(),
            P(),
            P(),
            P(None, "mp", None),
            P("mp", None),
            P(),
            P(),
            P(None, "mp"),
            P("mp"),
            P("mp", None),
            P(),
        ),
        check_vma=False,
    )
```
